32 devices in a mesh: dp: 4 (over y, x), sp: 8 (over z, core).
Axes of the slice: x: 2, y: 2, z: 4, core: 2. Of those that a mesh axis runs over, the one named last changes fastest.
Arguments:
- tokens: bfloat16 [32768, 1024], P(('dp', 'sp')), may hold values from -6 to 6
- doc_ids: int32 [4, 8192], P('dp'), may hold values from 0 to 15, never falling along the last dimension, each value on 1 to 4096 neighbouring positions
- gain_attn: bfloat16 [1024], P('sp'), may hold values from 0.5 to 1.5
- w_query: bfloat16 [1024, 256], P('sp'), may hold values from -0.1875 to 0.1875
- w_key: bfloat16 [1024, 256], P('sp'), may hold values from -0.1875 to 0.1875
- w_value: bfloat16 [1024, 1024], P('sp'), may hold values from -0.1875 to 0.1875
- w_out: bfloat16 [1024, 1024], P(None, 'sp'), may hold values from -2 to 2
- gain_mlp: bfloat16 [1024], P('sp'), may hold values from 0.5 to 1.5
- w_gate: bfloat16 [1024, 2752], P('sp'), may hold values from -0.1875 to 0.1875
- w_up: bfloat16 [1024, 2752], P('sp'), may hold values from -0.1875 to 0.1875
- w_down: bfloat16 [2752, 1024], P(None, 'sp'), may hold values from -0.109375 to 0.109375
- cotangent: bfloat16 [32768, 1024], P(('dp', 'sp')), may hold values from -6 to 6
Outputs:
- output: bfloat16 [32768, 1024], P(('dp', 'sp'))
- grad_input: float32 [32768, 1024], P(('dp', 'sp'))
- grad_gain_attn: float32 [1024], P('sp')
- grad_query: float32 [1024, 256], P('sp')
- grad_key: float32 [1024, 256], P('sp')
- grad_value: float32 [1024, 1024], P('sp')
- grad_out: float32 [1024, 1024], P(None, 'sp')
- grad_gain_mlp: float32 [1024], P('sp')
- grad_gate: float32 [1024, 2752], P('sp')
- grad_up: float32 [1024, 2752], P('sp')
- grad_down: float32 [2752, 1024], P(None, 'sp')
The draws below stay inside these ranges and needn't reach their ends.
Inputs may be any that keep to these rules, and one draw needn't show every extreme that they name: `doc_ids`: within each group document numbers never fall along the tokens, every number 0 to 15 is used, each document has 1 to 4096 tokens and one has exactly 4096.
All inputs are finite; a program needn't handle non-finite values.
Results may differ from the reference program's by a relative error of at most 0.019.
Values may be sent and summed in bfloat16 or wider, within the bound.
A program may use at most 192 MiB of HBM per device.

```python
import math
import jax
import jax.numpy as jnp
import numpy as np
from jax import lax

D = 1024
HEADS = 16
FEAT = 16
HEAD_V = 64
FF = 2752
BLOCK = 512
GROUP_TOK = 8192
MAX_LEN = 4096
DOCS = 16
TOKENS = 32768
N_DP = 4


def strengthened(values, own_key, source, target, parts, factor):
    def block_of(axis_at):
        return (jnp.arange(values.shape[axis_at]) // (values.shape[axis_at] // parts)).reshape((-1,) + (1,) * (values.ndim - 1 - axis_at))

    near = jax.random.permutation(own_key, parts)[block_of(target)]
    far = (block_of(target) + parts // 2) % parts
    return jnp.where((block_of(source) == near) | (block_of(source) == far), factor * values, values)


def block_scale(rng, extent, pieces, low, high):
    level = 1.0
    for dim, parts in pieces:
        draws = jax.random.uniform(jax.random.fold_in(jax.random.fold_in(rng, 6), dim), (parts,), jnp.float32, low / len(pieces), high / len(pieces))
        level = level * jnp.repeat(jnp.exp(draws), extent[dim] // parts).reshape((-1,) + (1,) * (len(extent) - 1 - dim))
    return level


def length_profile(number_of, total, bound, lean):
    loads = [(1 << 20) // math.isqrt(rank ** lean) + 1 for rank in range(2, number_of + 1)]
    surplus, given = total - bound - (number_of - 1), [1] * (number_of - 1)
    while surplus > 0:
        free = [i for i in range(number_of - 1) if given[i] < bound]
        mass, left = sum([loads[i] for i in free]), surplus
        for i in free:
            addition = min(bound - given[i], max(1, left * loads[i] // mass), surplus)
            given[i] = given[i] + addition
            surplus = surplus - addition
    return np.array([bound] + given)


def uneven_parts(own_key, amount, total, most, skew):
    if amount == 2:
        one = jax.random.randint(own_key, (), max(1, total - most), min(most, total - 1) + 1)
        return jnp.stack([one, total - one])
    sizes = jnp.asarray(length_profile(amount, total, most, skew), jnp.int32)
    twos = (amount - 1) // 2
    donor, sink = sizes[1:1 + 2 * twos:2], sizes[2:2 + 2 * twos:2]
    margin = jnp.minimum(donor - 1, most - sink)
    shifted = jax.random.randint(jax.random.fold_in(own_key, 1), (twos,), 0, 1 << 20) % (margin + 1)
    sizes = sizes.at[1:1 + 2 * twos:2].set(donor - shifted).at[2:2 + 2 * twos:2].set(sink + shifted)
    return sizes[jax.random.permutation(jax.random.fold_in(own_key, 2), amount)]


def noise(own_key, shape, scale, most, shards=(), held_as=jnp.bfloat16):
    values = jax.random.normal(own_key, shape, jnp.float32) * scale
    if len(shards) > 0:
        values = block_scale(own_key, shape, shards, -0.22, 0.18) * values
    return jnp.clip(values, min=-most, max=most).astype(held_as)


def heavy_noise(own_key, shape, scale, bound, split, heavy, kind=jnp.bfloat16):
    values = scale * jax.random.normal(own_key, shape, jnp.float32)
    if split:
        values = values * block_scale(own_key, shape, split, -0.22, 0.18)
    return jnp.clip(strengthened(values, jax.random.fold_in(own_key, 3), *heavy), -bound, bound).astype(kind)


def setup_inputs(seed: int = 0) -> dict:
    streams_of = jax.random.split(jax.random.key(seed), 13)
    return {
        "tokens": noise(streams_of[0], (TOKENS, D), 1.0, 6.0, ((0, 32),)),
        "doc_ids": jax.vmap(lambda own: jnp.searchsorted(jnp.cumsum(uneven_parts(own, DOCS, GROUP_TOK, MAX_LEN, 2)), jnp.arange(GROUP_TOK), side="right"))(jax.random.split(streams_of[1], N_DP)).reshape((N_DP, GROUP_TOK)).astype(jnp.int32),
        "gain_attn": jnp.clip(1.0 + 0.1 * jax.random.normal(streams_of[2], (D,), jnp.float32), 0.5, 1.5).astype(jnp.bfloat16),
        "w_query": noise(streams_of[3], (D, HEADS * FEAT), D ** -0.5, 0.1875, ((0, 8),)),
        "w_key": noise(streams_of[4], (D, HEADS * FEAT), D ** -0.5, 0.1875, ((0, 8),)),
        "w_value": noise(streams_of[5], (D, HEADS * HEAD_V), D ** -0.5, 0.1875, ((0, 8),)),
        "w_out": noise(streams_of[6], (HEADS * HEAD_V, D), (D // 128) ** -0.5, 2.0, ((1, 8),)),
        "gain_mlp": jnp.clip(1.0 + 0.1 * jax.random.normal(streams_of[7], (D,), jnp.float32), 0.5, 1.5).astype(jnp.bfloat16),
        "w_gate": noise(streams_of[8], (D, FF), D ** -0.5, 0.1875, ((0, 8),)),
        "w_up": noise(streams_of[9], (D, FF), D ** -0.5, 0.1875, ((0, 8),)),
        "w_down": noise(streams_of[10], (FF, D), FF ** -0.5, 0.109375, ((1, 8),)),
        "cotangent": heavy_noise(streams_of[11], (TOKENS, D), 1.0, 6.0, ((0, 32),), (0, 1, 32, 2.75)),
    }


EPSILON = 1e-05
PRECISE = lax.Precision.HIGHEST

@jax.custom_vjp
def low(v):
    return lax.optimization_barrier(v.astype(jnp.bfloat16)).astype(jnp.float32)

@jax.custom_vjp
def low_back(v):
    return v

def low_keep(v):
    return (low(v), None)

def low_pass(kept, grad):
    return (grad,)

def back_keep(v):
    return (v, None)

def back_low(kept, grad):
    return (low(grad),)
low.defvjp(low_keep, low_pass)
low_back.defvjp(back_keep, back_low)

def rms_scale(values, weights):
    return values * lax.rsqrt(lax.optimization_barrier(jnp.mean(values * values, axis=-1, keepdims=True)) + EPSILON) * weights

def taylor(vectors):
    feature_dim = vectors.shape[-1]
    scale_one = 1.0 / math.sqrt(math.sqrt(feature_dim))
    scale_two = 1.0 / (math.sqrt(2.0) * math.sqrt(feature_dim))
    products = (vectors[..., :, None] * vectors[..., None, :]).reshape(vectors.shape[:-1] + (feature_dim * feature_dim,))
    return jnp.concatenate([jnp.ones(vectors.shape[:-1] + (1,), vectors.dtype), vectors * scale_one, products * scale_two], axis=-1)

def attend_block(carried, blocks):
    kv_state, key_total, last_doc = carried
    query_blk, key_blk, value_blk, doc_blk = blocks
    feature_dim = query_blk.shape[-1]
    length_blk = doc_blk.shape[0]
    scores = jnp.einsum('hif,hjf->hij', query_blk, key_blk, precision=PRECISE)
    position = lax.iota(jnp.int32, length_blk)
    allowed = (position[:, None] >= position[None, :]) & (doc_blk[:, None] == doc_blk[None, :])
    weights = jnp.where(allowed[None], 1.0 + scores / math.sqrt(feature_dim) + scores * scores / (2.0 * feature_dim), 0.0)
    query_map = taylor(query_blk)
    key_map = taylor(key_blk)
    sees_prior = (doc_blk == last_doc).astype(query_blk.dtype)
    numerator = jnp.einsum('hij,hjv->hiv', weights, value_blk, precision=PRECISE) + sees_prior[None, :, None] * jnp.einsum('hif,hfv->hiv', query_map, kv_state, precision=PRECISE)
    denominator = lax.optimization_barrier(jnp.sum(weights, axis=-1)) + sees_prior[None, :] * jnp.einsum('hif,hf->hi', query_map, key_total, precision=PRECISE)
    attended = numerator / denominator[..., None]
    tail_doc = doc_blk[length_blk - 1]
    keep_old = (tail_doc == last_doc).astype(query_blk.dtype)
    in_tail = (doc_blk == tail_doc).astype(query_blk.dtype)
    key_tail = key_map * in_tail[None, :, None]
    kv_state = keep_old * kv_state + jnp.einsum('hjf,hjv->hfv', key_tail, value_blk, precision=PRECISE)
    key_total = keep_old * key_total + lax.optimization_barrier(jnp.sum(key_tail, axis=1))
    return ((kv_state, key_total, tail_doc), attended)

def attend(queries, keys_in, values_in, doc_row):
    head_count, feature_dim, length = queries.shape
    value_dim = values_in.shape[1]
    block_count = length // BLOCK
    mapped_dim = 1 + feature_dim + feature_dim * feature_dim

    def blocked(tensor):
        inner_dim = tensor.shape[1]
        return tensor.reshape(head_count, inner_dim, block_count, BLOCK).transpose(2, 0, 3, 1)
    initial = (jnp.zeros((head_count, mapped_dim, value_dim), queries.dtype), jnp.zeros((head_count, mapped_dim), queries.dtype), jnp.array(-1, jnp.int32))
    _, outputs = lax.scan(jax.checkpoint(attend_block), initial, (blocked(queries), blocked(keys_in), blocked(values_in), doc_row.reshape(block_count, BLOCK)))
    return outputs.transpose(1, 3, 0, 2).reshape(head_count, value_dim, length)

def reference(tokens, doc_ids, gain_attn, w_query, w_key, w_value, w_out, gain_mlp, w_gate, w_up, w_down, cotangent):
    total_tok = tokens.shape[0]
    group_count = doc_ids.shape[0]
    group_len = doc_ids.shape[1]

    def grouped(tensor, width):
        return tensor.reshape(group_count, group_len, HEADS, width).transpose(0, 2, 3, 1)

    def one_group(items):
        return attend(items[0], items[1], items[2], items[3])

    def forward(resid, gain_one, query_w, key_w, value_w, out_w, gain_two, gate_w, up_w, down_w):
        normed_one = low(rms_scale(resid, gain_one))
        queries = low_back(low(jnp.dot(normed_one, query_w, precision=PRECISE, preferred_element_type=jnp.float32)))
        keys_all = low_back(low(jnp.dot(normed_one, key_w, precision=PRECISE, preferred_element_type=jnp.float32)))
        values_all = low_back(low(jnp.dot(normed_one, value_w, precision=PRECISE, preferred_element_type=jnp.float32)))
        attended = lax.map(one_group, (grouped(queries, FEAT), grouped(keys_all, FEAT), grouped(values_all, HEAD_V), doc_ids))
        attended = attended.transpose(0, 3, 1, 2).reshape(total_tok, HEADS * HEAD_V)
        attended = low_back(low(attended))
        hidden = resid + low_back(jnp.dot(attended, out_w, precision=PRECISE, preferred_element_type=jnp.float32))
        normed_two = low(rms_scale(hidden, gain_two))
        gate = low_back(jnp.dot(normed_two, gate_w, precision=PRECISE, preferred_element_type=jnp.float32))
        up_proj = low_back(jnp.dot(normed_two, up_w, precision=PRECISE, preferred_element_type=jnp.float32))
        mixed = low(jax.nn.silu(gate) * up_proj)
        return hidden + low_back(jnp.dot(mixed, down_w, precision=PRECISE, preferred_element_type=jnp.float32))
    result, backward = jax.vjp(forward, tokens.astype(jnp.float32), gain_attn.astype(jnp.float32), w_query.astype(jnp.float32), w_key.astype(jnp.float32), w_value.astype(jnp.float32), w_out.astype(jnp.float32), gain_mlp.astype(jnp.float32), w_gate.astype(jnp.float32), w_up.astype(jnp.float32), w_down.astype(jnp.float32))
    grads = backward(cotangent.astype(jnp.float32))
    return (result.astype(jnp.bfloat16), grads[0], grads[1], grads[2], grads[3], grads[4], grads[5], grads[6], grads[7], grads[8], grads[9])
```

```python
import functools
import math

import jax
import jax.numpy as jnp
import numpy as np
from jax import lax
from jax.experimental import pallas as pl
from jax.experimental.pallas import tpu as pltpu
from jax.sharding import PartitionSpec as P

FEAT = 16
HEAD_V = 64
EPSILON = 1e-05
BF16 = jnp.bfloat16
F32 = jnp.float32
BLK = 256
PAD_F = 256
ROWS_S = 80
NN = (((1,), (0,)), ((), ()))
NT = (((1,), (1,)), ((), ()))
TN = (((0,), (0,)), ((), ()))


def mm(a, b, dims=NN):
    return lax.dot_general(a, b, dims, preferred_element_type=F32)


def feature_table():
    rows = []
    for a in range(FEAT):
        for b in range(a, FEAT):
            rows.append((a, b, 0.0, 0.0, 1.0 if a == b else 2.0))
    for a in range(FEAT):
        rows.append((a, -1, 0.0, 1.0, 8.0))
    rows.append((-1, -1, 1.0, 1.0, 32.0))
    while len(rows) < PAD_F:
        rows.append((-1, -1, 0.0, 0.0, 0.0))
    table = np.zeros((8, PAD_F), np.float32)
    table[:5] = np.array(rows, np.float32).T
    return jnp.asarray(table)


def selectors(table, head, lanes):
    row = lax.broadcasted_iota(jnp.int32, (lanes, PAD_F), 0).astype(F32)
    base = (head * FEAT).astype(F32)
    first = jnp.where((row == table[0:1] + base) & (table[0:1] >= 0), 1.0, 0.0).astype(BF16)
    second = jnp.where((row == table[1:2] + base) & (table[1:2] >= 0), 1.0, 0.0).astype(BF16)
    return first, second


def head_lanes(values, head, scale=1):
    lane = lax.broadcasted_iota(jnp.int32, values.shape, 1)
    return jnp.where(lane // FEAT == head, values * scale, jnp.zeros_like(values))


def factors(values, sel, table):
    one = mm(values, sel[0]) + table[2:3]
    two = mm(values, sel[1]) + table[3:4]
    return one, two


def with_ones(v_pair):
    return jnp.concatenate([v_pair, jnp.ones_like(v_pair)], axis=1)


def states_kernel(k_ref, v_ref, tail_ref, table_ref, out_ref):
    lanes = k_ref.shape[1]
    table = table_ref[...]
    tail = tail_ref[...]

    def pair(p, carry):
        columns = pl.ds(pl.multiple_of(p * 128, 128), 128)
        v_t = v_ref[:, columns].astype(F32).T * tail
        ones = jnp.broadcast_to(tail, (16, tail.shape[1]))
        for side in range(2):
            head = p * 2 + side
            sel = selectors(table, head, lanes)
            one, two = factors(k_ref[...], sel, table)
            phi = (one * two).astype(BF16)
            lhs = jnp.concatenate([v_t[side * 64 : side * 64 + 64], ones], axis=0)
            out_ref[head] = mm(lhs.astype(BF16), phi).astype(BF16)
        return carry

    lax.fori_loop(0, v_ref.shape[1] // 128, pair, 0)


def placed(state, side, z_rows):
    zero = jnp.zeros((64, PAD_F), state.dtype)
    values = [state[0:64], zero] if side == 0 else [zero, state[0:64]]
    return jnp.concatenate(values + [z_rows], axis=0)


def forward_kernel(
    q_ref, k_ref, v_ref, state_ref, doc_col_ref, doc_row_ref, prior_ref, table_ref,
    att_ref, inv_ref, mask_ref,
):
    tok, lanes = q_ref.shape
    table = table_ref[...]
    row = lax.broadcasted_iota(jnp.int32, (tok, tok), 0)
    col = lax.broadcasted_iota(jnp.int32, (tok, tok), 1)
    mask_ref[...] = jnp.where(
        (row >= col) & (doc_col_ref[...] == doc_row_ref[...]), 1.0, 0.0
    )
    lane = lax.broadcasted_iota(jnp.int32, (BLK, 128), 1)

    def pair(p, carry):
        columns = pl.ds(pl.multiple_of(p * 128, 128), 128)
        v_hat = with_ones(v_ref[:, columns])
        results = []
        for side in range(2):
            head = p * 2 + side
            sel = selectors(table, head, lanes)
            state = state_ref[head]
            z_rows = jnp.broadcast_to(state[64:65].astype(F32), (128, PAD_F)).astype(BF16)
            rows_n = placed(state, side, z_rows)
            one, two = factors(q_ref[...], sel, table)
            phi = (one * two).astype(BF16)
            inter = mm(phi, rows_n, NT) * prior_ref[...]
            q_head = head_lanes(q_ref[...], head)
            parts = []
            for i in range(tok // BLK):
                rows = slice(i * BLK, (i + 1) * BLK)
                keys = slice(0, (i + 1) * BLK)
                t = mm(q_head[rows], k_ref[keys, :], NT) + 4.0
                w = ((t * t + 16.0) * mask_ref[rows, keys]).astype(BF16)
                total = mm(w, v_hat[keys]) + inter[rows]
                inv = 1.0 / total[:, 128:]
                parts.append((total[:, :128] * inv, inv))
            results.append(parts)
        for i in range(tok // BLK):
            rows = slice(i * BLK, (i + 1) * BLK)
            att_ref[rows, columns] = jnp.where(
                lane < 64, results[0][i][0], results[1][i][0]
            ).astype(BF16)
            inv_ref[rows, columns] = jnp.where(lane < 64, results[0][i][1], results[1][i][1])
        return carry

    lax.fori_loop(0, v_ref.shape[1] // 128, pair, 0)


def ghat_kernel(q_ref, g_ref, att_ref, inv_ref, head_row_ref, table_ref, ghat_ref, out_ref):
    tok, lanes = q_ref.shape
    table = table_ref[...]
    r = lax.broadcasted_iota(jnp.int32, (128, 128), 0)
    c = lax.broadcasted_iota(jnp.int32, (128, 128), 1)
    same = jnp.where(r // 64 == c // 64, 1.0, 0.0).astype(BF16)
    lane = lax.broadcasted_iota(jnp.int32, (tok, 128), 1) % 64
    head_row = head_row_ref[...]

    def pair(p, carry):
        columns = pl.ds(pl.multiple_of(p * 128, 128), 128)
        scaled = g_ref[:, columns].astype(F32) * inv_ref[:, columns]
        product = scaled * att_ref[:, columns].astype(F32)
        high = product.astype(BF16)
        low = (product - high.astype(F32)).astype(BF16)
        dots = -(mm(high, same) + mm(low, same))
        dots_high = dots.astype(BF16)
        dots_low = (dots - dots_high.astype(F32)).astype(BF16)
        extra = jnp.where(lane == 0, dots_high, jnp.where(lane == 1, dots_low, jnp.zeros_like(dots_low)))
        ghat = jnp.concatenate([scaled.astype(BF16), extra], axis=1)
        ghat_ref[p] = ghat
        ghat_t = ghat.astype(F32).T * head_row
        for side in range(2):
            head = p * 2 + side
            sel = selectors(table, head, lanes)
            one, two = factors(q_ref[...], sel, table)
            phi = (one * two).astype(BF16)
            lhs = jnp.concatenate(
                [ghat_t[side * 64 : side * 64 + 64], ghat_t[128 + side * 64 : 128 + side * 64 + 16]], axis=0
            )
            state = mm(lhs.astype(BF16), phi)
            z_row = jnp.sum(state[64:80], axis=0, keepdims=True)
            out_ref[head] = jnp.concatenate(
                [state[0:64], jnp.broadcast_to(z_row, (16, PAD_F))], axis=0
            ).astype(BF16)
        return carry

    lax.fori_loop(0, g_ref.shape[1] // 128, pair, 0)


def backward_kernel(
    q_ref, k_ref, v_ref, ghat_ref, prior_state_ref, later_state_ref, doc_col_ref, doc_row_ref,
    prior_ref, later_ref, table_ref, gq_ref, gk_ref, gv_ref, mask_ref, gq_acc, gk_acc,
):
    tok, lanes = q_ref.shape
    table = table_ref[...]
    row = lax.broadcasted_iota(jnp.int32, (tok, tok), 0)
    col = lax.broadcasted_iota(jnp.int32, (tok, tok), 1)
    mask_ref[...] = jnp.where(
        (row <= col) & (doc_col_ref[...] == doc_row_ref[...]), 1.0, 0.0
    )
    gq_acc[...] = jnp.zeros_like(gq_acc)
    gk_acc[...] = jnp.zeros_like(gk_acc)
    lane = lax.broadcasted_iota(jnp.int32, (tok, 256), 1)
    first_row = lax.broadcasted_iota(jnp.int32, (128, PAD_F), 0)

    def pair(p, carry):
        columns = pl.ds(pl.multiple_of(p * 128, 128), 128)
        v_hat = with_ones(v_ref[:, columns])
        gv = [jnp.zeros((BLK, 128), F32) for _ in range(tok // BLK)]
        gv_inter = None
        for side in range(2):
            head = p * 2 + side
            sel = selectors(table, head, lanes)
            ghat = jnp.where((lane % 128) // 64 == side, ghat_ref[p], jnp.zeros((tok, 256), BF16))
            q_head = head_lanes(q_ref[...], head)
            q_twice = q_head + q_head
            k_twice = head_lanes(k_ref[...], head, 2)

            later = later_state_ref[head]
            z_one = jnp.where(first_row == 0, later[64:65], jnp.zeros((128, PAD_F), BF16))
            rows_n = placed(later, side, z_one)
            k_one, k_two = factors(k_ref[...], sel, table)
            phi_k = (k_one * k_two).astype(BF16)
            gvi = mm(phi_k, rows_n[0:128], NT)
            gv_inter = gvi if gv_inter is None else gv_inter + gvi
            d_phi = mm(v_hat, rows_n) * later_ref[...]
            gk_acc[...] += mm((d_phi * k_two).astype(BF16), sel[0], NT) + mm(
                (d_phi * k_one).astype(BF16), sel[1], NT
            )

            prior = prior_state_ref[head]
            z_two = jnp.where(first_row // 2 == side * 32, prior[64:65], jnp.zeros((128, PAD_F), BF16))
            rows_p = placed(prior, side, z_two)
            q_one, q_two = factors(q_ref[...], sel, table)
            d_phi = mm(ghat, rows_p) * prior_ref[...]
            gq_acc[...] += mm((d_phi * q_two).astype(BF16), sel[0], NT) + mm(
                (d_phi * q_one).astype(BF16), sel[1], NT
            )

            for j in range(tok // BLK):
                rows = slice(j * BLK, (j + 1) * BLK)
                onward = slice(j * BLK, tok)
                t = mm(k_ref[rows, :], q_head[onward], NT) + 4.0
                g_w = mm(v_hat[rows], ghat[onward], NT)
                mask = mask_ref[rows, onward]
                masked_t = t * mask
                w = (masked_t * t + 16.0 * mask).astype(BF16)
                g_s = (g_w * masked_t).astype(BF16)
                gv[j] = gv[j] + mm(w, ghat[onward, 0:128])
                gk_acc[rows, :] += mm(g_s, q_twice[onward])
                gq_acc[onward, :] += mm(g_s, k_twice[rows], TN)
        for j in range(tok // BLK):
            rows = slice(j * BLK, (j + 1) * BLK)
            gv_ref[rows, columns] = (gv[j] + gv_inter[rows] * later_ref[rows, :]).astype(BF16)
        return carry

    lax.fori_loop(0, v_ref.shape[1] // 128, pair, 0)
    gq_ref[...] = gq_acc[...].astype(BF16)
    gk_ref[...] = gk_acc[...].astype(BF16)


def call(kernel, out_shape, *args, scratch=(), name=None):
    vmem = pl.BlockSpec(memory_space=pltpu.VMEM)
    return pl.pallas_call(
        kernel,
        out_shape=out_shape,
        in_specs=[vmem] * len(args),
        out_specs=jax.tree.map(lambda _: vmem, out_shape),
        scratch_shapes=list(scratch),
        compiler_params=pltpu.CompilerParams(vmem_limit_bytes=60 << 20),
        name=name,
    )(*args)


def ffn_kernel(
    width, x_ref, att_ref, out_t_ref, gain_ref, cot_ref, wg_ref, wu_ref, wd_ref,
    output_ref, gh_ref, ggain_ref, dg_ref, du_ref, dd_ref,
    hid, n2, n2_t, cot_t, acc_o, acc_n,
):
    step = pl.program_id(0)

    @pl.when(step == 0)
    def _():
        hidden = x_ref[...].astype(F32) + mm(att_ref[...], out_t_ref[...], NT)
        hid[...] = hidden
        scale = lax.rsqrt(jnp.mean(hidden * hidden, axis=1, keepdims=True) + EPSILON)
        normed = (hidden * scale * gain_ref[...]).astype(BF16)
        n2[...] = normed
        n2_t[...] = normed.T
        cot_t[...] = cot_ref[...].T
        acc_o[...] = jnp.zeros_like(acc_o)
        acc_n[...] = jnp.zeros_like(acc_n)

    chunk = wg_ref.shape[1]
    lane = lax.broadcasted_iota(jnp.int32, wg_ref.shape, 1) + step * chunk
    valid = lane < width
    zero = jnp.zeros(wg_ref.shape, BF16)
    wg = jnp.where(valid, wg_ref[...], zero)
    wu = jnp.where(valid, wu_ref[...], zero)
    wd = jnp.where(valid, wd_ref[...], zero)
    gate = mm(n2[...], wg)
    up = mm(n2[...], wu)
    g_mixed = mm(cot_ref[...], wd)
    sig = 1.0 / (1.0 + jnp.exp(-gate))
    act = gate * sig
    mixed = (act * up).astype(BF16)
    g_gate = (g_mixed * up * sig * (1.0 + gate * (1.0 - sig))).astype(BF16)
    g_up = (g_mixed * act).astype(BF16)
    dd_ref[...] = mm(cot_t[...], mixed).astype(BF16)
    dg_ref[...] = mm(n2_t[...], g_gate).astype(BF16)
    du_ref[...] = mm(n2_t[...], g_up).astype(BF16)
    acc_o[...] += mm(mixed, wd, NT)
    acc_n[...] += mm(g_gate, wg, NT) + mm(g_up, wu, NT)

    @pl.when(step == pl.num_programs(0) - 1)
    def _():
        hidden = hid[...]
        output_ref[...] = (hidden + acc_o[...]).astype(BF16)
        scale = lax.rsqrt(jnp.mean(hidden * hidden, axis=1, keepdims=True) + EPSILON)
        e = acc_n[...]
        ggain_ref[...] = jnp.sum(e * hidden * scale, axis=0, keepdims=True)
        eg = e * gain_ref[...]
        inner = jnp.mean(eg * hidden, axis=1, keepdims=True)
        gh_ref[...] = (
            cot_ref[...].astype(F32) + scale * eg - hidden * (scale * scale * scale * inner)
        )


def ffn(x, att, out_t, gain, cot, wg, wu, wd):
    tok, dim = x.shape
    width = wg.shape[1]
    chunk = 256
    whole = lambda shape: pl.BlockSpec(shape, lambda i: (0, 0))
    lanes = pl.BlockSpec((dim, chunk), lambda i: (0, i))
    grad = jax.ShapeDtypeStruct((dim, width), BF16)
    return pl.pallas_call(
        functools.partial(ffn_kernel, width),
        grid=(pl.cdiv(width, chunk),),
        out_shape=(
            jax.ShapeDtypeStruct((tok, dim), BF16),
            jax.ShapeDtypeStruct((tok, dim), F32),
            jax.ShapeDtypeStruct((1, dim), F32),
            grad, grad, grad,
        ),
        in_specs=[
            whole((tok, dim)), whole((tok, dim)), whole((dim, dim)), whole((1, dim)), whole((tok, dim)),
            lanes, lanes, lanes,
        ],
        out_specs=(whole((tok, dim)), whole((tok, dim)), whole((1, dim)), lanes, lanes, lanes),
        scratch_shapes=[
            pltpu.VMEM((tok, dim), F32),
            pltpu.VMEM((tok, dim), BF16),
            pltpu.VMEM((dim, tok), BF16),
            pltpu.VMEM((dim, tok), BF16),
            pltpu.VMEM((tok, dim), F32),
            pltpu.VMEM((tok, dim), F32),
        ],
        compiler_params=pltpu.CompilerParams(vmem_limit_bytes=60 << 20),
        name="ffn",
    )(x, att, out_t, gain, cot, wg, wu, wd)


def rms_scale(values, weights):
    return values * lax.rsqrt(jnp.mean(values * values, axis=-1, keepdims=True) + EPSILON) * weights


def rms_back(u, gain, e):
    scale = lax.rsqrt(jnp.mean(u * u, axis=-1, keepdims=True) + EPSILON)
    grad_gain = jnp.sum(e * u * scale, axis=0)
    eg = e * gain
    inner = jnp.mean(eg * u, axis=-1, keepdims=True)
    return scale * eg - u * (scale * scale * scale * inner), grad_gain


def body(
    tokens, doc_ids, gain_attn, w_query, w_key, w_value, w_out, gain_mlp, w_gate, w_up, w_down, cotangent
):
    n_sp = lax.axis_size("sp")
    me = lax.axis_index("sp")
    tok = tokens.shape[0]
    heads = w_query.shape[1] // FEAT
    table = feature_table()
    gather = lambda a: lax.all_gather(a, "sp", axis=0, tiled=True)
    gain_one = gather(gain_attn).astype(F32)
    gain_two = gather(gain_mlp).astype(F32)
    w_joint = gather(jnp.concatenate([w_query, w_key, w_value], axis=1))
    out_t = gather(w_out.T)
    wg = gather(w_gate)
    wu = gather(w_up)
    wd = gather(w_down.T)

    doc_all = doc_ids[0]
    doc = lax.dynamic_slice(doc_all, (me * tok,), (tok,))
    ends = doc_all.reshape(n_sp, tok)
    firsts, lasts = ends[:, 0], ends[:, tok - 1]
    my_first, my_last = doc[0], doc[tok - 1]
    prev_last = jnp.where(me > 0, lasts[jnp.maximum(me - 1, 0)], -1)
    next_first = jnp.where(me < n_sp - 1, firsts[jnp.minimum(me + 1, n_sp - 1)], -1)
    order = jnp.arange(n_sp)
    from_prior = ((order < me) & (lasts == prev_last)).astype(F32)
    from_later = ((order > me) & (firsts == next_first)).astype(F32)
    tail_row = (doc == my_last).astype(F32)[None, :]
    head_row = (doc == my_first).astype(F32)[None, :]
    prior_col = (doc == prev_last).astype(F32)[:, None]
    later_col = (doc == next_first).astype(F32)[:, None]
    doc_col, doc_row = doc[:, None], doc[None, :]

    resid = tokens.astype(F32)
    normed_one = rms_scale(resid, gain_one).astype(BF16)
    projected = mm(normed_one, w_joint).astype(BF16)
    lanes = heads * FEAT
    q, k, v = projected[:, :lanes], projected[:, lanes : 2 * lanes], projected[:, 2 * lanes :]
    state_shape = jax.ShapeDtypeStruct((heads, ROWS_S, PAD_F), BF16)
    own_state = call(states_kernel, state_shape, k, v, tail_row, table, name="states")

    def combine(state, weights):
        every = lax.all_gather(state, "sp", axis=0, tiled=False).astype(F32)
        return (jnp.einsum("n,nhrf->hrf", weights, every) * table[4]).astype(BF16)

    prior_state = combine(own_state, from_prior)
    att, inv = call(
        forward_kernel,
        (jax.ShapeDtypeStruct(v.shape, BF16), jax.ShapeDtypeStruct(v.shape, F32)),
        q, k, v, prior_state, doc_col, doc_row, prior_col, table,
        scratch=[pltpu.VMEM((tok, tok), F32)],
        name="attend",
    )
    output, g_hidden, grad_gain_two, dg, du, dd = ffn(
        tokens, att, out_t, gain_two[None, :], cotangent, wg, wu, wd
    )
    g_branch = g_hidden.astype(BF16)
    grad_out = mm(g_branch, att, TN)
    g_att = mm(g_branch, out_t).astype(BF16)
    ghat, own_later = call(
        ghat_kernel,
        (jax.ShapeDtypeStruct((heads // 2, tok, 256), BF16), state_shape),
        q, g_att, att, inv, head_row, table,
        name="ghat",
    )
    later_state = combine(own_later, from_later)
    gq, gk, gv = call(
        backward_kernel,
        (
            jax.ShapeDtypeStruct(q.shape, BF16),
            jax.ShapeDtypeStruct(q.shape, BF16),
            jax.ShapeDtypeStruct(v.shape, BF16),
        ),
        q, k, v, ghat, prior_state, later_state, doc_col, doc_row, prior_col, later_col, table,
        scratch=[pltpu.VMEM((tok, tok), F32), pltpu.VMEM(q.shape, F32), pltpu.VMEM(q.shape, F32)],
        name="attend_back",
    )
    g_proj = jnp.concatenate([gq, gk, gv], axis=1)
    grad_joint = mm(normed_one, g_proj, TN)
    g_norm1 = mm(g_proj, w_joint, NT)
    g_in, grad_gain_one = rms_back(resid, gain_one, g_norm1)
    grad_input = g_hidden + g_in

    def reduced(grad):
        part = lax.psum_scatter(grad.astype(BF16), "sp", scatter_dimension=0, tiled=True)
        return lax.psum(part, "dp").astype(F32)

    s_joint = reduced(grad_joint)
    return (
        output,
        grad_input,
        reduced(grad_gain_one),
        s_joint[:, :lanes],
        s_joint[:, lanes : 2 * lanes],
        s_joint[:, 2 * lanes :],
        reduced(grad_out).T,
        reduced(grad_gain_two[0]),
        reduced(dg),
        reduced(du),
        reduced(dd).T,
    )


def solution(mesh):
    placed_in = (
        P(("dp", "sp"), None), P("dp", None), P("sp"), P("sp", None), P("sp", None), P("sp", None),
        P(None, "sp"), P("sp"), P("sp", None), P("sp", None), P(None, "sp"), P(("dp", "sp"), None),
    )
    return jax.shard_map(
        body,
        mesh=mesh,
        in_specs=placed_in,
        out_specs=(
            P(("dp", "sp"), None), P(("dp", "sp"), None), P("sp"), P("sp", None), P("sp", None),
            P("sp", None), P(None, "sp"), P("sp"), P("sp", None), P("sp", None), P(None, "sp"),
        ),
        check_vma=False,
    )
```

```python
import functools
import math

import jax
import jax.numpy as jnp
import numpy as np
from jax import lax
from jax.experimental import pallas as pl
from jax.experimental.pallas import tpu as pltpu
from jax.sharding import PartitionSpec as P

FEAT = 16
HEAD_V = 64
EPSILON = 1e-05
BF16 = jnp.bfloat16
F32 = jnp.float32
BLK = 256
PAD_F = 256
ROWS_S = 80
NN = (((1,), (0,)), ((), ()))
NT = (((1,), (1,)), ((), ()))
TN = (((0,), (0,)), ((), ()))


def mm(a, b, dims=NN):
    return lax.dot_general(a, b, dims, preferred_element_type=F32)


def feature_table():
    rows = []
    for a in range(FEAT):
        for b in range(a, FEAT):
            rows.append((a, b, 0.0, 0.0, 1.0 if a == b else 2.0))
    for a in range(FEAT):
        rows.append((a, -1, 0.0, 1.0, 8.0))
    rows.append((-1, -1, 1.0, 1.0, 32.0))
    while len(rows) < PAD_F:
        rows.append((-1, -1, 0.0, 0.0, 0.0))
    table = np.zeros((8, PAD_F), np.float32)
    table[:5] = np.array(rows, np.float32).T
    return jnp.asarray(table)


def selectors(table, head, lanes):
    row = lax.broadcasted_iota(jnp.int32, (lanes, PAD_F), 0).astype(F32)
    base = (head * FEAT).astype(F32)
    first = jnp.where((row == table[0:1] + base) & (table[0:1] >= 0), 1.0, 0.0).astype(BF16)
    second = jnp.where((row == table[1:2] + base) & (table[1:2] >= 0), 1.0, 0.0).astype(BF16)
    return first, second


def head_lanes(values, head, scale=1):
    lane = lax.broadcasted_iota(jnp.int32, values.shape, 1)
    return jnp.where(lane // FEAT == head, values * scale, jnp.zeros_like(values))


def factors(values, sel, table):
    one = mm(values, sel[0]) + table[2:3]
    two = mm(values, sel[1]) + table[3:4]
    return one, two


def with_ones(v_pair):
    return jnp.concatenate([v_pair, jnp.ones_like(v_pair)], axis=1)


class Copies:
    def __init__(self, send_sem, recv_sem):
        self.send_sem, self.recv_sem, self.made = send_sem, recv_sem, {}

    def add(self, name, src, dst, device):
        self.made[name] = (src, dst, len(self.made), device)

    def get(self, name):
        src, dst, index, device = self.made[name]
        return pltpu.make_async_remote_copy(
            src_ref=src,
            dst_ref=dst,
            send_sem=self.send_sem.at[index],
            recv_sem=self.recv_sem.at[index],
            device_id=device,
            device_id_type=pl.DeviceIdType.MESH,
        )

    def start(self, *names):
        for name in names:
            self.get(name).start()

    def arrived(self, *names):
        for name in names:
            self.get(name).wait_recv()

    def sent(self, *names):
        for name in names:
            self.get(name).wait_send()


GROUP = 4


def place(n_sp):
    dp, sp = lax.axis_index("dp"), lax.axis_index("sp")
    g = lax.rem(dp, GROUP)
    gy, gx = g // 2, lax.rem(g, 2)
    z, c = sp // 2, lax.rem(sp, 2)
    across_x = (dp - g + gy * 2 + (1 - gx), sp)
    across_y = (dp - g + (1 - gy) * 2 + gx, sp)
    diagonal = (dp - g + (1 - gy) * 2 + (1 - gx), sp)
    partner = (dp, z * 2 + (1 - c))
    return dp, sp, g, gy, gx, z, c, across_x, across_y, diagonal, partner


class Gather:
    def __init__(self, copies, tag, n_z, own, full, where):
        dp, sp, g, gy, gx, z, c, across_x, across_y, _, partner = where
        self.copies, self.tag, self.n_z = copies, tag, n_z
        shard = own.shape[0]
        quarter = shard // GROUP
        half = quarter // 2
        sub = 16 if half % 16 == 0 else 8

        def rows(zz, gg, count, hh=0):
            start = (zz * 2 + c) * shard + gg * quarter + hh * half
            return full.at[pl.ds(pl.multiple_of(start, sub), count)]

        gx_of, gy_of = gy * 2 + (1 - gx), (1 - gy) * 2 + gx
        diag = (1 - gy) * 2 + (1 - gx)
        add = lambda name, src, dst, device: copies.add((tag, name), src, dst, device)
        mine = own.at[pl.ds(pl.multiple_of(g * quarter, sub), quarter)]
        self.own_place = rows(z, 0, shard)
        add("c0", own, self.own_place, partner)
        for i in range(1, n_z):
            zt = lax.rem(z + i, n_z)
            zs = lax.rem(z + n_z - i, n_z)
            add(f"z{i}", mine, rows(z, g, quarter), (dp, zt * 2 + c))
            here = rows(zs, g, quarter)
            add(f"x{i}", here, here, across_x)
            add(f"y{i}", here, here, across_y)
            add(f"c1{i}", here, here, partner)
            first = rows(zs, gx_of, half)
            add(f"d0{i}", first, first, across_y)
            second = rows(zs, gy_of, half, 1)
            add(f"d1{i}", second, second, across_x)
            for name, gg in (("c2", gx_of), ("c3", gy_of), ("c4", diag)):
                there = rows(zs, gg, quarter)
                add(f"{name}{i}", there, there, partner)

    def each(self, *names):
        return [(self.tag, f"{name}{i}") for i in range(1, self.n_z) for name in names]

    def stage(self, n):
        copies = self.copies
        if n == 0:
            copies.start(*self.each("z"), (self.tag, "c0"))
        elif n == 1:
            for i in range(1, self.n_z):
                copies.arrived((self.tag, f"z{i}"))
                copies.start(*[(self.tag, f"{name}{i}") for name in ("x", "y", "c1")])
        elif n == 2:
            for i in range(1, self.n_z):
                copies.arrived((self.tag, f"x{i}"), (self.tag, f"y{i}"))
                copies.start(*[(self.tag, f"{name}{i}") for name in ("d0", "d1", "c2", "c3")])
        elif n == 3:
            for i in range(1, self.n_z):
                copies.arrived((self.tag, f"d0{i}"), (self.tag, f"d1{i}"))
                copies.start((self.tag, f"c4{i}"))
        else:
            copies.arrived((self.tag, "c0"), *self.each("c1", "c2", "c3", "c4"))
            copies.sent((self.tag, "c0"), *self.each("z", "x", "y", "c1", "d0", "d1", "c2", "c3", "c4"))


def n_copies(n_z):
    return 1 + 9 * (n_z - 1)


def meet(devices):
    barrier = pltpu.get_barrier_semaphore()
    for device in devices:
        pl.semaphore_signal(barrier, inc=1, device_id=device, device_id_type=pl.DeviceIdType.MESH)
    pl.semaphore_wait(barrier, len(devices))


def placed(state, side, z_rows):
    zero = jnp.zeros((64, PAD_F), state.dtype)
    values = [state[0:64], zero] if side == 0 else [zero, state[0:64]]
    return jnp.concatenate(values + [z_rows], axis=0)


def rows_sum(values):
    total = values[0]
    for value in values[1:]:
        total = total + value
    return total


def forward_kernel(
    n_sp, x_ref, gains_ref, doc_col_ref, doc_row_ref, prior_ref, tail_ref, passes_ref, table_ref,
    joint_own, out_own, gate_own, up_own, down_own,
    att_ref, inv_ref, q_ref, k_ref, v_ref, normed_ref, state_ref, gain_ref,
    joint_full, out_full, gate_full, up_full, down_full,
    mask_ref, joint_vm, num_ref, den_ref, own_state, in_state, out_state, gains_in,
    send_sem, recv_sem, local_sem,
):
    tok = x_ref.shape[0]
    n_z = n_sp // 2
    lanes = q_ref.shape[1]
    pairs = v_ref.shape[1] // 128
    where = place(n_sp)
    dp, sp, g, gy, gx, z, c, across_x, across_y, diagonal, partner = where
    copies = Copies(send_sem, recv_sem)
    owns = (joint_own, out_own, gate_own, up_own, down_own)
    fulls = (joint_full, out_full, gate_full, up_full, down_full)
    gathers = [Gather(copies, k, n_z, own, full, where) for k, (own, full) in enumerate(zip(owns, fulls))]
    others = [(dp, lax.rem(sp + i, n_sp)) for i in range(1, n_sp)]
    for i, device in enumerate(others, 1):
        copies.add(("gain", i), gains_ref, gains_in.at[i - 1], device)
    following = (dp, lax.rem(sp + 1, n_sp))
    copies.add("state", out_state, in_state, following)
    meet(others + [across_x, across_y])
    copies.start(*[("gain", i) for i in range(1, n_sp)])
    for gather in gathers:
        gather.stage(0)
    local = [
        pltpu.make_async_copy(own, gather.own_place, local_sem.at[k])
        for k, (own, gather) in enumerate(zip(owns, gathers))
    ]
    for copy in local:
        copy.start()

    table = table_ref[...]
    row = lax.broadcasted_iota(jnp.int32, (tok, tok), 0)
    col = lax.broadcasted_iota(jnp.int32, (tok, tok), 1)
    mask_ref[...] = jnp.where((row >= col) & (doc_col_ref[...] == doc_row_ref[...]), 1.0, 0.0)
    copies.arrived(*[("gain", i) for i in range(1, n_sp)])
    gain_ref[...] = gains_ref[...] + rows_sum([gains_in[i] for i in range(n_sp - 1)])
    x = x_ref[...].astype(F32)
    scale = lax.rsqrt(jnp.mean(x * x, axis=1, keepdims=True) + EPSILON)
    normed_ref[...] = (x * scale * gain_ref[0:1]).astype(BF16)
    gathers[0].stage(1)
    gathers[0].stage(2)
    gathers[0].stage(3)
    gathers[1].stage(1)
    gathers[2].stage(1)
    gathers[0].stage(4)
    for copy in local:
        copy.wait()
    fetch = pltpu.make_async_copy(joint_full, joint_vm, local_sem.at[0])
    fetch.start()
    fetch.wait()
    wide = joint_vm.shape[1]
    for first in range(0, wide, BLK):
        part = mm(normed_ref[...], joint_vm[:, first : first + BLK]).astype(BF16)
        if first < lanes:
            q_ref[:, first : first + BLK] = part
        elif first < 2 * lanes:
            k_ref[:, first - lanes : first - lanes + BLK] = part
        else:
            v_ref[:, first - 2 * lanes : first - 2 * lanes + BLK] = part

    tail = tail_ref[...]

    def at(p, step, *todo):
        @pl.when(p == step)
        def _():
            for k, n in todo:
                gathers[k].stage(n)

    def state_pair(p, carry):
        at(p, 2, (3, 1))
        at(p, 5, (1, 2), (2, 2))
        columns = pl.ds(pl.multiple_of(p * 128, 128), 128)
        v_t = v_ref[:, columns].astype(F32).T * tail
        ones = jnp.broadcast_to(tail, (16, tail.shape[1]))
        for side in range(2):
            head = p * 2 + side
            sel = selectors(table, head, lanes)
            one, two = factors(k_ref[...], sel, table)
            phi = (one * two).astype(BF16)
            lhs = jnp.concatenate([v_t[side * 64 : side * 64 + 64], ones], axis=0)
            own_state[head] = mm(lhs.astype(BF16), phi).astype(BF16)
        return carry

    lax.fori_loop(0, pairs, state_pair, 0)

    turn = jnp.minimum((z * 11 + c * 2 + 2) // 3, pairs - 1)

    def pass_state(p):
        @pl.when((p == turn) & (sp > 0))
        def _():
            copies.arrived("state")

        @pl.when((p == turn) & (sp == 0))
        def _():
            in_state[...] = jnp.zeros_like(in_state)

        @pl.when((p == turn) & (sp < n_sp - 1))
        def _():
            go_on = passes_ref[0:1, :]
            for head in range(in_state.shape[0]):
                out_state[head] = (
                    own_state[head].astype(F32) + go_on * in_state[head].astype(F32)
                ).astype(BF16)
            copies.start("state")

    lane = lax.broadcasted_iota(jnp.int32, (BLK, 128), 1)

    def intra_pair(p, carry):
        at(p, 0, (4, 1))
        at(p, 2, (1, 3), (2, 3))
        at(p, 4, (3, 2))
        at(p, 6, (4, 2))
        pass_state(p)
        columns = pl.ds(pl.multiple_of(p * 128, 128), 128)
        v_hat = with_ones(v_ref[:, columns])
        heads = [head_lanes(q_ref[...], p * 2 + side) for side in range(2)]
        for i in range(tok // BLK):
            rows = slice(i * BLK, (i + 1) * BLK)
            keys = slice(0, (i + 1) * BLK)
            totals = []
            for side in range(2):
                t = mm(heads[side][rows], k_ref[keys, :], NT) + 4.0
                w = ((t * t + 16.0) * mask_ref[rows, keys]).astype(BF16)
                totals.append(mm(w, v_hat[keys]))
            num_ref[rows, columns] = jnp.where(lane < 64, totals[0][:, :128], totals[1][:, :128])
            den_ref[rows, columns] = jnp.where(lane < 64, totals[0][:, 128:], totals[1][:, 128:])
        return carry

    lax.fori_loop(0, pairs, intra_pair, 0)
    for head in range(in_state.shape[0]):
        state_ref[head] = (in_state[head].astype(F32) * table[4:5]).astype(BF16)
    prior = prior_ref[...]
    wide_lane = lax.broadcasted_iota(jnp.int32, (tok, 128), 1)

    def inter_pair(p, carry):
        at(p, 2, (3, 3))
        at(p, 6, (4, 3))
        columns = pl.ds(pl.multiple_of(p * 128, 128), 128)
        totals = []
        for side in range(2):
            head = p * 2 + side
            sel = selectors(table, head, lanes)
            state = state_ref[head]
            z_rows = jnp.broadcast_to(state[64:65].astype(F32), (128, PAD_F)).astype(BF16)
            one, two = factors(q_ref[...], sel, table)
            totals.append(mm((one * two).astype(BF16), placed(state, side, z_rows), NT) * prior)
        num = num_ref[:, columns] + jnp.where(wide_lane < 64, totals[0][:, :128], totals[1][:, :128])
        den = den_ref[:, columns] + jnp.where(wide_lane < 64, totals[0][:, 128:], totals[1][:, 128:])
        inv = 1.0 / den
        inv_ref[:, columns] = inv
        att_ref[:, columns] = (num * inv).astype(BF16)
        return carry

    lax.fori_loop(0, pairs, inter_pair, 0)
    for gather in gathers[1:]:
        gather.stage(4)
    copies.sent(*[("gain", i) for i in range(1, n_sp)])

    @pl.when(sp < n_sp - 1)
    def _():
        copies.sent("state")


def forward(n_sp, x, gains, doc_col, doc_row, prior_col, tail_row, passes, table, shards):
    tok, dim = x.shape
    joint = shards[0]
    lanes = (joint.shape[1] // (2 * FEAT + HEAD_V)) * FEAT
    values = joint.shape[1] - 2 * lanes
    heads = lanes // FEAT
    vmem, anywhere = pl.BlockSpec(memory_space=pltpu.VMEM), pl.BlockSpec(memory_space=pl.ANY)
    n_z = n_sp // 2
    sems = 5 * n_copies(n_z) + n_sp
    shape = jax.ShapeDtypeStruct
    return pl.pallas_call(
        functools.partial(forward_kernel, n_sp),
        out_shape=(
            shape((tok, values), BF16), shape((tok, values), F32), shape((tok, lanes), BF16),
            shape((tok, lanes), BF16), shape((tok, values), BF16), shape((tok, dim), BF16),
            shape((heads, ROWS_S, PAD_F), BF16), shape((8, dim), F32),
        ) + tuple(shape((s.shape[0] * n_sp, s.shape[1]), BF16) for s in shards),
        in_specs=[vmem] * 8 + [anywhere] * 5,
        out_specs=(vmem,) * 8 + (anywhere,) * 5,
        scratch_shapes=[
            pltpu.VMEM((tok, tok), F32),
            pltpu.VMEM((dim, joint.shape[1]), BF16),
            pltpu.VMEM((tok, values), F32),
            pltpu.VMEM((tok, values), F32),
            pltpu.VMEM((heads, ROWS_S, PAD_F), BF16),
            pltpu.VMEM((heads, ROWS_S, PAD_F), BF16),
            pltpu.VMEM((heads, ROWS_S, PAD_F), BF16),
            pltpu.VMEM((n_sp - 1, 8, dim), F32),
            pltpu.SemaphoreType.DMA((sems,)),
            pltpu.SemaphoreType.DMA((sems,)),
            pltpu.SemaphoreType.DMA((5,)),
        ],
        compiler_params=pltpu.CompilerParams(
            collective_id=0, has_side_effects=True, vmem_limit_bytes=60 << 20
        ),
        name="forward",
    )(x, gains, doc_col, doc_row, prior_col, tail_row, passes, table, *shards)


def ghat_kernel(q_ref, g_ref, att_ref, inv_ref, head_row_ref, table_ref, ghat_ref, out_ref):
    tok, lanes = q_ref.shape
    table = table_ref[...]
    r = lax.broadcasted_iota(jnp.int32, (128, 128), 0)
    c = lax.broadcasted_iota(jnp.int32, (128, 128), 1)
    same = jnp.where(r // 64 == c // 64, 1.0, 0.0).astype(BF16)
    lane = lax.broadcasted_iota(jnp.int32, (tok, 128), 1) % 64
    head_row = head_row_ref[...]

    def pair(p, carry):
        columns = pl.ds(pl.multiple_of(p * 128, 128), 128)
        scaled = g_ref[:, columns].astype(F32) * inv_ref[:, columns]
        product = scaled * att_ref[:, columns].astype(F32)
        high = product.astype(BF16)
        low = (product - high.astype(F32)).astype(BF16)
        dots = -(mm(high, same) + mm(low, same))
        dots_high = dots.astype(BF16)
        dots_low = (dots - dots_high.astype(F32)).astype(BF16)
        extra = jnp.where(lane == 0, dots_high, jnp.where(lane == 1, dots_low, jnp.zeros_like(dots_low)))
        ghat = jnp.concatenate([scaled.astype(BF16), extra], axis=1)
        ghat_ref[p] = ghat
        ghat_t = ghat.astype(F32).T * head_row
        for side in range(2):
            head = p * 2 + side
            sel = selectors(table, head, lanes)
            one, two = factors(q_ref[...], sel, table)
            phi = (one * two).astype(BF16)
            lhs = jnp.concatenate(
                [ghat_t[side * 64 : side * 64 + 64], ghat_t[128 + side * 64 : 128 + side * 64 + 16]], axis=0
            )
            state = mm(lhs.astype(BF16), phi)
            z_row = jnp.sum(state[64:80], axis=0, keepdims=True)
            out_ref[head] = jnp.concatenate(
                [state[0:64], jnp.broadcast_to(z_row, (16, PAD_F))], axis=0
            ).astype(BF16)
        return carry

    lax.fori_loop(0, g_ref.shape[1] // 128, pair, 0)


def backward_kernel(
    q_ref, k_ref, v_ref, ghat_ref, prior_state_ref, later_state_ref, doc_col_ref, doc_row_ref,
    prior_ref, later_ref, table_ref, gq_ref, gk_ref, gv_ref, mask_ref, gq_acc, gk_acc,
):
    tok, lanes = q_ref.shape
    table = table_ref[...]
    row = lax.broadcasted_iota(jnp.int32, (tok, tok), 0)
    col = lax.broadcasted_iota(jnp.int32, (tok, tok), 1)
    mask_ref[...] = jnp.where(
        (row <= col) & (doc_col_ref[...] == doc_row_ref[...]), 1.0, 0.0
    )
    gq_acc[...] = jnp.zeros_like(gq_acc)
    gk_acc[...] = jnp.zeros_like(gk_acc)
    lane = lax.broadcasted_iota(jnp.int32, (tok, 256), 1)
    first_row = lax.broadcasted_iota(jnp.int32, (128, PAD_F), 0)

    def pair(p, carry):
        columns = pl.ds(pl.multiple_of(p * 128, 128), 128)
        v_hat = with_ones(v_ref[:, columns])
        gv = [jnp.zeros((BLK, 128), F32) for _ in range(tok // BLK)]
        gv_inter = None
        for side in range(2):
            head = p * 2 + side
            sel = selectors(table, head, lanes)
            ghat = jnp.where((lane % 128) // 64 == side, ghat_ref[p], jnp.zeros((tok, 256), BF16))
            q_head = head_lanes(q_ref[...], head)
            q_twice = q_head + q_head
            k_twice = head_lanes(k_ref[...], head, 2)

            later = later_state_ref[head]
            z_one = jnp.where(first_row == 0, later[64:65], jnp.zeros((128, PAD_F), BF16))
            rows_n = placed(later, side, z_one)
            k_one, k_two = factors(k_ref[...], sel, table)
            phi_k = (k_one * k_two).astype(BF16)
            gvi = mm(phi_k, rows_n[0:128], NT)
            gv_inter = gvi if gv_inter is None else gv_inter + gvi
            d_phi = mm(v_hat, rows_n) * later_ref[...]
            gk_acc[...] += mm((d_phi * k_two).astype(BF16), sel[0], NT) + mm(
                (d_phi * k_one).astype(BF16), sel[1], NT
            )

            prior = prior_state_ref[head]
            z_two = jnp.where(first_row // 2 == side * 32, prior[64:65], jnp.zeros((128, PAD_F), BF16))
            rows_p = placed(prior, side, z_two)
            q_one, q_two = factors(q_ref[...], sel, table)
            d_phi = mm(ghat, rows_p) * prior_ref[...]
            gq_acc[...] += mm((d_phi * q_two).astype(BF16), sel[0], NT) + mm(
                (d_phi * q_one).astype(BF16), sel[1], NT
            )

            for j in range(tok // BLK):
                rows = slice(j * BLK, (j + 1) * BLK)
                onward = slice(j * BLK, tok)
                t = mm(k_ref[rows, :], q_head[onward], NT) + 4.0
                g_w = mm(v_hat[rows], ghat[onward], NT)
                mask = mask_ref[rows, onward]
                masked_t = t * mask
                w = (masked_t * t + 16.0 * mask).astype(BF16)
                g_s = (g_w * masked_t).astype(BF16)
                gv[j] = gv[j] + mm(w, ghat[onward, 0:128])
                gk_acc[rows, :] += mm(g_s, q_twice[onward])
                gq_acc[onward, :] += mm(g_s, k_twice[rows], TN)
        for j in range(tok // BLK):
            rows = slice(j * BLK, (j + 1) * BLK)
            gv_ref[rows, columns] = (gv[j] + gv_inter[rows] * later_ref[rows, :]).astype(BF16)
        return carry

    lax.fori_loop(0, v_ref.shape[1] // 128, pair, 0)
    gq_ref[...] = gq_acc[...].astype(BF16)
    gk_ref[...] = gk_acc[...].astype(BF16)


def call(kernel, out_shape, *args, scratch=(), name=None):
    vmem = pl.BlockSpec(memory_space=pltpu.VMEM)
    return pl.pallas_call(
        kernel,
        out_shape=out_shape,
        in_specs=[vmem] * len(args),
        out_specs=jax.tree.map(lambda _: vmem, out_shape),
        scratch_shapes=list(scratch),
        compiler_params=pltpu.CompilerParams(vmem_limit_bytes=60 << 20),
        name=name,
    )(*args)


def ffn_kernel(
    width, x_ref, att_ref, out_t_ref, gain_ref, cot_ref, wg_ref, wu_ref, wd_ref,
    output_ref, gh_ref, ggain_ref, dg_ref, du_ref, dd_ref,
    hid, n2, n2_t, cot_t, acc_o, acc_n,
):
    step = pl.program_id(0)

    @pl.when(step == 0)
    def _():
        hidden = x_ref[...].astype(F32) + mm(att_ref[...], out_t_ref[...], NT)
        hid[...] = hidden
        scale = lax.rsqrt(jnp.mean(hidden * hidden, axis=1, keepdims=True) + EPSILON)
        normed = (hidden * scale * gain_ref[...]).astype(BF16)
        n2[...] = normed
        n2_t[...] = normed.T
        cot_t[...] = cot_ref[...].T
        acc_o[...] = jnp.zeros_like(acc_o)
        acc_n[...] = jnp.zeros_like(acc_n)

    chunk = wg_ref.shape[1]
    lane = lax.broadcasted_iota(jnp.int32, wg_ref.shape, 1) + step * chunk
    valid = lane < width
    zero = jnp.zeros(wg_ref.shape, BF16)
    wg = jnp.where(valid, wg_ref[...], zero)
    wu = jnp.where(valid, wu_ref[...], zero)
    wd = jnp.where(valid, wd_ref[...], zero)
    gate = mm(n2[...], wg)
    up = mm(n2[...], wu)
    g_mixed = mm(cot_ref[...], wd)
    sig = 1.0 / (1.0 + jnp.exp(-gate))
    act = gate * sig
    mixed = (act * up).astype(BF16)
    g_gate = (g_mixed * up * sig * (1.0 + gate * (1.0 - sig))).astype(BF16)
    g_up = (g_mixed * act).astype(BF16)
    dd_ref[...] = mm(cot_t[...], mixed).astype(BF16)
    dg_ref[...] = mm(n2_t[...], g_gate).astype(BF16)
    du_ref[...] = mm(n2_t[...], g_up).astype(BF16)
    acc_o[...] += mm(mixed, wd, NT)
    acc_n[...] += mm(g_gate, wg, NT) + mm(g_up, wu, NT)

    @pl.when(step == pl.num_programs(0) - 1)
    def _():
        hidden = hid[...]
        output_ref[...] = (hidden + acc_o[...]).astype(BF16)
        scale = lax.rsqrt(jnp.mean(hidden * hidden, axis=1, keepdims=True) + EPSILON)
        e = acc_n[...]
        ggain_ref[...] = jnp.sum(e * hidden * scale, axis=0, keepdims=True)
        eg = e * gain_ref[...]
        inner = jnp.mean(eg * hidden, axis=1, keepdims=True)
        gh_ref[...] = (
            cot_ref[...].astype(F32) + scale * eg - hidden * (scale * scale * scale * inner)
        )


def ffn(x, att, out_t, gain, cot, wg, wu, wd):
    tok, dim = x.shape
    width = wg.shape[1]
    chunk = 256
    whole = lambda shape: pl.BlockSpec(shape, lambda i: (0, 0))
    lanes = pl.BlockSpec((dim, chunk), lambda i: (0, i))
    grad = jax.ShapeDtypeStruct((dim, width), BF16)
    return pl.pallas_call(
        functools.partial(ffn_kernel, width),
        grid=(pl.cdiv(width, chunk),),
        out_shape=(
            jax.ShapeDtypeStruct((tok, dim), BF16),
            jax.ShapeDtypeStruct((tok, dim), F32),
            jax.ShapeDtypeStruct((1, dim), F32),
            grad, grad, grad,
        ),
        in_specs=[
            whole((tok, dim)), whole((tok, dim)), whole((dim, dim)), whole((1, dim)), whole((tok, dim)),
            lanes, lanes, lanes,
        ],
        out_specs=(whole((tok, dim)), whole((tok, dim)), whole((1, dim)), lanes, lanes, lanes),
        scratch_shapes=[
            pltpu.VMEM((tok, dim), F32),
            pltpu.VMEM((tok, dim), BF16),
            pltpu.VMEM((dim, tok), BF16),
            pltpu.VMEM((dim, tok), BF16),
            pltpu.VMEM((tok, dim), F32),
            pltpu.VMEM((tok, dim), F32),
        ],
        compiler_params=pltpu.CompilerParams(vmem_limit_bytes=60 << 20),
        name="ffn",
    )(x, att, out_t, gain, cot, wg, wu, wd)


def rms_scale(values, weights):
    return values * lax.rsqrt(jnp.mean(values * values, axis=-1, keepdims=True) + EPSILON) * weights


def rms_back(u, gain, e):
    scale = lax.rsqrt(jnp.mean(u * u, axis=-1, keepdims=True) + EPSILON)
    grad_gain = jnp.sum(e * u * scale, axis=0)
    eg = e * gain
    inner = jnp.mean(eg * u, axis=-1, keepdims=True)
    return scale * eg - u * (scale * scale * scale * inner), grad_gain


def body(
    tokens, doc_ids, gain_attn, w_query, w_key, w_value, w_out, gain_mlp, w_gate, w_up, w_down, cotangent
):
    n_sp = lax.axis_size("sp")
    me = lax.axis_index("sp")
    tok = tokens.shape[0]
    heads = w_query.shape[1] // FEAT
    table = feature_table()
    doc_all = doc_ids[0]
    doc = lax.dynamic_slice(doc_all, (me * tok,), (tok,))
    ends = doc_all.reshape(n_sp, tok)
    firsts, lasts = ends[:, 0], ends[:, tok - 1]
    my_first, my_last = doc[0], doc[tok - 1]
    prev_last = jnp.where(me > 0, lasts[jnp.maximum(me - 1, 0)], -1)
    next_first = jnp.where(me < n_sp - 1, firsts[jnp.minimum(me + 1, n_sp - 1)], -1)
    order = jnp.arange(n_sp)
    from_later = ((order > me) & (firsts == next_first)).astype(F32)
    tail_row = (doc == my_last).astype(F32)[None, :]
    head_row = (doc == my_first).astype(F32)[None, :]
    prior_col = (doc == prev_last).astype(F32)[:, None]
    later_col = (doc == next_first).astype(F32)[:, None]
    doc_col, doc_row = doc[:, None], doc[None, :]

    width = gain_attn.shape[0]
    dim = tokens.shape[1]
    gains = lax.dynamic_update_slice(
        jnp.zeros((8, dim), F32), jnp.stack([gain_attn, gain_mlp]).astype(F32), (0, me * width)
    )
    go_on = jnp.full((8, PAD_F), (my_last == prev_last).astype(F32))
    shards = (
        jnp.concatenate([w_query, w_key, w_value], axis=1), w_out.T, w_gate, w_up, w_down.T
    )
    (
        att, inv, q, k, v, normed_one, prior_state, gain, w_joint, out_t, wg, wu, wd
    ) = forward(n_sp, tokens, gains, doc_col, doc_row, prior_col, tail_row, go_on, table, shards)
    gain_one, gain_two = gain[0], gain[1]
    resid = tokens.astype(F32)
    lanes = heads * FEAT
    state_shape = jax.ShapeDtypeStruct((heads, ROWS_S, PAD_F), BF16)

    def combine(state, weights):
        every = lax.all_gather(state, "sp", axis=0, tiled=False).astype(F32)
        return (jnp.einsum("n,nhrf->hrf", weights, every) * table[4]).astype(BF16)

    output, g_hidden, grad_gain_two, dg, du, dd = ffn(
        tokens, att, out_t, gain_two[None, :], cotangent, wg, wu, wd
    )
    g_branch = g_hidden.astype(BF16)
    grad_out = mm(g_branch, att, TN)
    g_att = mm(g_branch, out_t).astype(BF16)
    ghat, own_later = call(
        ghat_kernel,
        (jax.ShapeDtypeStruct((heads // 2, tok, 256), BF16), state_shape),
        q, g_att, att, inv, head_row, table,
        name="ghat",
    )
    later_state = combine(own_later, from_later)
    gq, gk, gv = call(
        backward_kernel,
        (
            jax.ShapeDtypeStruct(q.shape, BF16),
            jax.ShapeDtypeStruct(q.shape, BF16),
            jax.ShapeDtypeStruct(v.shape, BF16),
        ),
        q, k, v, ghat, prior_state, later_state, doc_col, doc_row, prior_col, later_col, table,
        scratch=[pltpu.VMEM((tok, tok), F32), pltpu.VMEM(q.shape, F32), pltpu.VMEM(q.shape, F32)],
        name="attend_back",
    )
    g_proj = jnp.concatenate([gq, gk, gv], axis=1)
    grad_joint = mm(normed_one, g_proj, TN)
    g_norm1 = mm(g_proj, w_joint, NT)
    g_in, grad_gain_one = rms_back(resid, gain_one, g_norm1)
    grad_input = g_hidden + g_in

    def reduced(grad):
        part = lax.psum_scatter(grad.astype(BF16), "sp", scatter_dimension=0, tiled=True)
        return lax.psum(part, "dp").astype(F32)

    s_joint = reduced(grad_joint)
    return (
        output,
        grad_input,
        reduced(grad_gain_one),
        s_joint[:, :lanes],
        s_joint[:, lanes : 2 * lanes],
        s_joint[:, 2 * lanes :],
        reduced(grad_out).T,
        reduced(grad_gain_two[0]),
        reduced(dg),
        reduced(du),
        reduced(dd).T,
    )


def solution(mesh):
    placed_in = (
        P(("dp", "sp"), None), P("dp", None), P("sp"), P("sp", None), P("sp", None), P("sp", None),
        P(None, "sp"), P("sp"), P("sp", None), P("sp", None), P(None, "sp"), P(("dp", "sp"), None),
    )
    return jax.shard_map(
        body,
        mesh=mesh,
        in_specs=placed_in,
        out_specs=(
            P(("dp", "sp"), None), P(("dp", "sp"), None), P("sp"), P("sp", None), P("sp", None),
            P("sp", None), P(None, "sp"), P("sp"), P("sp", None), P("sp", None), P(None, "sp"),
        ),
        check_vma=False,
    )
```

```python
import functools
import math

import jax
import jax.numpy as jnp
import numpy as np
from jax import lax
from jax.experimental import pallas as pl
from jax.experimental.pallas import tpu as pltpu
from jax.sharding import PartitionSpec as P

FEAT = 16
HEAD_V = 64
EPSILON = 1e-05
BF16 = jnp.bfloat16
F32 = jnp.float32
BLK = 256
PAD_F = 256
ROWS_S = 80
NN = (((1,), (0,)), ((), ()))
NT = (((1,), (1,)), ((), ()))
TN = (((0,), (0,)), ((), ()))


def mm(a, b, dims=NN):
    return lax.dot_general(a, b, dims, preferred_element_type=F32)


def feature_table():
    rows = []
    for a in range(FEAT):
        for b in range(a, FEAT):
            rows.append((a, b, 0.0, 0.0, 1.0 if a == b else 2.0))
    for a in range(FEAT):
        rows.append((a, -1, 0.0, 1.0, 8.0))
    rows.append((-1, -1, 1.0, 1.0, 32.0))
    while len(rows) < PAD_F:
        rows.append((-1, -1, 0.0, 0.0, 0.0))
    table = np.zeros((8, PAD_F), np.float32)
    table[:5] = np.array(rows, np.float32).T
    return jnp.asarray(table)


def selectors(table, head, lanes):
    row = lax.broadcasted_iota(jnp.int32, (lanes, PAD_F), 0).astype(F32)
    base = (head * FEAT).astype(F32)
    first = jnp.where((row == table[0:1] + base) & (table[0:1] >= 0), 1.0, 0.0).astype(BF16)
    second = jnp.where((row == table[1:2] + base) & (table[1:2] >= 0), 1.0, 0.0).astype(BF16)
    return first, second


def head_lanes(values, head, scale=1):
    lane = lax.broadcasted_iota(jnp.int32, values.shape, 1)
    return jnp.where(lane // FEAT == head, values * scale, jnp.zeros_like(values))


def factors(values, sel, table):
    one = mm(values, sel[0]) + table[2:3]
    two = mm(values, sel[1]) + table[3:4]
    return one, two


def with_ones(v_pair):
    return jnp.concatenate([v_pair, jnp.ones_like(v_pair)], axis=1)


class Copies:
    def __init__(self, send_sem, recv_sem):
        self.send_sem, self.recv_sem, self.made = send_sem, recv_sem, {}

    def add(self, name, src, dst, device):
        self.made[name] = (src, dst, len(self.made), device)

    def get(self, name):
        src, dst, index, device = self.made[name]
        return pltpu.make_async_remote_copy(
            src_ref=src,
            dst_ref=dst,
            send_sem=self.send_sem.at[index],
            recv_sem=self.recv_sem.at[index],
            device_id=device,
            device_id_type=pl.DeviceIdType.MESH,
        )

    def start(self, *names):
        for name in names:
            self.get(name).start()

    def arrived(self, *names):
        for name in names:
            self.get(name).wait_recv()

    def sent(self, *names):
        for name in names:
            self.get(name).wait_send()


GROUP = 4


def place(n_sp):
    dp, sp = lax.axis_index("dp"), lax.axis_index("sp")
    g = lax.rem(dp, GROUP)
    gy, gx = g // 2, lax.rem(g, 2)
    z, c = sp // 2, lax.rem(sp, 2)
    across_x = (dp - g + gy * 2 + (1 - gx), sp)
    across_y = (dp - g + (1 - gy) * 2 + gx, sp)
    diagonal = (dp - g + (1 - gy) * 2 + (1 - gx), sp)
    partner = (dp, z * 2 + (1 - c))
    return dp, sp, g, gy, gx, z, c, across_x, across_y, diagonal, partner


class Gather:
    def __init__(self, copies, tag, n_z, own, full, where):
        dp, sp, g, gy, gx, z, c, across_x, across_y, _, partner = where
        self.copies, self.tag, self.n_z = copies, tag, n_z
        shard, width = own.shape
        quarter = shard // GROUP
        lower, upper = pl.ds(0, width // 2), pl.ds(width // 2, width // 2)

        def rows(zz, gg, count, lanes=None):
            start = pl.multiple_of((zz * 2 + c) * shard + gg * quarter, 16)
            return full.at[pl.ds(start, count)] if lanes is None else full.at[pl.ds(start, count), lanes]

        gx_of, gy_of = gy * 2 + (1 - gx), (1 - gy) * 2 + gx
        diag = (1 - gy) * 2 + (1 - gx)
        add = lambda name, src, dst, device: copies.add((tag, name), src, dst, device)
        mine = own.at[pl.ds(pl.multiple_of(g * quarter, 16), quarter)]
        self.own_place = rows(z, 0, shard)
        add("c0", own, self.own_place, partner)
        for i in range(1, n_z):
            zt = lax.rem(z + i, n_z)
            zs = lax.rem(z + n_z - i, n_z)
            add(f"z{i}", mine, rows(z, g, quarter), (dp, zt * 2 + c))
            here = rows(zs, g, quarter)
            add(f"x{i}", here, here, across_x)
            add(f"y{i}", here, here, across_y)
            add(f"c1{i}", here, here, partner)
            first = rows(zs, gx_of, quarter, lower)
            add(f"d0{i}", first, first, across_y)
            second = rows(zs, gy_of, quarter, upper)
            add(f"d1{i}", second, second, across_x)
            for name, gg in (("c2", gx_of), ("c3", gy_of), ("c4", diag)):
                there = rows(zs, gg, quarter)
                add(f"{name}{i}", there, there, partner)

    def each(self, *names):
        return [(self.tag, f"{name}{i}") for i in range(1, self.n_z) for name in names]

    def stage(self, n):
        copies = self.copies
        if n == 0:
            copies.start(*self.each("z"), (self.tag, "c0"))
        elif n == 1:
            for i in range(1, self.n_z):
                copies.arrived((self.tag, f"z{i}"))
                copies.start(*[(self.tag, f"{name}{i}") for name in ("x", "y", "c1")])
        elif n == 2:
            for i in range(1, self.n_z):
                copies.arrived((self.tag, f"x{i}"), (self.tag, f"y{i}"))
                copies.start(*[(self.tag, f"{name}{i}") for name in ("d0", "d1", "c2", "c3")])
        elif n == 3:
            for i in range(1, self.n_z):
                copies.arrived((self.tag, f"d0{i}"), (self.tag, f"d1{i}"))
                copies.start((self.tag, f"c4{i}"))
        else:
            copies.arrived((self.tag, "c0"), *self.each("c1", "c2", "c3", "c4"))
            copies.sent((self.tag, "c0"), *self.each("z", "x", "y", "c1", "d0", "d1", "c2", "c3", "c4"))


def n_copies(n_z):
    return 1 + 9 * (n_z - 1)


def meet(devices):
    barrier = pltpu.get_barrier_semaphore()
    for device in devices:
        pl.semaphore_signal(barrier, inc=1, device_id=device, device_id_type=pl.DeviceIdType.MESH)
    pl.semaphore_wait(barrier, len(devices))


def placed(state, side, z_rows):
    zero = jnp.zeros((64, PAD_F), state.dtype)
    values = [state[0:64], zero] if side == 0 else [zero, state[0:64]]
    return jnp.concatenate(values + [z_rows], axis=0)


class Reduce:
    def __init__(self, copies, tag, n_z, where, source, swapped, buffers, final, stage_buf=None, local_sem=None):
        dp, sp, g, gy, gx, z, c, across_x, across_y, diagonal, partner = where
        self.copies, self.tag, self.n_z = copies, tag, n_z
        self.gy, self.gx, self.z, self.c = gy, gx, z, c
        self.source, self.swapped, self.final = source, swapped, final
        self.work, self.first, self.second, self.along = buffers
        self.stage_buf, self.local_sem = stage_buf, local_sem
        work = self.work
        half = work.shape[-1] // 2
        self.halves = (pl.ds(0, half), pl.ds(half, half))
        lower, upper = self.halves
        everything = slice(None)
        add = lambda name, src, dst, device: copies.add((tag, name), src, dst, device)
        add("s", source.at[:, 1 - c], swapped, partner)
        add("a1", work.at[:, :, 1 - gx, everything, lower], self.first.at[0], across_x)
        add("b1", work.at[:, 1 - gy, :, everything, upper], self.first.at[1], across_y)
        add("a2", work.at[:, 1 - gy, gx, everything, lower], self.second.at[0], across_y)
        add("b2", work.at[:, gy, 1 - gx, everything, upper], self.second.at[1], across_x)
        for i in range(1, n_z):
            zt = lax.rem(z + i, n_z)
            add(f"z{i}", work.at[zt, gy, gx], self.along.at[i - 1], (dp, zt * 2 + c))
        for name, device in (("fx", across_x), ("fy", across_y), ("fd", diagonal)):
            add(name, final.at[gy, gx], final.at[gy, gx], device)

    def names(self, *names):
        return [(self.tag, name) for name in names]

    def load(self, zz):
        slot = zz % 2
        return (
            pltpu.make_async_copy(self.source.at[zz, self.c], self.stage_buf.at[slot, 0], self.local_sem.at[slot, 0]),
            pltpu.make_async_copy(self.swapped.at[zz], self.stage_buf.at[slot, 1], self.local_sem.at[slot, 1]),
        )

    def stage(self, n):
        copies, work, gy, gx, n_z = self.copies, self.work, self.gy, self.gx, self.n_z
        zs = ["z%d" % i for i in range(1, n_z)]
        lower, upper = self.halves
        if n == 0:
            copies.start(*self.names("s"))
        elif n == 1:
            copies.arrived(*self.names("s"))
            if self.stage_buf is None:

                def add_held(i, carry):
                    zz, yy, xx = i // 4, lax.rem(i // 2, 2), lax.rem(i, 2)
                    work[zz, yy, xx] = self.source[zz, self.c, yy, xx] + self.swapped[zz, yy, xx]
                    return carry

                lax.fori_loop(0, 4 * n_z, add_held, 0)
                copies.start(*self.names("a1", "b1"))
                return
            for copy in self.load(0):
                copy.start()
            for zz in range(n_z):
                if zz + 1 < n_z:
                    for copy in self.load(zz + 1):
                        copy.start()
                for copy in self.load(zz):
                    copy.wait()
                slot = zz % 2

                def add_quarter(i, carry):
                    yy, xx = i // 2, lax.rem(i, 2)
                    work[zz, yy, xx] = self.stage_buf[slot, 0, yy, xx] + self.stage_buf[slot, 1, yy, xx]
                    return carry

                lax.fori_loop(0, 4, add_quarter, 0)
            copies.start(*self.names("a1", "b1"))
        elif n == 2:
            copies.arrived(*self.names("a1"))

            def add_a(i, carry):
                zz, yy = i // 2, lax.rem(i, 2)
                work[zz, yy, gx, :, lower] = work[zz, yy, gx, :, lower] + self.first[0, zz, yy]
                return carry

            lax.fori_loop(0, 2 * n_z, add_a, 0)
            copies.start(*self.names("a2"))
            copies.arrived(*self.names("b1"))

            def add_b(i, carry):
                zz, xx = i // 2, lax.rem(i, 2)
                work[zz, gy, xx, :, upper] = work[zz, gy, xx, :, upper] + self.first[1, zz, xx]
                return carry

            lax.fori_loop(0, 2 * n_z, add_b, 0)
            copies.start(*self.names("b2"))
        elif n == 3:
            copies.arrived(*self.names("a2", "b2"))

            def add_c(zz, carry):
                work[zz, gy, gx, :, lower] = work[zz, gy, gx, :, lower] + self.second[0, zz]
                work[zz, gy, gx, :, upper] = work[zz, gy, gx, :, upper] + self.second[1, zz]
                return carry

            lax.fori_loop(0, n_z, add_c, 0)
            copies.start(*self.names(*zs))
        elif n == 4:
            copies.arrived(*self.names(*zs))
            total = work[self.z, gy, gx].astype(F32)
            for i in range(n_z - 1):
                total = total + self.along[i].astype(F32)
            self.final[gy, gx] = total.astype(BF16)
            copies.start(*self.names("fx", "fy", "fd"))
        else:
            copies.arrived(*self.names("fx", "fy", "fd"))
            copies.sent(*self.names("s", "a1", "b1", "a2", "b2", "fx", "fy", "fd", *zs))


def reduce_scratch(n_z, rows, width):
    return [
        pltpu.VMEM((n_z, 2, 2, rows, width), BF16),
        pltpu.VMEM((2, n_z, 2, rows, width // 2), BF16),
        pltpu.VMEM((2, n_z, rows, width // 2), BF16),
        pltpu.VMEM((n_z - 1, rows, width), BF16),
    ]


def n_reduce(n_z):
    return 8 + n_z - 1


class Chain:
    def __init__(self, copies, where, n_z, onward, own, mate, carry, out, pass_lead, pass_other):
        dp, sp, g, gy, gx, z, c, across_x, across_y, diagonal, partner = where
        lead = 1 if onward else 0
        self.copies, self.n_z = copies, n_z
        self.own, self.mate, self.carry, self.out = own, mate, carry, out
        self.pass_lead, self.pass_other = pass_lead, pass_other
        self.leads = c == lead
        self.place = z if onward else n_z - 1 - z
        to = lax.rem(z + 1, n_z) if onward else lax.rem(z + n_z - 1, n_z)
        before = lax.rem(z + n_z - 1, n_z) if onward else lax.rem(z + 1, n_z)
        self.next_device, self.last_device = (dp, to * 2 + c), (dp, before * 2 + c)
        copies.add("own", own, mate, partner)
        copies.add("raw", carry, carry, partner)
        copies.add("carry", out, carry, self.next_device)

    def begin(self):
        @pl.when(jnp.logical_not(self.leads))
        def _():
            self.copies.start("own")

        @pl.when(self.leads & (self.place == 0))
        def _():
            self.carry[...] = jnp.zeros_like(self.carry)

    def middle(self, now):
        now = now & self.leads

        @pl.when(now)
        def _():
            self.copies.arrived("own")

        @pl.when(now & (self.place > 0))
        def _():
            self.copies.arrived("carry")

        @pl.when(now)
        def _():
            self.copies.start("raw")

        @pl.when(now & (self.place < self.n_z - 1))
        def _():
            def one(head, carry):
                inner = self.mate[head].astype(F32) + self.pass_other * self.carry[head].astype(F32)
                self.out[head] = (self.own[head].astype(F32) + self.pass_lead * inner).astype(BF16)
                return carry

            lax.fori_loop(0, self.own.shape[0], one, 0)
            self.copies.start("carry")

    def finish(self, result, weights):
        @pl.when(jnp.logical_not(self.leads))
        def _():
            self.copies.arrived("raw")

            def one(head, carry):
                result[head] = (self.carry[head].astype(F32) * weights).astype(BF16)
                return carry

            lax.fori_loop(0, self.own.shape[0], one, 0)

        @pl.when(self.leads)
        def _():
            def one(head, carry):
                total = self.mate[head].astype(F32) + self.pass_other * self.carry[head].astype(F32)
                result[head] = (total * weights).astype(BF16)
                return carry

            lax.fori_loop(0, self.own.shape[0], one, 0)

    def drain(self):
        @pl.when(jnp.logical_not(self.leads))
        def _():
            self.copies.sent("own")

        @pl.when(self.leads)
        def _():
            self.copies.sent("raw")

        @pl.when(self.leads & (self.place < self.n_z - 1))
        def _():
            self.copies.sent("carry")


class Documents:
    def __init__(self, doc_ref, sp):
        self.ref, self.n_sp, self.tok = doc_ref, doc_ref.shape[0], doc_ref.shape[1]
        self.row = self.of(sp)
        self.column = jnp.broadcast_to(self.row, (128, self.tok)).T[:, 0:1]

    def of(self, sp):
        return self.ref[pl.ds(sp, 1), :].astype(F32)

    def last(self, sp):
        value = self.of(jnp.maximum(sp, 0))[:, self.tok - 1 : self.tok]
        return jnp.where(sp >= 0, value, -1.0)

    def first(self, sp):
        value = self.of(jnp.minimum(sp, self.n_sp - 1))[:, 0:1]
        return jnp.where(sp < self.n_sp, value, -2.0)

    def through(self, here, there):
        return jnp.broadcast_to(jnp.where(here == there, 1.0, 0.0), (1, PAD_F))


def rows_sum(values):
    total = values[0]
    for value in values[1:]:
        total = total + value
    return total


CHAIN_STEPS = 3
CHAIN_BACK_STEPS = 5
CHUNK = 256
UNITS = 4
EARLY = 2


def units_of(width):
    chunks = -(-width // CHUNK)
    step = -(-chunks // UNITS)
    return [(first, min(chunks, first + step)) for first in range(0, chunks, step)]


def forward_kernel(
    n_sp, x_ref, gain_parts_ref, doc_ref, table_ref, wo_ref, wg_ref, wu_ref, wd_ref, wq_ref, wk_ref, wv_ref, *rest,
):
    n_unit = len(units_of(wd_ref.shape[0]))
    (att_ref, inv_ref, q_ref, k_ref, v_ref, normed_ref, state_ref, gain_ref), rest = rest[:8], rest[8:]
    fulls, rest = rest[: 2 + EARLY], rest[2 + EARLY :]
    kept, rest = rest[: n_unit - EARLY], rest[n_unit - EARLY :]
    (joint_own, out_own), rest = rest[:2], rest[2:]
    ffn_own, rest = rest[:n_unit], rest[n_unit:]
    (
        mask_ref, joint_vm, num_ref, den_ref, own_state, mate_state, in_state, out_state, gains_ref, gains_in,
        prior_ref, send_sem, recv_sem, local_sem,
    ) = rest
    tok = x_ref.shape[0]
    n_z = n_sp // 2
    lanes = q_ref.shape[1]
    pairs = v_ref.shape[1] // 128
    where = place(n_sp)
    dp, sp, g, gy, gx, z, c, across_x, across_y, diagonal, partner = where
    copies = Copies(send_sem, recv_sem)
    joint_full = fulls[0]
    owns = (joint_own, out_own) + tuple(ffn_own[:EARLY])
    gathers = [Gather(copies, k, n_z, own, full, where) for k, (own, full) in enumerate(zip(owns, fulls))]
    others = [(dp, lax.rem(sp + i, n_sp)) for i in range(1, n_sp)]
    for i, device in enumerate(others, 1):
        copies.add(("gain", i), gains_ref, gains_in.at[i - 1], device)
    docs = Documents(doc_ref, sp)
    even = sp - c
    chain = Chain(
        copies, where, n_z, True, own_state, mate_state, in_state, out_state,
        docs.through(docs.last(even + 1), docs.last(even)), docs.through(docs.last(even), docs.last(even - 1)),
    )
    part_lane = lax.broadcasted_iota(jnp.int32, gains_ref.shape, 1)
    gains_ref[...] = jnp.where(part_lane // (gains_ref.shape[1] // n_sp) == sp, gain_parts_ref[...], 0.0)
    assembled = [
        pltpu.make_async_copy(wq_ref, joint_own.at[:, 0:lanes], local_sem.at[0]),
        pltpu.make_async_copy(wk_ref, joint_own.at[:, lanes : 2 * lanes], local_sem.at[1]),
        pltpu.make_async_copy(wv_ref, joint_own.at[:, 2 * lanes :], local_sem.at[2]),
    ]
    for copy in assembled:
        copy.start()
    meet(others + [across_x, across_y])
    copies.start(*[("gain", i) for i in range(1, n_sp)])
    for copy in assembled:
        copy.wait()
    gathers[0].stage(0)
    out_own[...] = wo_ref[...].T
    width = wd_ref.shape[0]
    for own, (first, last) in zip(ffn_own, units_of(width)):
        lo, hi = first * CHUNK, min(last * CHUNK, width)
        span = (last - first) * CHUNK
        for i, piece in enumerate((wg_ref[lo:hi, :].T, wu_ref[lo:hi, :].T, wd_ref[lo:hi, :].T)):
            if hi - lo < span:
                own[:, (i + 1) * span - CHUNK : (i + 1) * span] = jnp.zeros((own.shape[0], CHUNK), BF16)
            own[:, i * span : i * span + hi - lo] = piece

    table = table_ref[...]
    row = lax.broadcasted_iota(jnp.int32, (tok, tok), 0)
    col = lax.broadcasted_iota(jnp.int32, (tok, tok), 1)
    mask_ref[...] = jnp.where((row >= col) & (docs.column == docs.row), 1.0, 0.0)
    prior_ref[...] = jnp.broadcast_to(jnp.where(docs.column == docs.last(sp - 1), 1.0, 0.0), prior_ref.shape)
    copies.arrived(*[("gain", i) for i in range(1, n_sp)])
    gain_ref[...] = gains_ref[...] + rows_sum([gains_in[i] for i in range(n_sp - 1)])
    x = x_ref[...].astype(F32)
    scale = lax.rsqrt(jnp.mean(x * x, axis=1, keepdims=True) + EPSILON)
    normed_ref[...] = (x * scale * gain_ref[0:1]).astype(BF16)
    local = [
        pltpu.make_async_copy(own, gather.own_place, local_sem.at[k])
        for k, (own, gather) in enumerate(zip(owns, gathers))
    ] + [
        pltpu.make_async_copy(own, keep, local_sem.at[len(owns) + k])
        for k, (own, keep) in enumerate(zip(ffn_own[EARLY:], kept))
    ]
    for copy in local:
        copy.start()
    gathers[0].stage(1)
    gathers[1].stage(0)
    gathers[2].stage(0)
    gathers[0].stage(2)
    gathers[0].stage(3)
    gathers[0].stage(4)
    for copy in local:
        copy.wait()
    fetch = pltpu.make_async_copy(joint_full, joint_vm, local_sem.at[0])
    fetch.start()
    fetch.wait()
    wide = joint_vm.shape[1]
    for first in range(0, wide, BLK):
        part = mm(normed_ref[...], joint_vm[:, first : first + BLK]).astype(BF16)
        if first < lanes:
            q_ref[:, first : first + BLK] = part
        elif first < 2 * lanes:
            k_ref[:, first - lanes : first - lanes + BLK] = part
        else:
            v_ref[:, first - 2 * lanes : first - 2 * lanes + BLK] = part

    tail = jnp.where(docs.row == docs.last(sp), 1.0, 0.0)

    def at(p, step, *todo):
        @pl.when(p == step)
        def _():
            for k, n in todo:
                gathers[k].stage(n)

    def state_pair(p, carry):
        at(p, 0, (1, 1))
        at(p, 2, (2, 1), (3, 0))
        at(p, 5, (1, 2))
        columns = pl.ds(pl.multiple_of(p * 128, 128), 128)
        v_t = v_ref[:, columns].astype(F32).T * tail
        ones = jnp.broadcast_to(tail, (16, tail.shape[1]))
        for side in range(2):
            head = p * 2 + side
            sel = selectors(table, head, lanes)
            one, two = factors(k_ref[...], sel, table)
            phi = (one * two).astype(BF16)
            lhs = jnp.concatenate([v_t[side * 64 : side * 64 + 64], ones], axis=0)
            own_state[head] = mm(lhs.astype(BF16), phi).astype(BF16)
        return carry

    lax.fori_loop(0, pairs, state_pair, 0)

    chain.begin()
    turn = jnp.minimum(z * CHAIN_STEPS, pairs - 1)

    lane = lax.broadcasted_iota(jnp.int32, (BLK, 128), 1)

    def intra_pair(p, carry):
        at(p, 1, (1, 3), (2, 2))
        at(p, 3, (3, 1))
        at(p, 4, (2, 3))
        at(p, 7, (3, 2))
        chain.middle(p == turn)
        columns = pl.ds(pl.multiple_of(p * 128, 128), 128)
        v_hat = with_ones(v_ref[:, columns])
        heads = [head_lanes(q_ref[...], p * 2 + side) for side in range(2)]
        for i in range(tok // BLK):
            rows = slice(i * BLK, (i + 1) * BLK)
            keys = slice(0, (i + 1) * BLK)
            totals = []
            for side in range(2):
                t = mm(heads[side][rows], k_ref[keys, :], NT) + 4.0
                w = ((t * t + 16.0) * mask_ref[rows, keys]).astype(BF16)
                totals.append(mm(w, v_hat[keys]))
            num_ref[rows, columns] = jnp.where(lane < 64, totals[0][:, :128], totals[1][:, :128])
            den_ref[rows, columns] = jnp.where(lane < 64, totals[0][:, 128:], totals[1][:, 128:])
        return carry

    lax.fori_loop(0, pairs, intra_pair, 0)
    chain.finish(state_ref, table[4:5])
    prior = prior_ref[:, 0:1]
    wide_lane = lax.broadcasted_iota(jnp.int32, (tok, 128), 1)

    def inter_pair(p, carry):
        at(p, 4, (3, 3))
        columns = pl.ds(pl.multiple_of(p * 128, 128), 128)
        totals = []
        for side in range(2):
            head = p * 2 + side
            sel = selectors(table, head, lanes)
            state = state_ref[head]
            z_rows = jnp.broadcast_to(state[64:65].astype(F32), (128, PAD_F)).astype(BF16)
            one, two = factors(q_ref[...], sel, table)
            totals.append(mm((one * two).astype(BF16), placed(state, side, z_rows), NT) * prior)
        num = num_ref[:, columns] + jnp.where(wide_lane < 64, totals[0][:, :128], totals[1][:, :128])
        den = den_ref[:, columns] + jnp.where(wide_lane < 64, totals[0][:, 128:], totals[1][:, 128:])
        inv = 1.0 / den
        inv_ref[:, columns] = inv
        att_ref[:, columns] = (num * inv).astype(BF16)
        return carry

    lax.fori_loop(0, pairs, inter_pair, 0)
    for gather in gathers[1:]:
        gather.stage(4)
    copies.sent(*[("gain", i) for i in range(1, n_sp)])
    chain.drain()


def forward(n_sp, x, gains, docs, table, wo, wg, wu, wd, wq, wk, wv):
    tok, dim = x.shape
    lanes, values = wq.shape[1], wv.shape[1]
    heads = lanes // FEAT
    shard = wq.shape[0]
    vmem, anywhere = pl.BlockSpec(memory_space=pltpu.VMEM), pl.BlockSpec(memory_space=pl.ANY)
    n_z = n_sp // 2
    spans = [3 * CHUNK * (last - first) for first, last in units_of(wd.shape[0])]
    gathered = [2 * lanes + values, dim] + spans[:EARLY]
    sems = len(gathered) * n_copies(n_z) + n_sp + 2
    shape = jax.ShapeDtypeStruct
    result = pl.pallas_call(
        functools.partial(forward_kernel, n_sp),
        out_shape=(
            shape((tok, values), BF16), shape((tok, values), F32), shape((tok, lanes), BF16),
            shape((tok, lanes), BF16), shape((tok, values), BF16), shape((tok, dim), BF16),
            shape((heads, ROWS_S, PAD_F), BF16), shape((8, dim), F32),
        )
        + tuple(shape((shard * n_sp, w), BF16) for w in gathered)
        + tuple(shape((shard, w), BF16) for w in spans[EARLY:]),
        in_specs=[vmem] * 8 + [anywhere] * 3,
        out_specs=(vmem,) * 8 + (anywhere,) * (len(gathered) + len(spans) - EARLY),
        scratch_shapes=[pltpu.VMEM((shard, w), BF16) for w in [2 * lanes + values, dim] + spans]
        + [
            pltpu.VMEM((tok, tok), F32),
            pltpu.VMEM((dim, 2 * lanes + values), BF16),
            pltpu.VMEM((tok, values), F32),
            pltpu.VMEM((tok, values), F32),
            pltpu.VMEM((heads, ROWS_S, PAD_F), BF16),
            pltpu.VMEM((heads, ROWS_S, PAD_F), BF16),
            pltpu.VMEM((heads, ROWS_S, PAD_F), BF16),
            pltpu.VMEM((heads, ROWS_S, PAD_F), BF16),
            pltpu.VMEM((8, dim), F32),
            pltpu.VMEM((n_sp - 1, 8, dim), F32),
            pltpu.VMEM((tok, 128), F32),
            pltpu.SemaphoreType.DMA((sems,)),
            pltpu.SemaphoreType.DMA((sems,)),
            pltpu.SemaphoreType.DMA((8,)),
        ],
        compiler_params=pltpu.CompilerParams(
            collective_id=0, has_side_effects=True, vmem_limit_bytes=60 << 20
        ),
        name="forward",
    )(x, gains, docs, table, wo, wg, wu, wd, wq, wk, wv)
    n = 8 + len(gathered)
    return result[:8], result[8:10], result[10:n], result[n:]


def backward_kernel(
    n_sp, widths, q_ref, k_ref, v_ref, g_ref, att_ref, inv_ref, prior_state_ref, doc_ref, table_ref, *rest,
):
    n_red = len(widths)
    sources, rest = rest[:n_red], rest[n_red:]
    (gq_ref, gk_ref, gv_ref), rest = rest[:3], rest[3:]
    finals, rest = rest[:n_red], rest[n_red:]
    swaps, rest = rest[:n_red], rest[n_red:]
    buffers, rest = [rest[4 * i : 4 * i + 4] for i in range(n_red)], rest[4 * n_red :]
    (
        stage_buf, mask_ref, ghat_ref, gq_acc, gk_acc, own_state, mate_state, in_state, out_state, prior_ref, later_ref,
        send_sem, recv_sem, local_sem,
    ) = rest
    tok, lanes = q_ref.shape
    n_z = n_sp // 2
    pairs = v_ref.shape[1] // 128
    where = place(n_sp)
    dp, sp, g, gy, gx, z, c, across_x, across_y, diagonal, partner = where
    copies = Copies(send_sem, recv_sem)
    reduces = [
        Reduce(
            copies, k, n_z, where, sources[k], swaps[k], buffers[k], finals[k],
            stage_buf.at[:, :, :, :, :, 0 : widths[k]], local_sem,
        )
        for k in range(n_red)
    ]
    docs = Documents(doc_ref, sp)
    even = sp - c
    chain = Chain(
        copies, where, n_z, False, own_state, mate_state, in_state, out_state,
        docs.through(docs.first(even), docs.first(even + 1)), docs.through(docs.first(even + 1), docs.first(even + 2)),
    )
    along = [(dp, lax.rem(z + i, n_z) * 2 + c) for i in range(1, n_z)]
    meet([partner, across_x, across_y, diagonal] + along)
    for reduce in reduces:
        reduce.stage(0)

    def at(p, step, *todo):
        @pl.when(p == step)
        def _():
            for k, n in todo:
                reduces[k].stage(n)

    table = table_ref[...]
    row = lax.broadcasted_iota(jnp.int32, (tok, tok), 0)
    col = lax.broadcasted_iota(jnp.int32, (tok, tok), 1)
    mask_ref[...] = jnp.where((row <= col) & (docs.column == docs.row), 1.0, 0.0)
    prior_ref[...] = jnp.broadcast_to(jnp.where(docs.column == docs.last(sp - 1), 1.0, 0.0), prior_ref.shape)
    later_ref[...] = jnp.broadcast_to(jnp.where(docs.column == docs.first(sp + 1), 1.0, 0.0), later_ref.shape)
    gq_acc[...] = jnp.zeros_like(gq_acc)
    gk_acc[...] = jnp.zeros_like(gk_acc)
    r = lax.broadcasted_iota(jnp.int32, (128, 128), 0)
    c128 = lax.broadcasted_iota(jnp.int32, (128, 128), 1)
    same = jnp.where(r // 64 == c128 // 64, 1.0, 0.0).astype(BF16)
    lane64 = lax.broadcasted_iota(jnp.int32, (tok, 128), 1) % 64
    head_row = jnp.where(docs.row == docs.first(sp), 1.0, 0.0)

    def ghat_pair(p, carry):
        for when, todo in GHAT_SCHEDULE:
            at(p, when, *todo)
        columns = pl.ds(pl.multiple_of(p * 128, 128), 128)
        scaled = g_ref[:, columns].astype(F32) * inv_ref[:, columns]
        product = scaled * att_ref[:, columns].astype(F32)
        high = product.astype(BF16)
        low = (product - high.astype(F32)).astype(BF16)
        dots = -(mm(high, same) + mm(low, same))
        dots_high = dots.astype(BF16)
        dots_low = (dots - dots_high.astype(F32)).astype(BF16)
        extra = jnp.where(lane64 == 0, dots_high, jnp.where(lane64 == 1, dots_low, jnp.zeros_like(dots_low)))
        ghat = jnp.concatenate([scaled.astype(BF16), extra], axis=1)
        ghat_ref[p] = ghat
        ghat_t = ghat.astype(F32).T * head_row
        for side in range(2):
            head = p * 2 + side
            sel = selectors(table, head, lanes)
            one, two = factors(q_ref[...], sel, table)
            phi = (one * two).astype(BF16)
            lhs = jnp.concatenate(
                [ghat_t[side * 64 : side * 64 + 64], ghat_t[128 + side * 64 : 128 + side * 64 + 16]], axis=0
            )
            state = mm(lhs.astype(BF16), phi)
            z_row = jnp.sum(state[64:80], axis=0, keepdims=True)
            own_state[head] = jnp.concatenate(
                [state[0:64], jnp.broadcast_to(z_row, (16, PAD_F))], axis=0
            ).astype(BF16)
        return carry

    lax.fori_loop(0, pairs, ghat_pair, 0)

    chain.begin()
    turn = jnp.minimum((n_z - 1 - z) * CHAIN_BACK_STEPS, 2 * pairs - 1)

    lane = lax.broadcasted_iota(jnp.int32, (tok, 256), 1)
    first_row = lax.broadcasted_iota(jnp.int32, (128, PAD_F), 0)

    def main_pair(p, carry):
        columns = pl.ds(pl.multiple_of(p * 128, 128), 128)
        v_hat = with_ones(v_ref[:, columns])
        gv = [jnp.zeros((BLK, 128), F32) for _ in range(tok // BLK)]
        for side in range(2):
            step = p * 2 + side
            for when, todo in SCHEDULE:
                if when % 2 == side:
                    at(step, when, *todo)
            chain.middle(step == turn)
            head = p * 2 + side
            sel = selectors(table, head, lanes)
            ghat = jnp.where((lane % 128) // 64 == side, ghat_ref[p], jnp.zeros((tok, 256), BF16))
            q_head = head_lanes(q_ref[...], head)
            q_twice = q_head + q_head
            k_twice = head_lanes(k_ref[...], head, 2)
            prior = prior_state_ref[head]
            z_two = jnp.where(first_row // 2 == side * 32, prior[64:65], jnp.zeros((128, PAD_F), BF16))
            rows_p = placed(prior, side, z_two)
            q_one, q_two = factors(q_ref[...], sel, table)
            d_phi = mm(ghat, rows_p) * prior_ref[:, 0:1]
            gq_acc[...] += mm((d_phi * q_two).astype(BF16), sel[0], NT) + mm(
                (d_phi * q_one).astype(BF16), sel[1], NT
            )
            for j in range(tok // BLK):
                rows = slice(j * BLK, (j + 1) * BLK)
                onward = slice(j * BLK, tok)
                t = mm(k_ref[rows, :], q_head[onward], NT) + 4.0
                g_w = mm(v_hat[rows], ghat[onward], NT)
                mask = mask_ref[rows, onward]
                masked_t = t * mask
                w = (masked_t * t + 16.0 * mask).astype(BF16)
                g_s = (g_w * masked_t).astype(BF16)
                gv[j] = gv[j] + mm(w, ghat[onward, 0:128])
                gk_acc[rows, :] += mm(g_s, q_twice[onward])
                gq_acc[onward, :] += mm(g_s, k_twice[rows], TN)
        for j in range(tok // BLK):
            rows = slice(j * BLK, (j + 1) * BLK)
            gv_ref[rows, columns] = gv[j].astype(BF16)
        return carry

    lax.fori_loop(0, pairs, main_pair, 0)
    chain.drain()
    chain.finish(out_state, table[4:5])

    def later_pair(p, carry):
        for when, todo in LATE_SCHEDULE:
            at(p, when, *todo)
        columns = pl.ds(pl.multiple_of(p * 128, 128), 128)
        v_hat = with_ones(v_ref[:, columns])
        gv_inter = None
        for side in range(2):
            head = p * 2 + side
            sel = selectors(table, head, lanes)
            later = out_state[head]
            z_one = jnp.where(first_row == 0, later[64:65], jnp.zeros((128, PAD_F), BF16))
            rows_n = placed(later, side, z_one)
            k_one, k_two = factors(k_ref[...], sel, table)
            phi_k = (k_one * k_two).astype(BF16)
            gvi = mm(phi_k, rows_n[0:128], NT)
            gv_inter = gvi if gv_inter is None else gv_inter + gvi
            d_phi = mm(v_hat, rows_n) * later_ref[:, 0:1]
            gk_acc[...] += mm((d_phi * k_two).astype(BF16), sel[0], NT) + mm(
                (d_phi * k_one).astype(BF16), sel[1], NT
            )
        gv_ref[:, columns] = (gv_ref[:, columns].astype(F32) + gv_inter * later_ref[...]).astype(BF16)
        return carry

    lax.fori_loop(0, pairs, later_pair, 0)
    gq_ref[...] = gq_acc[...].astype(BF16)
    gk_ref[...] = gk_acc[...].astype(BF16)
    for k, n in LAST_SCHEDULE:
        reduces[k].stage(n)


GHAT_SCHEDULE = ((1, ((0, 1),)), (3, ((1, 1),)), (4, ((0, 2),)), (6, ((2, 1),)), (7, ((1, 2),)), )
SCHEDULE = ((1, ((0, 3),)), (2, ((3, 1),)), (4, ((2, 2),)), (6, ((1, 3),)), (7, ((0, 4),)), (9, ((3, 2),)), (10, ((2, 3),)), (12, ((1, 4),)), (14, ((0, 5),)), (15, ((3, 3),)), )
LATE_SCHEDULE = ((1, ((2, 4),)), (2, ((1, 5),)), (4, ((3, 4),)), (5, ((2, 5),)), (7, ((3, 5),)), )
LAST_SCHEDULE = ()


def shards_of(parts):
    return [part.reshape(-1, part.shape[-1]) for part in parts]


def backward(n_sp, arrays, grads):
    q, v = arrays[0], arrays[2]
    tok, lanes = q.shape
    heads = lanes // FEAT
    n_z = n_sp // 2
    rows = grads[0].shape[4]
    widths = tuple(grad.shape[5] for grad in grads)
    n_red = len(grads)
    vmem, anywhere = pl.BlockSpec(memory_space=pltpu.VMEM), pl.BlockSpec(memory_space=pl.ANY)
    shape = jax.ShapeDtypeStruct
    sems = n_red * n_reduce(n_z) + 3
    result = pl.pallas_call(
        functools.partial(backward_kernel, n_sp, widths),
        out_shape=(shape(q.shape, BF16), shape(q.shape, BF16), shape(v.shape, BF16))
        + tuple(shape((2, 2, rows, w), BF16) for w in widths)
        + tuple(shape((n_z, 2, 2, rows, w), BF16) for w in widths),
        in_specs=[vmem] * len(arrays) + [anywhere] * n_red,
        out_specs=(vmem,) * (3 + n_red) + (anywhere,) * n_red,
        scratch_shapes=sum([reduce_scratch(n_z, rows, w) for w in widths], [])
        + [
            pltpu.VMEM((2, 2, 2, 2, rows, max(widths)), BF16),
            pltpu.VMEM((tok, tok), F32),
            pltpu.VMEM((heads // 2, tok, 256), BF16),
            pltpu.VMEM(q.shape, F32),
            pltpu.VMEM(q.shape, F32),
            pltpu.VMEM((heads, ROWS_S, PAD_F), BF16),
            pltpu.VMEM((heads, ROWS_S, PAD_F), BF16),
            pltpu.VMEM((heads, ROWS_S, PAD_F), BF16),
            pltpu.VMEM((heads, ROWS_S, PAD_F), BF16),
            pltpu.VMEM((tok, 128), F32),
            pltpu.VMEM((tok, 128), F32),
            pltpu.SemaphoreType.DMA((sems,)),
            pltpu.SemaphoreType.DMA((sems,)),
            pltpu.SemaphoreType.DMA((2, 2)),
        ],
        compiler_params=pltpu.CompilerParams(
            collective_id=1, has_side_effects=True, vmem_limit_bytes=63 << 20
        ),
        name="backward",
    )(*arrays, *grads)
    return result[:3], shards_of(result[3 : 3 + n_red])


def reduce_units(chunks):
    edges = [0, 2, 4, 6, 8, chunks]
    return list(zip(edges[:-1], edges[1:]))


IN_FFN = 2
FFN_SCHEDULE = {
    1: (("g", 0, 1), ("g", 1, 0)),
    3: (("g", 0, 2), ("r", 0, 0)),
    4: (("g", 1, 1), ("g", 0, 3), ("r", 0, 1)),
    5: (("g", 0, 4), ("r", 1, 0)),
    6: (("g", 1, 2), ("r", 0, 2), ("r", 1, 1)),
    7: (("g", 1, 3),),
    8: (("g", 1, 4), ("r", 0, 3), ("r", 1, 2)),
    9: (("r", 1, 3),),
    10: (("r", 0, 4),),
}
FFN_LATE = (("r", 1, 4),)
FFN_LAST = (("r", 0, 5), ("r", 1, 5))


def ffn_kernel(n_sp, gather_units, chunks, x_ref, att_ref, out_w_ref, gain_ref, cot_ref, *rest):
    n_unit = len(gather_units)
    sums = reduce_units(chunks)
    n_sum = len(sums)
    early, rest = rest[:EARLY], rest[EARLY:]
    kept, rest = rest[: n_unit - EARLY], rest[n_unit - EARLY :]
    ggain_ref, rest = rest[0], rest[1:]
    finals, rest = rest[:IN_FFN], rest[IN_FFN:]
    (output_ref, gh_ref, gatt_ref, gout_ref), rest = rest[:4], rest[4:]
    grads, rest = rest[:n_sum], rest[n_sum:]
    swaps, rest = rest[:IN_FFN], rest[IN_FFN:]
    late, rest = rest[: n_unit - EARLY], rest[n_unit - EARLY :]
    buffers, rest = [rest[4 * i : 4 * i + 4] for i in range(IN_FFN)], rest[4 * IN_FFN :]
    (
        stage_buf, hid, n2, n2_t, cot_t, acc_o, acc_n, gout, w_buf, g_buf, send_sem, recv_sem, local_sem, w_sem, g_sem,
        o_sem,
    ) = rest
    tok, dim = x_ref.shape
    n_z = n_sp // 2
    where = place(n_sp)
    dp, sp, g, gy, gx, z, c, across_x, across_y, diagonal, partner = where
    copies = Copies(send_sem, recv_sem)
    gathers = [Gather(copies, ("g", k), n_z, own, full, where) for k, (own, full) in enumerate(zip(kept, late))]
    reduces = [
        Reduce(
            copies, ("r", k), n_z, where, grads[k], swaps[k], buffers[k], finals[k],
            stage_buf.at[:, :, :, :, :, 0 : grads[k].shape[-1]], local_sem,
        )
        for k in range(IN_FFN)
    ]
    along = [(dp, lax.rem(z + i, n_z) * 2 + c) for i in range(1, n_z)]
    meet([partner, across_x, across_y, diagonal] + along)
    gathers[0].stage(0)
    own_copies = [
        pltpu.make_async_copy(own, gather.own_place, o_sem.at[k])
        for k, (own, gather) in enumerate(zip(kept, gathers))
    ]
    for copy in own_copies:
        copy.start()

    def run(todo):
        for kind, k, n in todo:
            (gathers if kind == "g" else reduces)[k].stage(n)

    fulls = list(early) + list(late)

    def load(chunk, slot, do_wait=False):
        if do_wait:
            for i in range(3):
                pltpu.make_async_copy(fulls[0].at[:, 0:CHUNK], w_buf.at[slot, i], w_sem.at[slot, i]).wait()
            return
        for full, (first, last) in zip(fulls, gather_units):
            @pl.when((chunk >= first) & (chunk < last))
            def _():
                for i in range(3):
                    lane = pl.multiple_of((chunk - first + i * (last - first)) * CHUNK, CHUNK)
                    pltpu.make_async_copy(full.at[:, pl.ds(lane, CHUNK)], w_buf.at[slot, i], w_sem.at[slot, i]).start()

    def save(chunk, slot, do_wait=False):
        if do_wait:
            for i in range(3):
                pltpu.make_async_copy(
                    g_buf.at[slot, i], grads[0].at[:, :, :, :, :, 0:CHUNK], g_sem.at[slot, i]
                ).wait()
            return
        for grad, (first, last) in zip(grads, sums):
            @pl.when((chunk >= first) & (chunk < last))
            def _():
                for i in range(3):
                    lane = pl.multiple_of((chunk - first + i * (last - first)) * CHUNK, CHUNK)
                    pltpu.make_async_copy(
                        g_buf.at[slot, i], grad.at[:, :, :, :, :, pl.ds(lane, CHUNK)], g_sem.at[slot, i]
                    ).start()

    load(0, 0)
    gain = gain_ref[1:2]
    for i in range(tok // BLK):
        rows = slice(i * BLK, (i + 1) * BLK)
        hidden = x_ref[rows, :].astype(F32) + mm(att_ref[rows, :], out_w_ref[...], NT)
        hid[rows, :] = hidden
        scale = lax.rsqrt(jnp.mean(hidden * hidden, axis=1, keepdims=True) + EPSILON)
        normed = (hidden * scale * gain).astype(BF16)
        n2[rows, :] = normed
        n2_t[:, rows] = normed.T
        cot_t[:, rows] = cot_ref[rows, :].T
    acc_o[...] = jnp.zeros_like(acc_o)
    acc_n[...] = jnp.zeros_like(acc_n)
    for copy in own_copies:
        copy.wait()
    grad_shape = g_buf.shape[2:]

    def step(chunk, carry):
        slot = lax.rem(chunk, 2)
        load(chunk, slot, True)

        @pl.when(chunk >= 2)
        def _():
            save(chunk, slot, True)

        for when, todo in FFN_SCHEDULE.items():
            @pl.when(chunk == when)
            def _():
                run(todo)

        @pl.when(chunk + 1 < chunks)
        def _():
            load(chunk + 1, 1 - slot)

        wg, wu, wd = w_buf[slot, 0], w_buf[slot, 1], w_buf[slot, 2]
        gate = mm(n2[...], wg)
        up = mm(n2[...], wu)
        g_mixed = mm(cot_ref[...], wd)
        sig = 1.0 / (1.0 + jnp.exp(-gate))
        act = gate * sig
        mixed = (act * up).astype(BF16)
        g_gate = (g_mixed * up * sig * (1.0 + gate * (1.0 - sig))).astype(BF16)
        g_up = (g_mixed * act).astype(BF16)
        g_buf[slot, 0] = mm(n2_t[...], g_gate).astype(BF16).reshape(grad_shape)
        g_buf[slot, 1] = mm(n2_t[...], g_up).astype(BF16).reshape(grad_shape)
        g_buf[slot, 2] = mm(cot_t[...], mixed).astype(BF16).reshape(grad_shape)
        save(chunk, slot)
        acc_o[...] += mm(mixed, wd, NT)
        acc_n[...] += mm(g_gate, wg, NT) + mm(g_up, wu, NT)
        return carry

    lax.fori_loop(0, chunks, step, 0)
    run(FFN_LATE)
    total = jnp.zeros((1, dim), F32)
    for i in range(tok // BLK):
        rows = slice(i * BLK, (i + 1) * BLK)
        hidden = hid[rows, :]
        n2[rows, :] = (hidden + acc_o[rows, :]).astype(BF16)
        scale = lax.rsqrt(jnp.mean(hidden * hidden, axis=1, keepdims=True) + EPSILON)
        e = acc_n[rows, :]
        total = total + jnp.sum(e * hidden * scale, axis=0, keepdims=True)
        eg = e * gain
        inner = jnp.mean(eg * hidden, axis=1, keepdims=True)
        gh = cot_ref[rows, :].astype(F32) + scale * eg - hidden * (scale * scale * scale * inner)
        acc_o[rows, :] = gh
        n2_t[rows, :] = gh.astype(BF16)
        cot_t[rows, :] = mm(n2_t[rows, :], out_w_ref[...]).astype(BF16)
    ggain_ref[...] = jnp.broadcast_to(total, ggain_ref.shape)
    outs = [
        pltpu.make_async_copy(n2, output_ref, o_sem.at[0]),
        pltpu.make_async_copy(acc_o, gh_ref, o_sem.at[1]),
        pltpu.make_async_copy(cot_t, gatt_ref, o_sem.at[2]),
    ]
    for copy in outs:
        copy.start()
    for first in range(0, att_ref.shape[1], CHUNK):
        columns = slice(first, first + CHUNK)
        gout[:, :, :, :, :, columns] = (
            mm(n2_t[...], att_ref[:, columns], TN).astype(BF16).reshape(grad_shape)
        )
    outs.append(pltpu.make_async_copy(gout, gout_ref, o_sem.at[3]))
    outs[3].start()
    save(chunks - 2, (chunks - 2) % 2, True)
    save(chunks - 1, (chunks - 1) % 2, True)
    run(FFN_LAST)
    for copy in outs:
        copy.wait()


def ffn(n_sp, x, att, out_w, gain, cot, width, early, kept):
    tok, dim = x.shape
    values = att.shape[1]
    n_z = n_sp // 2
    chunks = -(-width // CHUNK)
    gather_units = units_of(width)
    sums = reduce_units(chunks)
    rows = dim // n_sp // GROUP
    spans = [3 * CHUNK * (last - first) for first, last in sums]
    vmem, anywhere = pl.BlockSpec(memory_space=pltpu.VMEM), pl.BlockSpec(memory_space=pl.ANY)
    shape = jax.ShapeDtypeStruct
    split = lambda w: shape((n_z, 2, 2, 2, rows, w), BF16)
    sems = len(kept) * n_copies(n_z) + IN_FFN * n_reduce(n_z)
    full_shapes = tuple(shape((k.shape[0] * n_sp, k.shape[1]), BF16) for k in kept)
    result = pl.pallas_call(
        functools.partial(ffn_kernel, n_sp, gather_units, chunks),
        out_shape=(shape((8, dim), F32),)
        + tuple(shape((2, 2, rows, w), BF16) for w in spans[:IN_FFN])
        + (shape((tok, dim), BF16), shape((tok, dim), F32), shape((tok, values), BF16), split(values))
        + tuple(split(w) for w in spans)
        + tuple(shape((n_z, 2, 2, rows, w), BF16) for w in spans[:IN_FFN])
        + full_shapes,
        in_specs=[vmem] * 5 + [anywhere] * len(early) + [vmem] * len(kept),
        out_specs=(vmem,) * (1 + IN_FFN) + (anywhere,) * (4 + len(spans) + IN_FFN + len(kept)),
        scratch_shapes=sum([reduce_scratch(n_z, rows, w) for w in spans[:IN_FFN]], [])
        + [
            pltpu.VMEM((2, 2, 2, 2, rows, max(spans[:IN_FFN])), BF16),
            pltpu.VMEM((tok, dim), F32),
            pltpu.VMEM((tok, dim), BF16),
            pltpu.VMEM((dim, tok), BF16),
            pltpu.VMEM((dim, tok), BF16),
            pltpu.VMEM((tok, dim), F32),
            pltpu.VMEM((tok, dim), F32),
            pltpu.VMEM((n_z, 2, 2, 2, rows, values), BF16),
            pltpu.VMEM((2, 3, dim, CHUNK), BF16),
            pltpu.VMEM((2, 3, n_z, 2, 2, 2, rows, CHUNK), BF16),
            pltpu.SemaphoreType.DMA((sems,)),
            pltpu.SemaphoreType.DMA((sems,)),
            pltpu.SemaphoreType.DMA((2, 2)),
            pltpu.SemaphoreType.DMA((2, 3)),
            pltpu.SemaphoreType.DMA((2, 3)),
            pltpu.SemaphoreType.DMA((4,)),
        ],
        compiler_params=pltpu.CompilerParams(
            collective_id=2, has_side_effects=True, vmem_limit_bytes=63 << 20
        ),
        name="ffn",
    )(x, att, out_w, gain, cot, *early, *kept)
    n = 1 + IN_FFN
    shards = shards_of(result[1:n])
    output, g_hidden, g_att, g_out = result[n : n + 4]
    grads = result[n + 4 + IN_FFN : n + 4 + len(spans)]
    return output, g_hidden, g_att, result[0], g_out, shards, grads


def tail_kernel(
    n_sp, normed_ref, gq_ref, gk_ref, gv_ref, w_ref, x_ref, gh_ref, gain_ref, ggain_ref,
    gin_ref, gains_ref, final_v, final_qk,
    src_v, src_qk, swap_v, swap_qk, *rest,
):
    buffers, rest = (rest[:4], rest[4:8]), rest[8:]
    own_gains, sum_gains, in_sp, in_dp, send_sem, recv_sem = rest
    tok, dim = x_ref.shape
    n_z = n_sp // 2
    lanes = gq_ref.shape[1]
    where = place(n_sp)
    dp, sp, g, gy, gx, z, c, across_x, across_y, diagonal, partner = where
    copies = Copies(send_sem, recv_sem)
    first = Reduce(copies, "v", n_z, where, src_v, swap_v, buffers[0], final_v)
    second = Reduce(copies, "qk", n_z, where, src_qk, swap_qk, buffers[1], final_qk)
    others = [(dp, lax.rem(sp + i, n_sp)) for i in range(1, n_sp)]
    groups = [across_x, across_y, diagonal]
    for i, device in enumerate(others):
        copies.add(("sp", i), own_gains, in_sp.at[i], device)
    for i, device in enumerate(groups):
        copies.add(("dp", i), sum_gains, in_dp.at[i], device)
    meet(others + groups)
    block = src_v.shape[:-1] + (BLK,)
    for i in range(0, gv_ref.shape[1], BLK):
        columns = slice(i, i + BLK)
        src_v[:, :, :, :, :, columns] = mm(normed_ref[...], gv_ref[:, columns], TN).astype(BF16).reshape(block)
    for i, ref in enumerate((gq_ref, gk_ref)):
        for j in range(0, lanes, BLK):
            src_qk[:, :, :, :, :, i * lanes + j : i * lanes + j + BLK] = (
                mm(normed_ref[...], ref[:, j : j + BLK], TN).astype(BF16).reshape(block)
            )
        if i == 0:
            first.stage(0)
    todo = [[(second, 0), (first, 1)], [(second, 1)], [(first, 2)], [(second, 2)]]
    total = jnp.zeros((1, dim), F32)
    gain = gain_ref[0:1]
    for i in range(tok // BLK):
        rows = slice(i * BLK, (i + 1) * BLK)
        e = (
            mm(gq_ref[rows, :], w_ref[:, 0:lanes], NT)
            + mm(gk_ref[rows, :], w_ref[:, lanes : 2 * lanes], NT)
            + mm(gv_ref[rows, :], w_ref[:, 2 * lanes :], NT)
        )
        u = x_ref[rows, :].astype(F32)
        scale = lax.rsqrt(jnp.mean(u * u, axis=1, keepdims=True) + EPSILON)
        total = total + jnp.sum(e * u * scale, axis=0, keepdims=True)
        eg = e * gain
        inner = jnp.mean(eg * u, axis=1, keepdims=True)
        gin_ref[rows, :] = gh_ref[rows, :] + scale * eg - u * (scale * scale * scale * inner)
        for reduce, n in todo[i] if i < len(todo) else ():
            reduce.stage(n)
    for i in range(tok // BLK, len(todo)):
        for reduce, n in todo[i]:
            reduce.stage(n)
    row = lax.broadcasted_iota(jnp.int32, own_gains.shape, 0)
    own_gains[...] = jnp.where(row == 0, jnp.broadcast_to(total, own_gains.shape), ggain_ref[...])
    first.stage(3)
    copies.start(*[("sp", i) for i in range(n_sp - 1)])
    second.stage(3)
    copies.arrived(*[("sp", i) for i in range(n_sp - 1)])
    sum_gains[...] = own_gains[...] + rows_sum([in_sp[i] for i in range(n_sp - 1)])
    first.stage(4)
    copies.start(*[("dp", i) for i in range(3)])
    second.stage(4)
    copies.arrived(*[("dp", i) for i in range(3)])
    gains_ref[...] = sum_gains[...] + rows_sum([in_dp[i] for i in range(3)])
    first.stage(5)
    second.stage(5)
    copies.sent(*[("sp", i) for i in range(n_sp - 1)], *[("dp", i) for i in range(3)])


def tail(n_sp, normed, gq, gk, gv, w_joint, x, g_hidden, gain, ggain):
    tok, dim = x.shape
    lanes, values = gq.shape[1], gv.shape[1]
    n_z = n_sp // 2
    rows = dim // n_sp // GROUP
    vmem = pl.BlockSpec(memory_space=pltpu.VMEM)
    shape = jax.ShapeDtypeStruct
    widths = (values, 2 * lanes)
    sems = 2 * n_reduce(n_z) + n_sp + 2
    return pl.pallas_call(
        functools.partial(tail_kernel, n_sp),
        out_shape=(shape((tok, dim), F32), shape((8, dim), F32))
        + tuple(shape((2, 2, rows, w), BF16) for w in widths),
        in_specs=[vmem] * 9,
        out_specs=(vmem,) * 4,
        scratch_shapes=[pltpu.VMEM((n_z, 2, 2, 2, rows, w), BF16) for w in widths]
        + [pltpu.VMEM((n_z, 2, 2, rows, w), BF16) for w in widths]
        + sum([reduce_scratch(n_z, rows, w) for w in widths], [])
        + [
            pltpu.VMEM((8, dim), F32),
            pltpu.VMEM((8, dim), F32),
            pltpu.VMEM((n_sp - 1, 8, dim), F32),
            pltpu.VMEM((3, 8, dim), F32),
            pltpu.SemaphoreType.DMA((sems,)),
            pltpu.SemaphoreType.DMA((sems,)),
        ],
        compiler_params=pltpu.CompilerParams(
            collective_id=3, has_side_effects=True, vmem_limit_bytes=60 << 20
        ),
        name="tail",
    )(normed, gq, gk, gv, w_joint, x, g_hidden, gain, ggain)


def finish_kernel(sums, *refs):
    n = len(sums) + 3
    sources, refs = refs[:n], refs[n:]
    (q_out, k_out, v_out, out_out, gate_out, up_out, down_out), refs = refs[:7], refs[7:]
    held, sem = refs[:n], refs[n]
    copies = [pltpu.make_async_copy(src, dst, sem.at[i]) for i, (src, dst) in enumerate(zip(sources, held))]
    for copy in copies:
        copy.start()
    for copy in copies:
        copy.wait()
    qk_ref, v_ref, out_ref, units = held[0], held[1], held[2], held[3:]
    lanes = q_out.shape[1]
    width = gate_out.shape[0]
    q_out[...] = qk_ref[:, :lanes].astype(F32)
    k_out[...] = qk_ref[:, lanes:].astype(F32)
    v_out[...] = v_ref[...].astype(F32)
    out_out[...] = out_ref[...].astype(F32).T
    for unit, (first, last) in zip(units, sums):
        lo, hi = first * CHUNK, min(last * CHUNK, width)
        span = (last - first) * CHUNK
        for i, out in enumerate((gate_out, up_out, down_out)):
            out[lo:hi, :] = unit[:, i * span : i * span + hi - lo].astype(F32).T


def finish(width, lanes, qk, v, out, units):
    shard = v.shape[0]
    vmem, anywhere = pl.BlockSpec(memory_space=pltpu.VMEM), pl.BlockSpec(memory_space=pl.ANY)
    shape = jax.ShapeDtypeStruct
    arrays = (qk, v, out, *units)
    return pl.pallas_call(
        functools.partial(finish_kernel, reduce_units(-(-width // CHUNK))),
        out_shape=(
            shape((shard, lanes), F32), shape((shard, lanes), F32), shape(v.shape, F32),
            shape(out.shape[::-1], F32), shape((width, shard), F32), shape((width, shard), F32),
            shape((width, shard), F32),
        ),
        in_specs=[anywhere] * len(arrays),
        out_specs=(vmem,) * 7,
        scratch_shapes=[pltpu.VMEM(a.shape, BF16) for a in arrays] + [pltpu.SemaphoreType.DMA((len(arrays),))],
        compiler_params=pltpu.CompilerParams(vmem_limit_bytes=63 << 20),
        name="finish",
    )(*arrays)


def body(
    tokens, doc_ids, gain_attn, w_query, w_key, w_value, w_out, gain_mlp, w_gate, w_up, w_down, cotangent
):
    n_sp = lax.axis_size("sp")
    me = lax.axis_index("sp")
    tok = tokens.shape[0]
    heads = w_query.shape[1] // FEAT
    table = feature_table()
    docs = doc_ids.reshape(n_sp, tok)
    width = gain_attn.shape[0]
    lanes = heads * FEAT
    hidden_units = w_gate.shape[1]
    gain_parts = jnp.tile(jnp.stack([gain_attn, gain_mlp] + [gain_mlp] * 6).astype(F32), (1, n_sp))
    (
        (att, inv, q, k, v, normed_one, prior_state, gain), (w_joint, out_t), early, kept
    ) = forward(
        n_sp, tokens, gain_parts, docs, table, w_out, w_gate.T, w_up.T, w_down, w_query, w_key, w_value
    )
    output, g_hidden, g_att, grad_gain_two, g_out, shards, grads = ffn(
        n_sp, tokens, att, out_t, gain, cotangent, hidden_units, early, kept
    )
    (gq, gk, gv), (s_out, *more) = backward(
        n_sp, (q, k, v, g_att, att, inv, prior_state, docs, table), (g_out, *grads)
    )
    grad_input, grad_gains, *joint = tail(
        n_sp, normed_one, gq, gk, gv, w_joint, tokens, g_hidden, gain, grad_gain_two
    )
    n_dp = lax.axis_size("dp")

    def over_groups(shard):
        if n_dp > GROUP:
            shard = lax.psum(shard, "dp") * jnp.asarray(GROUP / n_dp, shard.dtype)
        return shard

    s_value, s_query_key = shards_of(joint)
    g_query, g_key, g_value, g_w_out, g_gate, g_up, g_down = finish(
        hidden_units, lanes, over_groups(s_query_key), over_groups(s_value), over_groups(s_out),
        [over_groups(shard) for shard in (*shards, *more)],
    )
    s_gains = over_groups(lax.dynamic_slice(grad_gains, (0, me * width), (2, width)))
    return (
        output, grad_input, s_gains[0], g_query, g_key, g_value, g_w_out, s_gains[1], g_gate.T, g_up.T, g_down
    )


def solution(mesh):
    placed_in = (
        P(("dp", "sp"), None), P("dp", None), P("sp"), P("sp", None), P("sp", None), P("sp", None),
        P(None, "sp"), P("sp"), P("sp", None), P("sp", None), P(None, "sp"), P(("dp", "sp"), None),
    )
    return jax.shard_map(
        body,
        mesh=mesh,
        in_specs=placed_in,
        out_specs=(
            P(("dp", "sp"), None), P(("dp", "sp"), None), P("sp"), P("sp", None), P("sp", None),
            P("sp", None), P(None, "sp"), P("sp"), P("sp", None), P("sp", None), P(None, "sp"),
        ),
        check_vma=False,
    )
```

```python
import functools
import math

import jax
import jax.numpy as jnp
import numpy as np
from jax import lax
from jax.experimental import pallas as pl
from jax.experimental.pallas import tpu as pltpu
from jax.sharding import PartitionSpec as P

FEAT = 16
HEAD_V = 64
EPSILON = 1e-05
BF16 = jnp.bfloat16
F32 = jnp.float32
BLK = 256
PAD_F = 256
ROWS_S = 80
NN = (((1,), (0,)), ((), ()))
NT = (((1,), (1,)), ((), ()))
TN = (((0,), (0,)), ((), ()))


def mm(a, b, dims=NN):
    return lax.dot_general(a, b, dims, preferred_element_type=F32)


def feature_table():
    rows = []
    for a in range(FEAT):
        for b in range(a, FEAT):
            rows.append((a, b, 0.0, 0.0, 1.0 if a == b else 2.0))
    for a in range(FEAT):
        rows.append((a, -1, 0.0, 1.0, 8.0))
    rows.append((-1, -1, 1.0, 1.0, 32.0))
    while len(rows) < PAD_F:
        rows.append((-1, -1, 0.0, 0.0, 0.0))
    table = np.zeros((8, PAD_F), np.float32)
    table[:5] = np.array(rows, np.float32).T
    return jnp.asarray(table)


def selectors(table, head, lanes):
    row = lax.broadcasted_iota(jnp.int32, (lanes, PAD_F), 0).astype(F32)
    base = (head * FEAT).astype(F32)
    first = jnp.where((row == table[0:1] + base) & (table[0:1] >= 0), 1.0, 0.0).astype(BF16)
    second = jnp.where((row == table[1:2] + base) & (table[1:2] >= 0), 1.0, 0.0).astype(BF16)
    return first, second


def head_lanes(values, head, scale=1):
    lane = lax.broadcasted_iota(jnp.int32, values.shape, 1)
    return jnp.where(lane // FEAT == head, values * scale, jnp.zeros_like(values))


def factors(values, sel, table):
    one = mm(values, sel[0]) + table[2:3]
    two = mm(values, sel[1]) + table[3:4]
    return one, two


def with_ones(v_pair):
    return jnp.concatenate([v_pair, jnp.ones_like(v_pair)], axis=1)


class Copies:
    def __init__(self, send_sem, recv_sem):
        self.send_sem, self.recv_sem, self.made = send_sem, recv_sem, {}

    def add(self, name, src, dst, device):
        self.made[name] = (src, dst, len(self.made), device)

    def get(self, name):
        src, dst, index, device = self.made[name]
        return pltpu.make_async_remote_copy(
            src_ref=src,
            dst_ref=dst,
            send_sem=self.send_sem.at[index],
            recv_sem=self.recv_sem.at[index],
            device_id=device,
            device_id_type=pl.DeviceIdType.MESH,
        )

    def start(self, *names):
        for name in names:
            self.get(name).start()

    def arrived(self, *names):
        for name in names:
            self.get(name).wait_recv()

    def sent(self, *names):
        for name in names:
            self.get(name).wait_send()


GROUP = 4


def place(n_sp):
    dp, sp = lax.axis_index("dp"), lax.axis_index("sp")
    g = lax.rem(dp, GROUP)
    gy, gx = g // 2, lax.rem(g, 2)
    z, c = sp // 2, lax.rem(sp, 2)
    across_x = (dp - g + gy * 2 + (1 - gx), sp)
    across_y = (dp - g + (1 - gy) * 2 + gx, sp)
    diagonal = (dp - g + (1 - gy) * 2 + (1 - gx), sp)
    partner = (dp, z * 2 + (1 - c))
    return dp, sp, g, gy, gx, z, c, across_x, across_y, diagonal, partner


class Gather:
    def __init__(self, copies, tag, n_z, own, full, where):
        dp, sp, g, gy, gx, z, c, across_x, across_y, _, partner = where
        self.copies, self.tag, self.n_z = copies, tag, n_z
        shard, width = own.shape
        quarter = shard // GROUP
        lower, upper = pl.ds(0, width // 2), pl.ds(width // 2, width // 2)

        def rows(zz, gg, count, lanes=None):
            start = pl.multiple_of((zz * 2 + c) * shard + gg * quarter, 16)
            return full.at[pl.ds(start, count)] if lanes is None else full.at[pl.ds(start, count), lanes]

        gx_of, gy_of = gy * 2 + (1 - gx), (1 - gy) * 2 + gx
        diag = (1 - gy) * 2 + (1 - gx)
        add = lambda name, src, dst, device: copies.add((tag, name), src, dst, device)
        mine = own.at[pl.ds(pl.multiple_of(g * quarter, 16), quarter)]
        self.own_place = rows(z, 0, shard)
        add("c0", own, self.own_place, partner)
        for i in range(1, n_z):
            zt = lax.rem(z + i, n_z)
            zs = lax.rem(z + n_z - i, n_z)
            add(f"z{i}", mine, rows(z, g, quarter), (dp, zt * 2 + c))
            here = rows(zs, g, quarter)
            add(f"x{i}", here, here, across_x)
            add(f"y{i}", here, here, across_y)
            add(f"c1{i}", here, here, partner)
            first = rows(zs, gx_of, quarter, lower)
            add(f"d0{i}", first, first, across_y)
            second = rows(zs, gy_of, quarter, upper)
            add(f"d1{i}", second, second, across_x)
            for name, gg in (("c2", gx_of), ("c3", gy_of), ("c4", diag)):
                there = rows(zs, gg, quarter)
                add(f"{name}{i}", there, there, partner)

    def each(self, *names):
        return [(self.tag, f"{name}{i}") for i in range(1, self.n_z) for name in names]

    def stage(self, n):
        copies = self.copies
        if n == 0:
            copies.start(*self.each("z"), (self.tag, "c0"))
        elif n == 1:
            for i in range(1, self.n_z):
                copies.arrived((self.tag, f"z{i}"))
                copies.start(*[(self.tag, f"{name}{i}") for name in ("x", "y", "c1")])
        elif n == 2:
            for i in range(1, self.n_z):
                copies.arrived((self.tag, f"x{i}"), (self.tag, f"y{i}"))
                copies.start(*[(self.tag, f"{name}{i}") for name in ("d0", "d1", "c2", "c3")])
        elif n == 3:
            for i in range(1, self.n_z):
                copies.arrived((self.tag, f"d0{i}"), (self.tag, f"d1{i}"))
                copies.start((self.tag, f"c4{i}"))
        else:
            copies.arrived((self.tag, "c0"), *self.each("c1", "c2", "c3", "c4"))
            copies.sent((self.tag, "c0"), *self.each("z", "x", "y", "c1", "d0", "d1", "c2", "c3", "c4"))


def n_copies(n_z):
    return 1 + 9 * (n_z - 1)


def meet(devices):
    barrier = pltpu.get_barrier_semaphore()
    for device in devices:
        pl.semaphore_signal(barrier, inc=1, device_id=device, device_id_type=pl.DeviceIdType.MESH)
    pl.semaphore_wait(barrier, len(devices))


def placed(state, side, z_rows):
    zero = jnp.zeros((64, PAD_F), state.dtype)
    values = [state[0:64], zero] if side == 0 else [zero, state[0:64]]
    return jnp.concatenate(values + [z_rows], axis=0)


class Reduce:
    def __init__(self, copies, tag, n_z, where, source, swapped, buffers, final, stage_buf=None, local_sem=None):
        dp, sp, g, gy, gx, z, c, across_x, across_y, diagonal, partner = where
        self.copies, self.tag, self.n_z = copies, tag, n_z
        self.gy, self.gx, self.z, self.c = gy, gx, z, c
        self.source, self.swapped, self.final = source, swapped, final
        self.work, self.first, self.second, self.along = buffers
        self.stage_buf, self.local_sem = stage_buf, local_sem
        work = self.work
        half = work.shape[-1] // 2
        self.halves = (pl.ds(0, half), pl.ds(half, half))
        lower, upper = self.halves
        everything = slice(None)
        add = lambda name, src, dst, device: copies.add((tag, name), src, dst, device)
        add("s", source.at[:, 1 - c], swapped, partner)
        add("a1", work.at[:, :, 1 - gx, everything, lower], self.first.at[0], across_x)
        add("b1", work.at[:, 1 - gy, :, everything, upper], self.first.at[1], across_y)
        add("a2", work.at[:, 1 - gy, gx, everything, lower], self.second.at[0], across_y)
        add("b2", work.at[:, gy, 1 - gx, everything, upper], self.second.at[1], across_x)
        for i in range(1, n_z):
            zt = lax.rem(z + i, n_z)
            add(f"z{i}", work.at[zt, gy, gx], self.along.at[i - 1], (dp, zt * 2 + c))
        for name, device in (("fx", across_x), ("fy", across_y), ("fd", diagonal)):
            add(name, final.at[gy, gx], final.at[gy, gx], device)

    def names(self, *names):
        return [(self.tag, name) for name in names]

    def load(self, zz):
        slot = zz % 2
        return (
            pltpu.make_async_copy(self.source.at[zz, self.c], self.stage_buf.at[slot, 0], self.local_sem.at[slot, 0]),
            pltpu.make_async_copy(self.swapped.at[zz], self.stage_buf.at[slot, 1], self.local_sem.at[slot, 1]),
        )

    def stage(self, n):
        copies, work, gy, gx, n_z = self.copies, self.work, self.gy, self.gx, self.n_z
        zs = ["z%d" % i for i in range(1, n_z)]
        lower, upper = self.halves
        if n == 0:
            copies.start(*self.names("s"))
        elif n == 1:
            copies.arrived(*self.names("s"))
            if self.stage_buf is None:

                def add_held(i, carry):
                    zz, yy, xx = i // 4, lax.rem(i // 2, 2), lax.rem(i, 2)
                    work[zz, yy, xx] = self.source[zz, self.c, yy, xx] + self.swapped[zz, yy, xx]
                    return carry

                lax.fori_loop(0, 4 * n_z, add_held, 0)
                copies.start(*self.names("a1", "b1"))
                return
            for copy in self.load(0):
                copy.start()
            for zz in range(n_z):
                if zz + 1 < n_z:
                    for copy in self.load(zz + 1):
                        copy.start()
                for copy in self.load(zz):
                    copy.wait()
                slot = zz % 2

                def add_quarter(i, carry):
                    yy, xx = i // 2, lax.rem(i, 2)
                    work[zz, yy, xx] = self.stage_buf[slot, 0, yy, xx] + self.stage_buf[slot, 1, yy, xx]
                    return carry

                lax.fori_loop(0, 4, add_quarter, 0)
            copies.start(*self.names("a1", "b1"))
        elif n == 2:
            copies.arrived(*self.names("a1"))

            def add_a(i, carry):
                zz, yy = i // 2, lax.rem(i, 2)
                work[zz, yy, gx, :, lower] = work[zz, yy, gx, :, lower] + self.first[0, zz, yy]
                return carry

            lax.fori_loop(0, 2 * n_z, add_a, 0)
            copies.start(*self.names("a2"))
            copies.arrived(*self.names("b1"))

            def add_b(i, carry):
                zz, xx = i // 2, lax.rem(i, 2)
                work[zz, gy, xx, :, upper] = work[zz, gy, xx, :, upper] + self.first[1, zz, xx]
                return carry

            lax.fori_loop(0, 2 * n_z, add_b, 0)
            copies.start(*self.names("b2"))
        elif n == 3:
            copies.arrived(*self.names("a2", "b2"))

            def add_c(zz, carry):
                work[zz, gy, gx, :, lower] = work[zz, gy, gx, :, lower] + self.second[0, zz]
                work[zz, gy, gx, :, upper] = work[zz, gy, gx, :, upper] + self.second[1, zz]
                return carry

            lax.fori_loop(0, n_z, add_c, 0)
            copies.start(*self.names(*zs))
        elif n == 4:
            copies.arrived(*self.names(*zs))
            total = work[self.z, gy, gx].astype(F32)
            for i in range(n_z - 1):
                total = total + self.along[i].astype(F32)
            self.final[gy, gx] = total.astype(BF16)
            copies.start(*self.names("fx", "fy", "fd"))
        else:
            copies.arrived(*self.names("fx", "fy", "fd"))
            copies.sent(*self.names("s", "a1", "b1", "a2", "b2", "fx", "fy", "fd", *zs))


def reduce_scratch(n_z, rows, width):
    return [
        pltpu.VMEM((n_z, 2, 2, rows, width), BF16),
        pltpu.VMEM((2, n_z, 2, rows, width // 2), BF16),
        pltpu.VMEM((2, n_z, rows, width // 2), BF16),
        pltpu.VMEM((n_z - 1, rows, width), BF16),
    ]


def n_reduce(n_z):
    return 8 + n_z - 1


TAIL_LANES = 32
PER_TILE = 128 // TAIL_LANES


def packed_shape(heads):
    return (heads + heads // PER_TILE, ROWS_S, 128)


def pack(ref, heads, p, side, state):
    head = p * 2 + side
    block = heads + head // PER_TILE
    ref[head] = state[:, :128].astype(BF16)
    rest = state[:, 128:]
    first, second = [pltpu.roll(rest, TAIL_LANES * (side + 2 * half), 1) if side + 2 * half else rest for half in range(2)]
    moved = jnp.where(lax.rem(p, 2) == 0, first, second).astype(BF16)
    if side == 0:
        held = jnp.where(lax.rem(p, 2) == 0, jnp.zeros_like(moved), ref[block])
        ref[block] = held + moved
    else:
        ref[block] = ref[block] + moved


class Chain:
    def __init__(self, copies, where, n_z, onward, own, mate, carry, out, pass_lead, pass_other):
        dp, sp, g, gy, gx, z, c, across_x, across_y, diagonal, partner = where
        lead = 1 if onward else 0
        self.copies, self.n_z = copies, n_z
        self.own, self.mate, self.carry, self.out = own, mate, carry, out
        self.pass_lead, self.pass_other = pass_lead, pass_other
        self.leads = c == lead
        self.place = z if onward else n_z - 1 - z
        to = lax.rem(z + 1, n_z) if onward else lax.rem(z + n_z - 1, n_z)
        before = lax.rem(z + n_z - 1, n_z) if onward else lax.rem(z + 1, n_z)
        self.next_device, self.last_device = (dp, to * 2 + c), (dp, before * 2 + c)
        copies.add("own", own, mate, partner)
        copies.add("raw", carry, carry, partner)
        copies.add("carry", out, carry, self.next_device)

    def begin(self):
        @pl.when(jnp.logical_not(self.leads))
        def _():
            self.copies.start("own")

        @pl.when(self.leads & (self.place == 0))
        def _():
            self.carry[...] = jnp.zeros_like(self.carry)

    def middle(self, now):
        now = now & self.leads

        @pl.when(now)
        def _():
            self.copies.arrived("own")

        @pl.when(now & (self.place > 0))
        def _():
            self.copies.arrived("carry")

        @pl.when(now)
        def _():
            self.copies.start("raw")

        @pl.when(now & (self.place < self.n_z - 1))
        def _():
            def one(head, carry):
                inner = self.mate[head].astype(F32) + self.pass_other * self.carry[head].astype(F32)
                self.out[head] = (self.own[head].astype(F32) + self.pass_lead * inner).astype(BF16)
                return carry

            lax.fori_loop(0, self.own.shape[0], one, 0)
            self.copies.start("carry")

    def finish(self, result, weights):
        heads = result.shape[0]

        def unpack(value):
            def group(q, carry):
                rest = value(heads + q)
                for j in range(PER_TILE):
                    head = q * PER_TILE + j
                    tail = pltpu.roll(rest, 128 - TAIL_LANES * j, 1) if j else rest
                    result[head] = jnp.concatenate(
                        [value(head) * weights[:, :128], tail * weights[:, 128:]], axis=1
                    ).astype(BF16)
                return carry

            lax.fori_loop(0, heads // PER_TILE, group, 0)

        @pl.when(jnp.logical_not(self.leads))
        def _():
            self.copies.arrived("raw")
            unpack(lambda i: self.carry[i].astype(F32))

        @pl.when(self.leads)
        def _():
            unpack(lambda i: self.mate[i].astype(F32) + self.pass_other * self.carry[i].astype(F32))

    def drain(self):
        @pl.when(jnp.logical_not(self.leads))
        def _():
            self.copies.sent("own")

        @pl.when(self.leads)
        def _():
            self.copies.sent("raw")

        @pl.when(self.leads & (self.place < self.n_z - 1))
        def _():
            self.copies.sent("carry")


class Documents:
    def __init__(self, doc_ref, sp, n_sp):
        self.ref, self.n_sp, self.tok = doc_ref, n_sp, doc_ref.shape[1] // n_sp
        self.row = self.of(sp)
        self.column = jnp.broadcast_to(self.row, (128, self.tok)).T[:, 0:1]

    def of(self, sp):
        return self.ref[:, pl.ds(pl.multiple_of(sp * self.tok, 128), self.tok)].astype(F32)

    def last(self, sp):
        value = self.of(jnp.maximum(sp, 0))[:, self.tok - 1 : self.tok]
        return jnp.where(sp >= 0, value, -1.0)

    def first(self, sp):
        value = self.of(jnp.minimum(sp, self.n_sp - 1))[:, 0:1]
        return jnp.where(sp < self.n_sp, value, -2.0)

    def through(self, here, there):
        return jnp.broadcast_to(jnp.where(here == there, 1.0, 0.0), (1, 128))


def rows_sum(values):
    total = values[0]
    for value in values[1:]:
        total = total + value
    return total


CHAIN_STEPS = 3
CHAIN_BACK_STEPS = 5
CHUNK = 256
UNITS = 4
EARLY = 2


def units_of(width):
    chunks = -(-width // CHUNK)
    step = -(-chunks // UNITS)
    return [(first, min(chunks, first + step)) for first in range(0, chunks, step)]


def forward_kernel(
    n_sp, x_ref, gain_a_ref, gain_m_ref, doc_ref, table_ref, wo_ref, wg_ref, wu_ref, wd_ref, wq_ref, wk_ref, wv_ref, *rest,
):
    n_unit = len(units_of(wd_ref.shape[0]))
    (att_ref, inv_ref, state_ref, gain_ref, q_ref, k_ref, v_ref, normed_ref, w_joint_ref), rest = rest[:9], rest[9:]
    fulls, rest = rest[: 3 + EARLY], rest[3 + EARLY :]
    kept, rest = rest[: n_unit - EARLY], rest[n_unit - EARLY :]
    (joint_own, more_own, out_own), rest = rest[:3], rest[3:]
    ffn_own, rest = rest[:n_unit], rest[n_unit:]
    (
        mask_ref, joint_vm, num_ref, den_ref, own_state, mate_state, in_state, out_state, gains_ref, gains_in,
        prior_ref, q_scr, k_scr, v_scr, normed_scr, send_sem, recv_sem, local_sem,
    ) = rest
    tok = x_ref.shape[0]
    n_z = n_sp // 2
    lanes = q_ref.shape[1]
    pairs = v_ref.shape[1] // 128
    where = place(n_sp)
    dp, sp, g, gy, gx, z, c, across_x, across_y, diagonal, partner = where
    copies = Copies(send_sem, recv_sem)
    joint_full, more_full = fulls[:2]
    owns = (joint_own, more_own, out_own) + tuple(ffn_own[:EARLY])
    gathers = [Gather(copies, k, n_z, own, full, where) for k, (own, full) in enumerate(zip(owns, fulls))]
    others = [(dp, lax.rem(sp + i, n_sp)) for i in range(1, n_sp)]
    for i, device in enumerate(others, 1):
        copies.add(("gain", i), gains_ref, gains_in.at[i - 1], device)
    docs = Documents(doc_ref, sp, n_sp)
    even = sp - c
    chain = Chain(
        copies, where, n_z, True, own_state, mate_state, in_state, out_state,
        docs.through(docs.last(even + 1), docs.last(even)), docs.through(docs.last(even), docs.last(even - 1)),
    )
    part_lane = lax.broadcasted_iota(jnp.int32, gains_ref.shape, 1)
    part = jnp.concatenate([jnp.broadcast_to(gain_a_ref[...], (4, gain_a_ref.shape[1])),
                            jnp.broadcast_to(gain_m_ref[...], (4, gain_m_ref.shape[1]))], axis=0).astype(F32)
    if part.shape[1] < gains_ref.shape[1]:
        part = jnp.concatenate([part] * n_sp, axis=1)
    gains_ref[...] = jnp.where(part_lane // (gains_ref.shape[1] // n_sp) == sp, part, 0.0)
    assembled = [
        pltpu.make_async_copy(wq_ref, joint_own.at[:, 0:lanes], local_sem.at[0]),
        pltpu.make_async_copy(wk_ref, joint_own.at[:, lanes : 2 * lanes], local_sem.at[1]),
        pltpu.make_async_copy(
            wv_ref.at[:, 0 : joint_own.shape[1] - 2 * lanes], joint_own.at[:, 2 * lanes :], local_sem.at[2]
        ),
        pltpu.make_async_copy(wv_ref.at[:, joint_own.shape[1] - 2 * lanes :], more_own, local_sem.at[3]),
    ]
    for copy in assembled:
        copy.start()
    meet(others + [across_x, across_y])
    copies.start(*[("gain", i) for i in range(1, n_sp)])
    for copy in assembled:
        copy.wait()
    gathers[0].stage(0)
    gathers[1].stage(0)
    out_own[...] = wo_ref[...].T
    width = wd_ref.shape[0]
    for own, (first, last) in zip(ffn_own, units_of(width)):
        lo, hi = first * CHUNK, min(last * CHUNK, width)
        span = (last - first) * CHUNK
        for i, piece in enumerate((wg_ref[lo:hi, :].T, wu_ref[lo:hi, :].T, wd_ref[lo:hi, :].T)):
            if hi - lo < span:
                own[:, (i + 1) * span - CHUNK : (i + 1) * span] = jnp.zeros((own.shape[0], CHUNK), BF16)
            own[:, i * span : i * span + hi - lo] = piece

    table = table_ref[...]
    row = lax.broadcasted_iota(jnp.int32, (tok, tok), 0)
    col = lax.broadcasted_iota(jnp.int32, (tok, tok), 1)
    mask_ref[...] = jnp.where((row >= col) & (docs.column == docs.row), 1.0, 0.0)
    prior_ref[...] = jnp.broadcast_to(jnp.where(docs.column == docs.last(sp - 1), 1.0, 0.0), prior_ref.shape)
    copies.arrived(*[("gain", i) for i in range(1, n_sp)])
    gain_ref[...] = gains_ref[...] + rows_sum([gains_in[i] for i in range(n_sp - 1)])
    x = x_ref[...].astype(F32)
    scale = lax.rsqrt(jnp.mean(x * x, axis=1, keepdims=True) + EPSILON)
    normed_scr[...] = (x * scale * gain_ref[0:1]).astype(BF16)
    local = [
        pltpu.make_async_copy(own, gather.own_place, local_sem.at[k])
        for k, (own, gather) in enumerate(zip(owns, gathers))
    ] + [
        pltpu.make_async_copy(own, keep, local_sem.at[len(owns) + k])
        for k, (own, keep) in enumerate(zip(ffn_own[EARLY:], kept))
    ]
    for copy in local:
        copy.start()
    gathers[0].stage(1)
    gathers[1].stage(1)
    gathers[0].stage(2)
    gathers[2].stage(0)
    gathers[3].stage(0)
    gathers[1].stage(2)
    gathers[0].stage(3)
    gathers[1].stage(3)
    gathers[0].stage(4)
    for copy in local:
        copy.wait()
    split = joint_full.shape[1]
    fetches = [
        pltpu.make_async_copy(joint_full, joint_vm.at[:, 0:split], local_sem.at[0]),
        pltpu.make_async_copy(more_full, joint_vm.at[:, split:], local_sem.at[1]),
    ]
    fetches[0].start()
    fetches[0].wait()
    wide = joint_vm.shape[1]
    for first in range(0, wide, BLK):
        if first == split:
            gathers[1].stage(4)
            fetches[1].start()
            fetches[1].wait()
        part = mm(normed_scr[...], joint_vm[:, first : first + BLK]).astype(BF16)
        if first < lanes:
            q_scr[:, first : first + BLK] = part
        elif first < 2 * lanes:
            k_scr[:, first - lanes : first - lanes + BLK] = part
        else:
            v_scr[:, first - 2 * lanes : first - 2 * lanes + BLK] = part
    saves = [
        pltpu.make_async_copy(src, dst, local_sem.at[i])
        for i, (src, dst) in enumerate(
            ((q_scr, q_ref), (k_scr, k_ref), (v_scr, v_ref), (normed_scr, normed_ref), (joint_vm, w_joint_ref))
        )
    ]
    for copy in saves:
        copy.start()

    tail = jnp.where(docs.row == docs.last(sp), 1.0, 0.0)

    def at(p, step, *todo):
        @pl.when(p == step)
        def _():
            for k, n in todo:
                gathers[k].stage(n)

    def state_pair(p, carry):
        at(p, 0, (2, 1))
        at(p, 2, (3, 1), (4, 0))
        at(p, 5, (2, 2))
        columns = pl.ds(pl.multiple_of(p * 128, 128), 128)
        v_t = v_scr[:, columns].astype(F32).T * tail
        ones = jnp.broadcast_to(tail, (16, tail.shape[1]))
        for side in range(2):
            head = p * 2 + side
            sel = selectors(table, head, lanes)
            one, two = factors(k_scr[...], sel, table)
            phi = (one * two).astype(BF16)
            lhs = jnp.concatenate([v_t[side * 64 : side * 64 + 64], ones], axis=0)
            pack(own_state, 2 * pairs, p, side, mm(lhs.astype(BF16), phi))
        return carry

    lax.fori_loop(0, pairs, state_pair, 0)

    chain.begin()
    turn = jnp.minimum(z * CHAIN_STEPS, pairs - 1)

    lane = lax.broadcasted_iota(jnp.int32, (BLK, 128), 1)

    def intra_pair(p, carry):
        at(p, 1, (2, 3), (3, 2))
        at(p, 3, (4, 1))
        at(p, 4, (3, 3))
        at(p, 7, (4, 2))
        chain.middle(p == turn)
        columns = pl.ds(pl.multiple_of(p * 128, 128), 128)
        v_hat = with_ones(v_scr[:, columns])
        heads = [head_lanes(q_scr[...], p * 2 + side) for side in range(2)]
        for i in range(tok // BLK):
            rows = slice(i * BLK, (i + 1) * BLK)
            keys = slice(0, (i + 1) * BLK)
            totals = []
            for side in range(2):
                t = mm(heads[side][rows], k_scr[keys, :], NT) + 4.0
                w = ((t * t + 16.0) * mask_ref[rows, keys]).astype(BF16)
                totals.append(mm(w, v_hat[keys]))
            num_ref[rows, columns] = jnp.where(lane < 64, totals[0][:, :128], totals[1][:, :128])
            den_ref[rows, columns] = jnp.where(lane < 64, totals[0][:, 128:], totals[1][:, 128:])
        return carry

    lax.fori_loop(0, pairs, intra_pair, 0)
    chain.finish(state_ref, table[4:5])
    prior = prior_ref[:, 0:1]
    wide_lane = lax.broadcasted_iota(jnp.int32, (tok, 128), 1)

    def inter_pair(p, carry):
        at(p, 4, (4, 3))
        columns = pl.ds(pl.multiple_of(p * 128, 128), 128)
        totals = []
        for side in range(2):
            head = p * 2 + side
            sel = selectors(table, head, lanes)
            state = state_ref[head]
            z_rows = jnp.broadcast_to(state[64:65].astype(F32), (128, PAD_F)).astype(BF16)
            one, two = factors(q_scr[...], sel, table)
            totals.append(mm((one * two).astype(BF16), placed(state, side, z_rows), NT) * prior)
        num = num_ref[:, columns] + jnp.where(wide_lane < 64, totals[0][:, :128], totals[1][:, :128])
        den = den_ref[:, columns] + jnp.where(wide_lane < 64, totals[0][:, 128:], totals[1][:, 128:])
        inv = 1.0 / den
        inv_ref[:, columns] = inv.astype(BF16)
        att_ref[:, columns] = (num * inv).astype(BF16)
        return carry

    lax.fori_loop(0, pairs, inter_pair, 0)
    for gather in gathers[2:]:
        gather.stage(4)
    for copy in saves:
        copy.wait()
    copies.sent(*[("gain", i) for i in range(1, n_sp)])
    chain.drain()


def forward(n_sp, x, gain_a, gain_m, docs, table, wo, wg, wu, wd, wq, wk, wv):
    tok, dim = x.shape
    lanes, values = wq.shape[1], wv.shape[1]
    heads = lanes // FEAT
    shard = wq.shape[0]
    vmem, anywhere = pl.BlockSpec(memory_space=pltpu.VMEM), pl.BlockSpec(memory_space=pl.ANY)
    n_z = n_sp // 2
    spans = [3 * CHUNK * (last - first) for first, last in units_of(wd.shape[0])]
    joint = 2 * lanes + values
    gathered = [joint // 2, joint // 2, dim] + spans[:EARLY]
    sems = len(gathered) * n_copies(n_z) + n_sp + 2
    shape = jax.ShapeDtypeStruct
    result = pl.pallas_call(
        functools.partial(forward_kernel, n_sp),
        out_shape=(
            shape((tok, values), BF16), shape((tok, values), BF16), shape((heads, ROWS_S, PAD_F), BF16),
            shape((8, dim), F32), shape((tok, lanes), BF16), shape((tok, lanes), BF16),
            shape((tok, values), BF16), shape((tok, dim), BF16), shape((dim, joint), BF16),
        )
        + tuple(shape((shard * n_sp, w), BF16) for w in gathered)
        + tuple(shape((shard, w), BF16) for w in spans[EARLY:]),
        in_specs=[vmem] * 9 + [anywhere] * 3,
        out_specs=(vmem,) * 4 + (anywhere,) * (5 + len(gathered) + len(spans) - EARLY),
        scratch_shapes=[pltpu.VMEM((shard, w), BF16) for w in [joint // 2, joint // 2, dim] + spans]
        + [
            pltpu.VMEM((tok, tok), F32),
            pltpu.VMEM((dim, joint), BF16),
            pltpu.VMEM((tok, values), F32),
            pltpu.VMEM((tok, values), F32),
            pltpu.VMEM(packed_shape(heads), BF16),
            pltpu.VMEM(packed_shape(heads), BF16),
            pltpu.VMEM(packed_shape(heads), BF16),
            pltpu.VMEM(packed_shape(heads), BF16),
            pltpu.VMEM((8, dim), F32),
            pltpu.VMEM((n_sp - 1, 8, dim), F32),
            pltpu.VMEM((tok, 128), F32),
            pltpu.VMEM((tok, lanes), BF16),
            pltpu.VMEM((tok, lanes), BF16),
            pltpu.VMEM((tok, values), BF16),
            pltpu.VMEM((tok, dim), BF16),
            pltpu.SemaphoreType.DMA((sems,)),
            pltpu.SemaphoreType.DMA((sems,)),
            pltpu.SemaphoreType.DMA((10,)),
        ],
        compiler_params=pltpu.CompilerParams(
            collective_id=0, has_side_effects=True, vmem_limit_bytes=60 << 20
        ),
        name="forward",
    )(x, gain_a, gain_m, docs, table, wo, wg, wu, wd, wq, wk, wv)
    n = 9 + len(gathered)
    return result[:9], result[11], result[12:n], result[n:]


def backward_kernel(
    n_sp, widths, q_ref, k_ref, v_ref, g_ref, att_ref, inv_ref, prior_state_ref, doc_ref, table_ref, *rest,
):
    n_red = len(widths)
    sources, rest = rest[:n_red], rest[n_red:]
    (gq_ref, gk_ref, gv_ref), rest = rest[:3], rest[3:]
    finals, rest = rest[:n_red], rest[n_red:]
    swaps, rest = rest[:n_red], rest[n_red:]
    buffers, rest = [rest[4 * i : 4 * i + 4] for i in range(n_red)], rest[4 * n_red :]
    (
        stage_buf, mask_ref, ghat_ref, gq_acc, gk_acc, own_state, mate_state, in_state, out_state, later_state,
        prior_ref, later_ref,
        send_sem, recv_sem, local_sem,
    ) = rest
    tok, lanes = q_ref.shape
    n_z = n_sp // 2
    pairs = v_ref.shape[1] // 128
    where = place(n_sp)
    dp, sp, g, gy, gx, z, c, across_x, across_y, diagonal, partner = where
    copies = Copies(send_sem, recv_sem)
    reduces = [
        Reduce(
            copies, k, n_z, where, sources[k], swaps[k], buffers[k], finals[k],
            stage_buf.at[:, :, :, :, :, 0 : widths[k]], local_sem,
        )
        for k in range(n_red)
    ]
    docs = Documents(doc_ref, sp, n_sp)
    even = sp - c
    chain = Chain(
        copies, where, n_z, False, own_state, mate_state, in_state, out_state,
        docs.through(docs.first(even), docs.first(even + 1)), docs.through(docs.first(even + 1), docs.first(even + 2)),
    )
    along = [(dp, lax.rem(z + i, n_z) * 2 + c) for i in range(1, n_z)]
    meet([partner, across_x, across_y, diagonal] + along)
    for reduce in reduces:
        reduce.stage(0)

    def at(p, step, *todo):
        @pl.when(p == step)
        def _():
            for k, n in todo:
                reduces[k].stage(n)

    table = table_ref[...]
    row = lax.broadcasted_iota(jnp.int32, (tok, tok), 0)
    col = lax.broadcasted_iota(jnp.int32, (tok, tok), 1)
    mask_ref[...] = jnp.where((row <= col) & (docs.column == docs.row), 1.0, 0.0)
    prior_ref[...] = jnp.broadcast_to(jnp.where(docs.column == docs.last(sp - 1), 1.0, 0.0), prior_ref.shape)
    later_ref[...] = jnp.broadcast_to(jnp.where(docs.column == docs.first(sp + 1), 1.0, 0.0), later_ref.shape)
    gq_acc[...] = jnp.zeros_like(gq_acc)
    gk_acc[...] = jnp.zeros_like(gk_acc)
    r = lax.broadcasted_iota(jnp.int32, (128, 128), 0)
    c128 = lax.broadcasted_iota(jnp.int32, (128, 128), 1)
    same = jnp.where(r // 64 == c128 // 64, 1.0, 0.0).astype(BF16)
    lane64 = lax.broadcasted_iota(jnp.int32, (tok, 128), 1) % 64
    head_row = jnp.where(docs.row == docs.first(sp), 1.0, 0.0)

    def ghat_pair(p, carry):
        for when, todo in GHAT_SCHEDULE:
            at(p, when, *todo)
        columns = pl.ds(pl.multiple_of(p * 128, 128), 128)
        scaled = g_ref[:, columns].astype(F32) * inv_ref[:, columns].astype(F32)
        product = scaled * att_ref[:, columns].astype(F32)
        high = product.astype(BF16)
        low = (product - high.astype(F32)).astype(BF16)
        dots = -(mm(high, same) + mm(low, same))
        dots_high = dots.astype(BF16)
        dots_low = (dots - dots_high.astype(F32)).astype(BF16)
        extra = jnp.where(lane64 == 0, dots_high, jnp.where(lane64 == 1, dots_low, jnp.zeros_like(dots_low)))
        ghat = jnp.concatenate([scaled.astype(BF16), extra], axis=1)
        ghat_ref[p] = ghat
        ghat_t = ghat.astype(F32).T * head_row
        for side in range(2):
            head = p * 2 + side
            sel = selectors(table, head, lanes)
            one, two = factors(q_ref[...], sel, table)
            phi = (one * two).astype(BF16)
            lhs = jnp.concatenate(
                [ghat_t[side * 64 : side * 64 + 64], ghat_t[128 + side * 64 : 128 + side * 64 + 16]], axis=0
            )
            state = mm(lhs.astype(BF16), phi)
            z_row = jnp.sum(state[64:80], axis=0, keepdims=True)
            pack(
                own_state, 2 * pairs, p, side,
                jnp.concatenate([state[0:64], jnp.broadcast_to(z_row, (16, PAD_F))], axis=0),
            )
        return carry

    lax.fori_loop(0, pairs, ghat_pair, 0)

    chain.begin()
    turn = jnp.minimum((n_z - 1 - z) * CHAIN_BACK_STEPS, 2 * pairs - 1)

    lane = lax.broadcasted_iota(jnp.int32, (tok, 256), 1)
    first_row = lax.broadcasted_iota(jnp.int32, (128, PAD_F), 0)

    def main_pair(p, carry):
        columns = pl.ds(pl.multiple_of(p * 128, 128), 128)
        v_hat = with_ones(v_ref[:, columns])
        gv = [jnp.zeros((BLK, 128), F32) for _ in range(tok // BLK)]
        for side in range(2):
            step = p * 2 + side
            for when, todo in SCHEDULE:
                if when % 2 == side:
                    at(step, when, *todo)
            chain.middle(step == turn)
            head = p * 2 + side
            sel = selectors(table, head, lanes)
            ghat = jnp.where((lane % 128) // 64 == side, ghat_ref[p], jnp.zeros((tok, 256), BF16))
            q_head = head_lanes(q_ref[...], head)
            q_twice = q_head + q_head
            k_twice = head_lanes(k_ref[...], head, 2)
            prior = prior_state_ref[head]
            z_two = jnp.where(first_row // 2 == side * 32, prior[64:65], jnp.zeros((128, PAD_F), BF16))
            rows_p = placed(prior, side, z_two)
            q_one, q_two = factors(q_ref[...], sel, table)
            d_phi = mm(ghat, rows_p) * prior_ref[:, 0:1]
            gq_acc[...] += mm((d_phi * q_two).astype(BF16), sel[0], NT) + mm(
                (d_phi * q_one).astype(BF16), sel[1], NT
            )
            for j in range(tok // BLK):
                rows = slice(j * BLK, (j + 1) * BLK)
                onward = slice(j * BLK, tok)
                t = mm(k_ref[rows, :], q_head[onward], NT) + 4.0
                g_w = mm(v_hat[rows], ghat[onward], NT)
                mask = mask_ref[rows, onward]
                masked_t = t * mask
                w = (masked_t * t + 16.0 * mask).astype(BF16)
                g_s = (g_w * masked_t).astype(BF16)
                gv[j] = gv[j] + mm(w, ghat[onward, 0:128])
                gk_acc[rows, :] += mm(g_s, q_twice[onward])
                gq_acc[onward, :] += mm(g_s, k_twice[rows], TN)
        for j in range(tok // BLK):
            rows = slice(j * BLK, (j + 1) * BLK)
            gv_ref[rows, columns] = gv[j].astype(BF16)
        return carry

    lax.fori_loop(0, pairs, main_pair, 0)
    chain.drain()
    chain.finish(later_state, table[4:5])

    def later_pair(p, carry):
        for when, todo in LATE_SCHEDULE:
            at(p, when, *todo)
        columns = pl.ds(pl.multiple_of(p * 128, 128), 128)
        v_hat = with_ones(v_ref[:, columns])
        gv_inter = None
        for side in range(2):
            head = p * 2 + side
            sel = selectors(table, head, lanes)
            later = later_state[head]
            z_one = jnp.where(first_row == 0, later[64:65], jnp.zeros((128, PAD_F), BF16))
            rows_n = placed(later, side, z_one)
            k_one, k_two = factors(k_ref[...], sel, table)
            phi_k = (k_one * k_two).astype(BF16)
            gvi = mm(phi_k, rows_n[0:128], NT)
            gv_inter = gvi if gv_inter is None else gv_inter + gvi
            d_phi = mm(v_hat, rows_n) * later_ref[:, 0:1]
            gk_acc[...] += mm((d_phi * k_two).astype(BF16), sel[0], NT) + mm(
                (d_phi * k_one).astype(BF16), sel[1], NT
            )
        gv_ref[:, columns] = (gv_ref[:, columns].astype(F32) + gv_inter * later_ref[...]).astype(BF16)
        return carry

    lax.fori_loop(0, pairs, later_pair, 0)
    gq_ref[...] = gq_acc[...].astype(BF16)
    gk_ref[...] = gk_acc[...].astype(BF16)
    for k, n in LAST_SCHEDULE:
        reduces[k].stage(n)


GHAT_SCHEDULE = ((1, ((0, 1),)), (3, ((1, 1),)), (4, ((0, 2),)), (6, ((2, 1),)), (7, ((1, 2),)), )
SCHEDULE = ((1, ((0, 3),)), (2, ((3, 1),)), (4, ((2, 2),)), (6, ((1, 3),)), (7, ((0, 4),)), (9, ((3, 2),)), (10, ((2, 3),)), (12, ((1, 4),)), (14, ((0, 5),)), (15, ((3, 3),)), )
LATE_SCHEDULE = ((1, ((2, 4),)), (2, ((1, 5),)), (4, ((3, 4),)), (5, ((2, 5),)), (7, ((3, 5),)), )
LAST_SCHEDULE = ()


def shards_of(parts):
    return [part.reshape(-1, part.shape[-1]) for part in parts]


def backward(n_sp, arrays, grads):
    q, v = arrays[0], arrays[2]
    tok, lanes = q.shape
    heads = lanes // FEAT
    n_z = n_sp // 2
    rows = grads[0].shape[4]
    widths = tuple(grad.shape[5] for grad in grads)
    n_red = len(grads)
    vmem, anywhere = pl.BlockSpec(memory_space=pltpu.VMEM), pl.BlockSpec(memory_space=pl.ANY)
    shape = jax.ShapeDtypeStruct
    sems = n_red * n_reduce(n_z) + 3
    result = pl.pallas_call(
        functools.partial(backward_kernel, n_sp, widths),
        out_shape=(shape(q.shape, BF16), shape(q.shape, BF16), shape(v.shape, BF16))
        + tuple(shape((2, 2, rows, w), BF16) for w in widths)
        + tuple(shape((n_z, 2, 2, rows, w), BF16) for w in widths),
        in_specs=[vmem] * len(arrays) + [anywhere] * n_red,
        out_specs=(vmem,) * (3 + n_red) + (anywhere,) * n_red,
        scratch_shapes=sum([reduce_scratch(n_z, rows, w) for w in widths], [])
        + [
            pltpu.VMEM((2, 2, 2, 2, rows, max(widths)), BF16),
            pltpu.VMEM((tok, tok), F32),
            pltpu.VMEM((heads // 2, tok, 256), BF16),
            pltpu.VMEM(q.shape, F32),
            pltpu.VMEM(q.shape, F32),
            pltpu.VMEM(packed_shape(heads), BF16),
            pltpu.VMEM(packed_shape(heads), BF16),
            pltpu.VMEM(packed_shape(heads), BF16),
            pltpu.VMEM(packed_shape(heads), BF16),
            pltpu.VMEM((heads, ROWS_S, PAD_F), BF16),
            pltpu.VMEM((tok, 128), F32),
            pltpu.VMEM((tok, 128), F32),
            pltpu.SemaphoreType.DMA((sems,)),
            pltpu.SemaphoreType.DMA((sems,)),
            pltpu.SemaphoreType.DMA((2, 2)),
        ],
        compiler_params=pltpu.CompilerParams(
            collective_id=1, has_side_effects=True, vmem_limit_bytes=63 << 20
        ),
        name="backward",
    )(*arrays, *grads)
    return result[:3], shards_of(result[3 : 3 + n_red])


def reduce_units(chunks):
    edges = [0, 2, 4, 6, 8, chunks]
    return list(zip(edges[:-1], edges[1:]))


IN_FFN = 2
FFN_SCHEDULE = {
    1: (("g", 0, 1), ("g", 1, 0)),
    3: (("g", 0, 2), ("r", 0, 0)),
    4: (("g", 1, 1), ("g", 0, 3), ("r", 0, 1)),
    5: (("g", 0, 4), ("r", 1, 0)),
    6: (("g", 1, 2), ("r", 0, 2), ("r", 1, 1)),
    7: (("g", 1, 3),),
    8: (("g", 1, 4), ("r", 0, 3), ("r", 1, 2)),
    9: (("r", 1, 3),),
    10: (("r", 0, 4),),
}
FFN_LATE = (("r", 1, 4),)
FFN_LAST = (("r", 0, 5), ("r", 1, 5))


def ffn_kernel(n_sp, gather_units, chunks, x_ref, att_ref, out_w_ref, gain_ref, cot_ref, *rest):
    n_unit = len(gather_units)
    sums = reduce_units(chunks)
    n_sum = len(sums)
    early, rest = rest[:EARLY], rest[EARLY:]
    kept, rest = rest[: n_unit - EARLY], rest[n_unit - EARLY :]
    ggain_ref, rest = rest[0], rest[1:]
    finals, rest = rest[:IN_FFN], rest[IN_FFN:]
    (output_ref, gh_ref, gatt_ref, gout_ref), rest = rest[:4], rest[4:]
    grads, rest = rest[: n_sum - IN_FFN], rest[n_sum - IN_FFN :]
    late, rest = rest[: n_unit - EARLY], rest[n_unit - EARLY :]
    grads, rest = rest[:IN_FFN] + grads, rest[IN_FFN:]
    swaps, rest = rest[:IN_FFN], rest[IN_FFN:]
    buffers, rest = [rest[4 * i : 4 * i + 4] for i in range(IN_FFN)], rest[4 * IN_FFN :]
    (
        hid, n2, n2_t, cot_t, acc_o, acc_n, w_buf, g_buf, send_sem, recv_sem, w_sem, g_sem, o_sem,
    ) = rest
    tok, dim = x_ref.shape
    n_z = n_sp // 2
    where = place(n_sp)
    dp, sp, g, gy, gx, z, c, across_x, across_y, diagonal, partner = where
    copies = Copies(send_sem, recv_sem)
    gathers = [Gather(copies, ("g", k), n_z, own, full, where) for k, (own, full) in enumerate(zip(kept, late))]
    reduces = [
        Reduce(copies, ("r", k), n_z, where, grads[k], swaps[k], buffers[k], finals[k])
        for k in range(IN_FFN)
    ]
    along = [(dp, lax.rem(z + i, n_z) * 2 + c) for i in range(1, n_z)]
    meet([partner, across_x, across_y, diagonal] + along)
    gathers[0].stage(0)
    own_copies = [
        pltpu.make_async_copy(own, gather.own_place, o_sem.at[k])
        for k, (own, gather) in enumerate(zip(kept, gathers))
    ]
    for copy in own_copies:
        copy.start()

    def run(todo):
        for kind, k, n in todo:
            (gathers if kind == "g" else reduces)[k].stage(n)

    fulls = list(early) + list(late)

    def load(chunk, slot, do_wait=False):
        if do_wait:
            for i in range(3):
                pltpu.make_async_copy(fulls[0].at[:, 0:CHUNK], w_buf.at[slot, i], w_sem.at[slot, i]).wait()
            return
        for full, (first, last) in zip(fulls, gather_units):
            @pl.when((chunk >= first) & (chunk < last))
            def _():
                for i in range(3):
                    lane = pl.multiple_of((chunk - first + i * (last - first)) * CHUNK, CHUNK)
                    pltpu.make_async_copy(full.at[:, pl.ds(lane, CHUNK)], w_buf.at[slot, i], w_sem.at[slot, i]).start()

    def save(chunk, slot, do_wait=False):
        if do_wait:
            for i in range(3):
                pltpu.make_async_copy(
                    g_buf.at[slot, i], grads[0].at[:, :, :, :, :, 0:CHUNK], g_sem.at[slot, i]
                ).wait()
            return
        for grad, (first, last) in zip(grads, sums):
            @pl.when((chunk >= first) & (chunk < last))
            def _():
                for i in range(3):
                    lane = pl.multiple_of((chunk - first + i * (last - first)) * CHUNK, CHUNK)
                    pltpu.make_async_copy(
                        g_buf.at[slot, i], grad.at[:, :, :, :, :, pl.ds(lane, CHUNK)], g_sem.at[slot, i]
                    ).start()

    load(0, 0)
    gain = gain_ref[4:5]
    for i in range(tok // BLK):
        rows = slice(i * BLK, (i + 1) * BLK)
        hidden = x_ref[rows, :].astype(F32) + mm(att_ref[rows, :], out_w_ref[...], NT)
        hid[rows, :] = hidden
        scale = lax.rsqrt(jnp.mean(hidden * hidden, axis=1, keepdims=True) + EPSILON)
        normed = (hidden * scale * gain).astype(BF16)
        n2[rows, :] = normed
        n2_t[:, rows] = normed.T
        cot_t[:, rows] = cot_ref[rows, :].T
    acc_o[...] = jnp.zeros_like(acc_o)
    acc_n[...] = jnp.zeros_like(acc_n)
    for copy in own_copies:
        copy.wait()
    grad_shape = g_buf.shape[2:]

    def step(chunk, carry):
        slot = lax.rem(chunk, 2)
        load(chunk, slot, True)

        @pl.when(chunk >= 2)
        def _():
            save(chunk, slot, True)

        for when, todo in FFN_SCHEDULE.items():
            @pl.when(chunk == when)
            def _():
                run(todo)

        @pl.when(chunk + 1 < chunks)
        def _():
            load(chunk + 1, 1 - slot)

        wg, wu, wd = w_buf[slot, 0], w_buf[slot, 1], w_buf[slot, 2]
        gate = mm(n2[...], wg)
        up = mm(n2[...], wu)
        g_mixed = mm(cot_ref[...], wd)
        sig = 1.0 / (1.0 + jnp.exp(-gate))
        act = gate * sig
        mixed = (act * up).astype(BF16)
        g_gate = (g_mixed * up * sig * (1.0 + gate * (1.0 - sig))).astype(BF16)
        g_up = (g_mixed * act).astype(BF16)
        g_buf[slot, 0] = mm(n2_t[...], g_gate).astype(BF16).reshape(grad_shape)
        g_buf[slot, 1] = mm(n2_t[...], g_up).astype(BF16).reshape(grad_shape)
        g_buf[slot, 2] = mm(cot_t[...], mixed).astype(BF16).reshape(grad_shape)
        save(chunk, slot)
        acc_o[...] += mm(mixed, wd, NT)
        acc_n[...] += mm(g_gate, wg, NT) + mm(g_up, wu, NT)
        return carry

    lax.fori_loop(0, chunks, step, 0)
    run(FFN_LATE)
    total = jnp.zeros((1, dim), F32)
    for i in range(tok // BLK):
        rows = slice(i * BLK, (i + 1) * BLK)
        hidden = hid[rows, :]
        n2[rows, :] = (hidden + acc_o[rows, :]).astype(BF16)
        scale = lax.rsqrt(jnp.mean(hidden * hidden, axis=1, keepdims=True) + EPSILON)
        e = acc_n[rows, :]
        total = total + jnp.sum(e * hidden * scale, axis=0, keepdims=True)
        eg = e * gain
        inner = jnp.mean(eg * hidden, axis=1, keepdims=True)
        gh = cot_ref[rows, :].astype(F32) + scale * eg - hidden * (scale * scale * scale * inner)
        acc_o[rows, :] = gh
        n2_t[rows, :] = gh.astype(BF16)
        cot_t[rows, :] = mm(n2_t[rows, :], out_w_ref[...]).astype(BF16)
    ggain_ref[...] = jnp.broadcast_to(total, ggain_ref.shape)
    outs = [
        pltpu.make_async_copy(n2, output_ref, o_sem.at[0]),
        pltpu.make_async_copy(acc_o, gh_ref, o_sem.at[1]),
        pltpu.make_async_copy(cot_t, gatt_ref, o_sem.at[2]),
    ]
    for copy in outs:
        copy.start()
    save(chunks - 2, (chunks - 2) % 2, True)
    save(chunks - 1, (chunks - 1) % 2, True)
    for i, first in enumerate(range(0, att_ref.shape[1], CHUNK)):
        columns = slice(first, first + CHUNK)
        piece = g_buf.at[i // 3, i % 3]
        piece[...] = mm(n2_t[...], att_ref[:, columns], TN).astype(BF16).reshape(grad_shape)
        outs.append(
            pltpu.make_async_copy(
                piece, gout_ref.at[:, :, :, :, :, pl.ds(first, CHUNK)], g_sem.at[i // 3, i % 3]
            )
        )
        outs[-1].start()
    run(FFN_LAST)
    for copy in outs:
        copy.wait()


def ffn(n_sp, x, att, out_w, gain, cot, width, early, kept):
    tok, dim = x.shape
    values = att.shape[1]
    n_z = n_sp // 2
    chunks = -(-width // CHUNK)
    gather_units = units_of(width)
    sums = reduce_units(chunks)
    rows = dim // n_sp // GROUP
    spans = [3 * CHUNK * (last - first) for first, last in sums]
    vmem, anywhere = pl.BlockSpec(memory_space=pltpu.VMEM), pl.BlockSpec(memory_space=pl.ANY)
    shape = jax.ShapeDtypeStruct
    split = lambda w: shape((n_z, 2, 2, 2, rows, w), BF16)
    sems = len(kept) * n_copies(n_z) + IN_FFN * n_reduce(n_z)
    full_shapes = tuple(shape((k.shape[0] * n_sp, k.shape[1]), BF16) for k in kept)
    result = pl.pallas_call(
        functools.partial(ffn_kernel, n_sp, gather_units, chunks),
        out_shape=(shape((8, dim), F32),)
        + tuple(shape((2, 2, rows, w), BF16) for w in spans[:IN_FFN])
        + (shape((tok, dim), BF16), shape((tok, dim), F32), shape((tok, values), BF16), split(values))
        + tuple(split(w) for w in spans[IN_FFN:])
        + full_shapes,
        in_specs=[vmem] * 5 + [anywhere] * len(early) + [vmem] * len(kept),
        out_specs=(vmem,) * (1 + IN_FFN) + (anywhere,) * (4 + len(spans) - IN_FFN + len(kept)),
        scratch_shapes=[pltpu.VMEM((n_z, 2, 2, 2, rows, w), BF16) for w in spans[:IN_FFN]]
        + [pltpu.VMEM((n_z, 2, 2, rows, w), BF16) for w in spans[:IN_FFN]]
        + sum([reduce_scratch(n_z, rows, w) for w in spans[:IN_FFN]], [])
        + [
            pltpu.VMEM((tok, dim), F32),
            pltpu.VMEM((tok, dim), BF16),
            pltpu.VMEM((dim, tok), BF16),
            pltpu.VMEM((dim, tok), BF16),
            pltpu.VMEM((tok, dim), F32),
            pltpu.VMEM((tok, dim), F32),
            pltpu.VMEM((2, 3, dim, CHUNK), BF16),
            pltpu.VMEM((2, 3, n_z, 2, 2, 2, rows, CHUNK), BF16),
            pltpu.SemaphoreType.DMA((sems,)),
            pltpu.SemaphoreType.DMA((sems,)),
            pltpu.SemaphoreType.DMA((2, 3)),
            pltpu.SemaphoreType.DMA((2, 3)),
            pltpu.SemaphoreType.DMA((4,)),
        ],
        compiler_params=pltpu.CompilerParams(
            collective_id=2, has_side_effects=True, vmem_limit_bytes=63 << 20
        ),
        name="ffn",
    )(x, att, out_w, gain, cot, *early, *kept)
    n = 1 + IN_FFN
    shards = shards_of(result[1:n])
    output, g_hidden, g_att, g_out = result[n : n + 4]
    grads = result[n + 4 : n + 4 + len(spans) - IN_FFN]
    return output, g_hidden, g_att, result[0], g_out, shards, grads


def tail_kernel(
    n_sp, normed_ref, gq_ref, gk_ref, gv_ref, gain_ref, ggain_ref, w_hbm, x_hbm, gh_hbm, gains_ref, *rest,
):
    finals, rest = rest[:3], rest[3:]
    gin_ref, rest = rest[0], rest[1:]
    sources, rest = rest[:3], rest[3:]
    swaps, rest = rest[:3], rest[3:]
    buffers, rest = [rest[4 * i : 4 * i + 4] for i in range(3)], rest[12:]
    w_ref, x_ref, gh_ref, own_gains, sum_gains, in_sp, in_dp, send_sem, recv_sem, local_sem = rest
    tok, dim = x_ref.shape
    n_z = n_sp // 2
    lanes = gq_ref.shape[1]
    where = place(n_sp)
    dp, sp, g, gy, gx, z, c, across_x, across_y, diagonal, partner = where
    loads = [
        pltpu.make_async_copy(src, dst, local_sem.at[i])
        for i, (src, dst) in enumerate(((w_hbm, w_ref), (x_hbm, x_ref), (gh_hbm, gh_ref)))
    ]
    for copy in loads:
        copy.start()
    copies = Copies(send_sem, recv_sem)
    reduces = [Reduce(copies, k, n_z, where, sources[k], swaps[k], buffers[k], finals[k]) for k in range(3)]
    others = [(dp, lax.rem(sp + i, n_sp)) for i in range(1, n_sp)]
    groups = [across_x, across_y, diagonal]
    for i, device in enumerate(others):
        copies.add(("sp", i), own_gains, in_sp.at[i], device)
    for i, device in enumerate(groups):
        copies.add(("dp", i), sum_gains, in_dp.at[i], device)
    meet(others + groups)
    block = sources[0].shape[:-1] + (BLK,)
    half = gv_ref.shape[1] // 2
    pieces = [
        [(gv_ref, i) for i in range(0, half, BLK)],
        [(gv_ref, i) for i in range(half, 2 * half, BLK)],
        [(ref, i) for ref in (gq_ref, gk_ref) for i in range(0, lanes, BLK)],
    ]
    for k, piece in enumerate(pieces):
        for j, (ref, i) in enumerate(piece):
            sources[k][:, :, :, :, :, j * BLK : (j + 1) * BLK] = (
                mm(normed_ref[...], ref[:, i : i + BLK], TN).astype(BF16).reshape(block)
            )
            if j == 0 and k > 0:
                reduces[k - 1].stage(0)
    for copy in loads:
        copy.wait()
    todo = [[(2, 0), (0, 1)], [(1, 1)], [(0, 2), (2, 1)], [(1, 2)]]
    total = jnp.zeros((1, dim), F32)
    gain = gain_ref[0:1]
    saves = []
    for i in range(tok // BLK):
        rows = slice(i * BLK, (i + 1) * BLK)
        e = (
            mm(gq_ref[rows, :], w_ref[:, 0:lanes], NT)
            + mm(gk_ref[rows, :], w_ref[:, lanes : 2 * lanes], NT)
            + mm(gv_ref[rows, :], w_ref[:, 2 * lanes :], NT)
        )
        u = x_ref[rows, :].astype(F32)
        scale = lax.rsqrt(jnp.mean(u * u, axis=1, keepdims=True) + EPSILON)
        total = total + jnp.sum(e * u * scale, axis=0, keepdims=True)
        eg = e * gain
        inner = jnp.mean(eg * u, axis=1, keepdims=True)
        gh_ref[rows, :] = gh_ref[rows, :] + scale * eg - u * (scale * scale * scale * inner)
        for k, n in todo[i] if i < len(todo) else ():
            reduces[k].stage(n)
    for i in range(tok // BLK, len(todo)):
        for k, n in todo[i]:
            reduces[k].stage(n)
    save = pltpu.make_async_copy(gh_ref, gin_ref, local_sem.at[0])
    save.start()
    row = lax.broadcasted_iota(jnp.int32, own_gains.shape, 0)
    own_gains[...] = jnp.where(row == 0, jnp.broadcast_to(total, own_gains.shape), ggain_ref[...])
    reduces[0].stage(3)
    reduces[2].stage(2)
    copies.start(*[("sp", i) for i in range(n_sp - 1)])
    reduces[1].stage(3)
    reduces[0].stage(4)
    reduces[2].stage(3)
    copies.arrived(*[("sp", i) for i in range(n_sp - 1)])
    sum_gains[...] = own_gains[...] + rows_sum([in_sp[i] for i in range(n_sp - 1)])
    reduces[1].stage(4)
    copies.start(*[("dp", i) for i in range(3)])
    reduces[2].stage(4)
    copies.arrived(*[("dp", i) for i in range(3)])
    gains_ref[...] = sum_gains[...] + rows_sum([in_dp[i] for i in range(3)])
    for reduce in reduces:
        reduce.stage(5)
    copies.sent(*[("sp", i) for i in range(n_sp - 1)], *[("dp", i) for i in range(3)])
    save.wait()


def tail(n_sp, normed, gq, gk, gv, w_joint, x, g_hidden, gain, ggain):
    tok, dim = x.shape
    lanes, values = gq.shape[1], gv.shape[1]
    n_z = n_sp // 2
    rows = dim // n_sp // GROUP
    vmem, anywhere = pl.BlockSpec(memory_space=pltpu.VMEM), pl.BlockSpec(memory_space=pl.ANY)
    shape = jax.ShapeDtypeStruct
    widths = (values // 2, values // 2, 2 * lanes)
    sems = 3 * n_reduce(n_z) + n_sp + 2
    return pl.pallas_call(
        functools.partial(tail_kernel, n_sp),
        out_shape=(shape((8, dim), F32),)
        + tuple(shape((2, 2, rows, w), BF16) for w in widths)
        + (shape((tok, dim), F32),),
        in_specs=[vmem] * 6 + [anywhere] * 3,
        out_specs=(vmem,) * 4 + (anywhere,),
        scratch_shapes=[pltpu.VMEM((n_z, 2, 2, 2, rows, w), BF16) for w in widths]
        + [pltpu.VMEM((n_z, 2, 2, rows, w), BF16) for w in widths]
        + sum([reduce_scratch(n_z, rows, w) for w in widths], [])
        + [
            pltpu.VMEM(w_joint.shape, BF16),
            pltpu.VMEM(x.shape, BF16),
            pltpu.VMEM((tok, dim), F32),
            pltpu.VMEM((8, dim), F32),
            pltpu.VMEM((8, dim), F32),
            pltpu.VMEM((n_sp - 1, 8, dim), F32),
            pltpu.VMEM((3, 8, dim), F32),
            pltpu.SemaphoreType.DMA((sems,)),
            pltpu.SemaphoreType.DMA((sems,)),
            pltpu.SemaphoreType.DMA((3,)),
        ],
        compiler_params=pltpu.CompilerParams(
            collective_id=3, has_side_effects=True, vmem_limit_bytes=63 << 20
        ),
        name="tail",
    )(normed, gq, gk, gv, gain, ggain, w_joint, x, g_hidden)


def finish_kernel(sums, *refs):
    n = len(sums) + 4
    sources, refs = refs[:n], refs[n:]
    (q_out, k_out, v_out, out_out, gate_out, up_out, down_out), refs = refs[:7], refs[7:]
    held, sem = refs[:n], refs[n]
    copies = [pltpu.make_async_copy(src, dst, sem.at[i]) for i, (src, dst) in enumerate(zip(sources, held))]
    for copy in copies:
        copy.start()
    for copy in copies:
        copy.wait()
    qk_ref, va_ref, vb_ref, out_ref, units = held[0], held[1], held[2], held[3], held[4:]
    lanes = q_out.shape[1]
    width = gate_out.shape[0]
    q_out[...] = qk_ref[:, :lanes].astype(F32)
    k_out[...] = qk_ref[:, lanes:].astype(F32)
    v_out[:, : va_ref.shape[1]] = va_ref[...].astype(F32)
    v_out[:, va_ref.shape[1] :] = vb_ref[...].astype(F32)
    out_out[...] = out_ref[...].astype(F32).T
    for unit, (first, last) in zip(units, sums):
        lo, hi = first * CHUNK, min(last * CHUNK, width)
        span = (last - first) * CHUNK
        for i, out in enumerate((gate_out, up_out, down_out)):
            out[lo:hi, :] = unit[:, i * span : i * span + hi - lo].astype(F32).T


def finish(width, lanes, qk, va, vb, out, units):
    shard = va.shape[0]
    vmem, anywhere = pl.BlockSpec(memory_space=pltpu.VMEM), pl.BlockSpec(memory_space=pl.ANY)
    shape = jax.ShapeDtypeStruct
    arrays = (qk, va, vb, out, *units)
    return pl.pallas_call(
        functools.partial(finish_kernel, reduce_units(-(-width // CHUNK))),
        out_shape=(
            shape((shard, lanes), F32), shape((shard, lanes), F32), shape((shard, 2 * va.shape[1]), F32),
            shape(out.shape[::-1], F32), shape((width, shard), F32), shape((width, shard), F32),
            shape((width, shard), F32),
        ),
        in_specs=[anywhere] * len(arrays),
        out_specs=(vmem,) * 7,
        scratch_shapes=[pltpu.VMEM(a.shape, BF16) for a in arrays] + [pltpu.SemaphoreType.DMA((len(arrays),))],
        compiler_params=pltpu.CompilerParams(vmem_limit_bytes=63 << 20),
        name="finish",
    )(*arrays)


def body(
    tokens, doc_ids, gain_attn, w_query, w_key, w_value, w_out, gain_mlp, w_gate, w_up, w_down, cotangent
):
    n_sp = lax.axis_size("sp")
    me = lax.axis_index("sp")
    tok = tokens.shape[0]
    heads = w_query.shape[1] // FEAT
    table = feature_table()
    docs = doc_ids
    width = gain_attn.shape[0]
    lanes = heads * FEAT
    hidden_units = w_gate.shape[1]
    parts = [part[None, :] for part in (gain_attn, gain_mlp)]
    if width % 128:
        parts = [jnp.tile(part, (1, n_sp)) for part in parts]
    (
        (att, inv, prior_state, gain, q, k, v, normed_one, w_joint), out_t, early, kept
    ) = forward(
        n_sp, tokens, *parts, docs, table, w_out, w_gate.T, w_up.T, w_down, w_query, w_key, w_value
    )
    output, g_hidden, g_att, grad_gain_two, g_out, shards, grads = ffn(
        n_sp, tokens, att, out_t, gain, cotangent, hidden_units, early, kept
    )
    (gq, gk, gv), (s_out, *more) = backward(
        n_sp, (q, k, v, g_att, att, inv, prior_state, docs, table), (g_out, *grads)
    )
    grad_gains, *joint, grad_input = tail(
        n_sp, normed_one, gq, gk, gv, w_joint, tokens, g_hidden, gain, grad_gain_two
    )
    n_dp = lax.axis_size("dp")

    def over_groups(shard):
        if n_dp > GROUP:
            shard = lax.psum(shard, "dp") * jnp.asarray(GROUP / n_dp, shard.dtype)
        return shard

    s_va, s_vb, s_query_key = shards_of(joint)
    g_query, g_key, g_value, g_w_out, g_gate, g_up, g_down = finish(
        hidden_units, lanes, over_groups(s_query_key), over_groups(s_va), over_groups(s_vb), over_groups(s_out),
        [over_groups(shard) for shard in (*shards, *more)],
    )
    s_gains = over_groups(lax.dynamic_slice(grad_gains, (0, me * width), (2, width)))
    return (
        output, grad_input, s_gains[0], g_query, g_key, g_value, g_w_out, s_gains[1], g_gate.T, g_up.T, g_down
    )


def solution(mesh):
    placed_in = (
        P(("dp", "sp"), None), P("dp", None), P("sp"), P("sp", None), P("sp", None), P("sp", None),
        P(None, "sp"), P("sp"), P("sp", None), P("sp", None), P(None, "sp"), P(("dp", "sp"), None),
    )
    return jax.shard_map(
        body,
        mesh=mesh,
        in_specs=placed_in,
        out_specs=(
            P(("dp", "sp"), None), P(("dp", "sp"), None), P("sp"), P("sp", None), P("sp", None),
            P("sp", None), P(None, "sp"), P("sp"), P("sp", None), P("sp", None), P(None, "sp"),
        ),
        check_vma=False,
    )
```

```python
import functools
import math

import jax
import jax.numpy as jnp
import numpy as np
from jax import lax
from jax.experimental import pallas as pl
from jax.experimental.pallas import tpu as pltpu
from jax.sharding import PartitionSpec as P

FEAT = 16
HEAD_V = 64
EPSILON = 1e-05
BF16 = jnp.bfloat16
F32 = jnp.float32
BLK = 256
PAD_F = 256
ROWS_S = 80
NN = (((1,), (0,)), ((), ()))
NT = (((1,), (1,)), ((), ()))
TN = (((0,), (0,)), ((), ()))


def mm(a, b, dims=NN):
    return lax.dot_general(a, b, dims, preferred_element_type=F32)


def feature_table():
    rows = []
    for a in range(FEAT):
        for b in range(a, FEAT):
            rows.append((a, b, 0.0, 0.0, 1.0 if a == b else 2.0))
    for a in range(FEAT):
        rows.append((a, -1, 0.0, 1.0, 8.0))
    rows.append((-1, -1, 1.0, 1.0, 32.0))
    while len(rows) < PAD_F:
        rows.append((-1, -1, 0.0, 0.0, 0.0))
    table = np.zeros((8, PAD_F), np.float32)
    table[:5] = np.array(rows, np.float32).T
    return jnp.asarray(table)


def selectors(table, head, lanes):
    row = lax.broadcasted_iota(jnp.int32, (lanes, PAD_F), 0).astype(F32)
    base = (head * FEAT).astype(F32)
    first = jnp.where((row == table[0:1] + base) & (table[0:1] >= 0), 1.0, 0.0).astype(BF16)
    second = jnp.where((row == table[1:2] + base) & (table[1:2] >= 0), 1.0, 0.0).astype(BF16)
    return first, second


def head_lanes(values, head, scale=1):
    lane = lax.broadcasted_iota(jnp.int32, values.shape, 1)
    return jnp.where(lane // FEAT == head, values * scale, jnp.zeros_like(values))


def factors(values, sel, table):
    one = mm(values, sel[0]) + table[2:3]
    two = mm(values, sel[1]) + table[3:4]
    return one, two


def with_ones(v_pair):
    return jnp.concatenate([v_pair, jnp.ones_like(v_pair)], axis=1)


class Copies:
    def __init__(self, send_sem, recv_sem):
        self.send_sem, self.recv_sem, self.made = send_sem, recv_sem, {}

    def add(self, name, src, dst, device):
        self.made[name] = (src, dst, len(self.made), device)

    def get(self, name):
        src, dst, index, device = self.made[name]
        return pltpu.make_async_remote_copy(
            src_ref=src,
            dst_ref=dst,
            send_sem=self.send_sem.at[index],
            recv_sem=self.recv_sem.at[index],
            device_id=device,
            device_id_type=pl.DeviceIdType.MESH,
        )

    def start(self, *names):
        for name in names:
            self.get(name).start()

    def arrived(self, *names):
        for name in names:
            self.get(name).wait_recv()

    def sent(self, *names):
        for name in names:
            self.get(name).wait_send()


GROUP = 4


def place(n_sp):
    dp, sp = lax.axis_index("dp"), lax.axis_index("sp")
    g = lax.rem(dp, GROUP)
    gy, gx = g // 2, lax.rem(g, 2)
    z, c = sp // 2, lax.rem(sp, 2)
    across_x = (dp - g + gy * 2 + (1 - gx), sp)
    across_y = (dp - g + (1 - gy) * 2 + gx, sp)
    diagonal = (dp - g + (1 - gy) * 2 + (1 - gx), sp)
    partner = (dp, z * 2 + (1 - c))
    return dp, sp, g, gy, gx, z, c, across_x, across_y, diagonal, partner


class Gather:
    def __init__(self, copies, tag, n_z, own, full, where):
        dp, sp, g, gy, gx, z, c, across_x, across_y, _, partner = where
        self.copies, self.tag, self.n_z = copies, tag, n_z
        shard, width = own.shape
        quarter = shard // GROUP
        lower, upper = pl.ds(0, width // 2), pl.ds(width // 2, width // 2)

        def rows(zz, gg, count, lanes=None):
            start = pl.multiple_of((zz * 2 + c) * shard + gg * quarter, 16)
            return full.at[pl.ds(start, count)] if lanes is None else full.at[pl.ds(start, count), lanes]

        gx_of, gy_of = gy * 2 + (1 - gx), (1 - gy) * 2 + gx
        diag = (1 - gy) * 2 + (1 - gx)
        add = lambda name, src, dst, device: copies.add((tag, name), src, dst, device)
        mine = own.at[pl.ds(pl.multiple_of(g * quarter, 16), quarter)]
        self.own_place = rows(z, 0, shard)
        add("c0", own, self.own_place, partner)
        for i in range(1, n_z):
            zt = lax.rem(z + i, n_z)
            zs = lax.rem(z + n_z - i, n_z)
            add(f"z{i}", mine, rows(z, g, quarter), (dp, zt * 2 + c))
            here = rows(zs, g, quarter)
            add(f"x{i}", here, here, across_x)
            add(f"y{i}", here, here, across_y)
            add(f"c1{i}", here, here, partner)
            first = rows(zs, gx_of, quarter, lower)
            add(f"d0{i}", first, first, across_y)
            second = rows(zs, gy_of, quarter, upper)
            add(f"d1{i}", second, second, across_x)
            for name, gg in (("c2", gx_of), ("c3", gy_of), ("c4", diag)):
                there = rows(zs, gg, quarter)
                add(f"{name}{i}", there, there, partner)

    def each(self, *names):
        return [(self.tag, f"{name}{i}") for i in range(1, self.n_z) for name in names]

    def stage(self, n):
        copies = self.copies
        if n == 0:
            copies.start(*self.each("z"), (self.tag, "c0"))
        elif n == 1:
            for i in range(1, self.n_z):
                copies.arrived((self.tag, f"z{i}"))
                copies.start(*[(self.tag, f"{name}{i}") for name in ("x", "y", "c1")])
        elif n == 2:
            for i in range(1, self.n_z):
                copies.arrived((self.tag, f"x{i}"), (self.tag, f"y{i}"))
                copies.start(*[(self.tag, f"{name}{i}") for name in ("d0", "d1", "c2", "c3")])
        elif n == 3:
            for i in range(1, self.n_z):
                copies.arrived((self.tag, f"d0{i}"), (self.tag, f"d1{i}"))
                copies.start((self.tag, f"c4{i}"))
        else:
            copies.arrived((self.tag, "c0"), *self.each("c1", "c2", "c3", "c4"))
            copies.sent((self.tag, "c0"), *self.each("z", "x", "y", "c1", "d0", "d1", "c2", "c3", "c4"))


def n_copies(n_z):
    return 1 + 9 * (n_z - 1)


def meet(devices):
    barrier = pltpu.get_barrier_semaphore()
    for device in devices:
        pl.semaphore_signal(barrier, inc=1, device_id=device, device_id_type=pl.DeviceIdType.MESH)
    pl.semaphore_wait(barrier, len(devices))


def placed(state, side, z_rows):
    zero = jnp.zeros((64, PAD_F), state.dtype)
    values = [state[0:64], zero] if side == 0 else [zero, state[0:64]]
    return jnp.concatenate(values + [z_rows], axis=0)


class Reduce:
    def __init__(self, copies, tag, n_z, where, source, swapped, buffers, final, stage_buf=None, local_sem=None):
        dp, sp, g, gy, gx, z, c, across_x, across_y, diagonal, partner = where
        self.copies, self.tag, self.n_z = copies, tag, n_z
        self.gy, self.gx, self.z, self.c = gy, gx, z, c
        self.source, self.swapped, self.final = source, swapped, final
        self.work, self.first, self.second, self.along = buffers
        self.stage_buf, self.local_sem = stage_buf, local_sem
        work = self.work
        half = work.shape[-1] // 2
        self.halves = (pl.ds(0, half), pl.ds(half, half))
        lower, upper = self.halves
        everything = slice(None)
        add = lambda name, src, dst, device: copies.add((tag, name), src, dst, device)
        add("s", source.at[:, 1 - c], swapped, partner)
        add("a1", work.at[:, :, 1 - gx, everything, lower], self.first.at[0], across_x)
        add("b1", work.at[:, 1 - gy, :, everything, upper], self.first.at[1], across_y)
        add("a2", work.at[:, 1 - gy, gx, everything, lower], self.second.at[0], across_y)
        add("b2", work.at[:, gy, 1 - gx, everything, upper], self.second.at[1], across_x)
        for i in range(1, n_z):
            zt = lax.rem(z + i, n_z)
            add(f"z{i}", work.at[zt, gy, gx], self.along.at[i - 1], (dp, zt * 2 + c))
        for name, device in (("fx", across_x), ("fy", across_y), ("fd", diagonal)):
            add(name, final.at[gy, gx], final.at[gy, gx], device)

    def names(self, *names):
        return [(self.tag, name) for name in names]

    def load(self, zz):
        slot = zz % 2
        return (
            pltpu.make_async_copy(self.source.at[zz, self.c], self.stage_buf.at[slot, 0], self.local_sem.at[slot, 0]),
            pltpu.make_async_copy(self.swapped.at[zz], self.stage_buf.at[slot, 1], self.local_sem.at[slot, 1]),
        )

    def stage(self, n):
        copies, work, gy, gx, n_z = self.copies, self.work, self.gy, self.gx, self.n_z
        zs = ["z%d" % i for i in range(1, n_z)]
        lower, upper = self.halves
        if n == 0:
            copies.start(*self.names("s"))
        elif n == 1:
            copies.arrived(*self.names("s"))
            if self.stage_buf is None:

                def add_held(i, carry):
                    zz, yy, xx = i // 4, lax.rem(i // 2, 2), lax.rem(i, 2)
                    work[zz, yy, xx] = self.source[zz, self.c, yy, xx] + self.swapped[zz, yy, xx]
                    return carry

                lax.fori_loop(0, 4 * n_z, add_held, 0)
                copies.start(*self.names("a1", "b1"))
                return
            for copy in self.load(0):
                copy.start()
            for zz in range(n_z):
                if zz + 1 < n_z:
                    for copy in self.load(zz + 1):
                        copy.start()
                for copy in self.load(zz):
                    copy.wait()
                slot = zz % 2

                def add_quarter(i, carry):
                    yy, xx = i // 2, lax.rem(i, 2)
                    work[zz, yy, xx] = self.stage_buf[slot, 0, yy, xx] + self.stage_buf[slot, 1, yy, xx]
                    return carry

                lax.fori_loop(0, 4, add_quarter, 0)
            copies.start(*self.names("a1", "b1"))
        elif n == 2:
            copies.arrived(*self.names("a1"))

            def add_a(i, carry):
                zz, yy = i // 2, lax.rem(i, 2)
                work[zz, yy, gx, :, lower] = work[zz, yy, gx, :, lower] + self.first[0, zz, yy]
                return carry

            lax.fori_loop(0, 2 * n_z, add_a, 0)
            copies.start(*self.names("a2"))
            copies.arrived(*self.names("b1"))

            def add_b(i, carry):
                zz, xx = i // 2, lax.rem(i, 2)
                work[zz, gy, xx, :, upper] = work[zz, gy, xx, :, upper] + self.first[1, zz, xx]
                return carry

            lax.fori_loop(0, 2 * n_z, add_b, 0)
            copies.start(*self.names("b2"))
        elif n == 3:
            copies.arrived(*self.names("a2", "b2"))

            def add_c(zz, carry):
                work[zz, gy, gx, :, lower] = work[zz, gy, gx, :, lower] + self.second[0, zz]
                work[zz, gy, gx, :, upper] = work[zz, gy, gx, :, upper] + self.second[1, zz]
                return carry

            lax.fori_loop(0, n_z, add_c, 0)
            copies.start(*self.names(*zs))
        elif n == 4:
            copies.arrived(*self.names(*zs))
            total = work[self.z, gy, gx].astype(F32)
            for i in range(n_z - 1):
                total = total + self.along[i].astype(F32)
            self.final[gy, gx] = total.astype(BF16)
            copies.start(*self.names("fx", "fy", "fd"))
        else:
            copies.arrived(*self.names("fx", "fy", "fd"))
            copies.sent(*self.names("s", "a1", "b1", "a2", "b2", "fx", "fy", "fd", *zs))


def reduce_scratch(n_z, rows, width):
    return [
        pltpu.VMEM((n_z, 2, 2, rows, width), BF16),
        pltpu.VMEM((2, n_z, 2, rows, width // 2), BF16),
        pltpu.VMEM((2, n_z, rows, width // 2), BF16),
        pltpu.VMEM((n_z - 1, rows, width), BF16),
    ]


def n_reduce(n_z):
    return 8 + n_z - 1


TAIL_LANES = 32
PER_TILE = 128 // TAIL_LANES


def packed_shape(heads):
    return (heads + heads // PER_TILE, ROWS_S, 128)


def pack(ref, heads, p, side, state):
    head = p * 2 + side
    block = heads + head // PER_TILE
    ref[head] = state[:, :128].astype(BF16)
    rest = state[:, 128:]
    first, second = [pltpu.roll(rest, TAIL_LANES * (side + 2 * half), 1) if side + 2 * half else rest for half in range(2)]
    moved = jnp.where(lax.rem(p, 2) == 0, first, second).astype(BF16)
    if side == 0:
        held = jnp.where(lax.rem(p, 2) == 0, jnp.zeros_like(moved), ref[block])
        ref[block] = held + moved
    else:
        ref[block] = ref[block] + moved


class Chain:
    def __init__(self, copies, where, n_z, onward, own, mate, carry, out, pass_lead, pass_other):
        dp, sp, g, gy, gx, z, c, across_x, across_y, diagonal, partner = where
        lead = 1 if onward else 0
        self.copies, self.n_z = copies, n_z
        self.own, self.mate, self.carry, self.out = own, mate, carry, out
        self.pass_lead, self.pass_other = pass_lead, pass_other
        self.leads = c == lead
        self.place = z if onward else n_z - 1 - z
        to = lax.rem(z + 1, n_z) if onward else lax.rem(z + n_z - 1, n_z)
        before = lax.rem(z + n_z - 1, n_z) if onward else lax.rem(z + 1, n_z)
        self.next_device, self.last_device = (dp, to * 2 + c), (dp, before * 2 + c)
        copies.add("own", own, mate, partner)
        copies.add("raw", carry, carry, partner)
        copies.add("carry", out, carry, self.next_device)

    def begin(self):
        @pl.when(jnp.logical_not(self.leads))
        def _():
            self.copies.start("own")

        @pl.when(self.leads & (self.place == 0))
        def _():
            self.carry[...] = jnp.zeros_like(self.carry)

    def middle(self, now):
        now = now & self.leads

        @pl.when(now)
        def _():
            self.copies.arrived("own")

        @pl.when(now & (self.place > 0))
        def _():
            self.copies.arrived("carry")

        @pl.when(now)
        def _():
            self.copies.start("raw")

        @pl.when(now & (self.place < self.n_z - 1))
        def _():
            def one(head, carry):
                inner = self.mate[head].astype(F32) + self.pass_other * self.carry[head].astype(F32)
                self.out[head] = (self.own[head].astype(F32) + self.pass_lead * inner).astype(BF16)
                return carry

            lax.fori_loop(0, self.own.shape[0], one, 0)
            self.copies.start("carry")

    def finish(self, result, weights):
        heads = result.shape[0]

        def unpack(value):
            def group(q, carry):
                rest = value(heads + q)
                for j in range(PER_TILE):
                    head = q * PER_TILE + j
                    tail = pltpu.roll(rest, 128 - TAIL_LANES * j, 1) if j else rest
                    result[head] = jnp.concatenate(
                        [value(head) * weights[:, :128], tail * weights[:, 128:]], axis=1
                    ).astype(BF16)
                return carry

            lax.fori_loop(0, heads // PER_TILE, group, 0)

        @pl.when(jnp.logical_not(self.leads))
        def _():
            self.copies.arrived("raw")
            unpack(lambda i: self.carry[i].astype(F32))

        @pl.when(self.leads)
        def _():
            unpack(lambda i: self.mate[i].astype(F32) + self.pass_other * self.carry[i].astype(F32))

    def drain(self):
        @pl.when(jnp.logical_not(self.leads))
        def _():
            self.copies.sent("own")

        @pl.when(self.leads)
        def _():
            self.copies.sent("raw")

        @pl.when(self.leads & (self.place < self.n_z - 1))
        def _():
            self.copies.sent("carry")


class Documents:
    def __init__(self, doc_ref, sp, n_sp):
        self.ref, self.n_sp, self.tok = doc_ref, n_sp, doc_ref.shape[1] // n_sp
        self.row = self.of(sp)
        self.column = jnp.broadcast_to(self.row, (128, self.tok)).T[:, 0:1]

    def of(self, sp):
        return self.ref[:, pl.ds(pl.multiple_of(sp * self.tok, 128), self.tok)].astype(F32)

    def last(self, sp):
        value = self.of(jnp.maximum(sp, 0))[:, self.tok - 1 : self.tok]
        return jnp.where(sp >= 0, value, -1.0)

    def first(self, sp):
        value = self.of(jnp.minimum(sp, self.n_sp - 1))[:, 0:1]
        return jnp.where(sp < self.n_sp, value, -2.0)

    def through(self, here, there):
        return jnp.broadcast_to(jnp.where(here == there, 1.0, 0.0), (1, 128))


def rows_sum(values):
    total = values[0]
    for value in values[1:]:
        total = total + value
    return total


STRIP = 512
CHAIN_STEPS = 3
CHAIN_BACK_STEPS = 5
CHUNK = 256
UNITS = 4
EARLY = 2


def units_of(width):
    chunks = -(-width // CHUNK)
    step = -(-chunks // UNITS)
    return [(first, min(chunks, first + step)) for first in range(0, chunks, step)]


def forward_kernel(
    n_sp, x_ref, gain_a_ref, gain_m_ref, doc_ref, table_ref, wo_ref, wg_ref, wu_ref, wd_ref, wq_ref, wk_ref, wv_ref, *rest,
):
    n_unit = len(units_of(wd_ref.shape[0]))
    (att_ref, inv_ref, state_ref, gain_ref, q_ref, k_ref, v_ref, normed_ref, w_joint_ref), rest = rest[:9], rest[9:]
    fulls, rest = rest[: 3 + EARLY], rest[3 + EARLY :]
    kept, rest = rest[: n_unit - EARLY], rest[n_unit - EARLY :]
    (joint_own, more_own, out_own), rest = rest[:3], rest[3:]
    ffn_own, rest = rest[:n_unit], rest[n_unit:]
    (
        mask_ref, joint_vm, num_ref, den_ref, own_state, mate_state, in_state, out_state, gains_ref, gains_in,
        prior_ref, q_scr, k_scr, v_scr, normed_scr, normed_t, send_sem, recv_sem, local_sem,
    ) = rest
    tok = x_ref.shape[0]
    n_z = n_sp // 2
    lanes = q_ref.shape[1]
    pairs = v_ref.shape[1] // 128
    where = place(n_sp)
    dp, sp, g, gy, gx, z, c, across_x, across_y, diagonal, partner = where
    copies = Copies(send_sem, recv_sem)
    joint_full, more_full = fulls[:2]
    owns = (joint_own, more_own, out_own) + tuple(ffn_own[:EARLY])
    gathers = [Gather(copies, k, n_z, own, full, where) for k, (own, full) in enumerate(zip(owns, fulls))]
    others = [(dp, lax.rem(sp + i, n_sp)) for i in range(1, n_sp)]
    for i, device in enumerate(others, 1):
        copies.add(("gain", i), gains_ref, gains_in.at[i - 1], device)
    docs = Documents(doc_ref, sp, n_sp)
    even = sp - c
    chain = Chain(
        copies, where, n_z, True, own_state, mate_state, in_state, out_state,
        docs.through(docs.last(even + 1), docs.last(even)), docs.through(docs.last(even), docs.last(even - 1)),
    )
    part_lane = lax.broadcasted_iota(jnp.int32, gains_ref.shape, 1)
    part = jnp.concatenate([jnp.broadcast_to(gain_a_ref[...], (4, gain_a_ref.shape[1])),
                            jnp.broadcast_to(gain_m_ref[...], (4, gain_m_ref.shape[1]))], axis=0).astype(F32)
    if part.shape[1] < gains_ref.shape[1]:
        part = jnp.concatenate([part] * n_sp, axis=1)
    gains_ref[...] = jnp.where(part_lane // (gains_ref.shape[1] // n_sp) == sp, part, 0.0)
    assembled = [
        pltpu.make_async_copy(wq_ref, joint_own.at[:, 0:lanes], local_sem.at[0]),
        pltpu.make_async_copy(wk_ref, joint_own.at[:, lanes : 2 * lanes], local_sem.at[1]),
        pltpu.make_async_copy(
            wv_ref.at[:, 0 : joint_own.shape[1] - 2 * lanes], joint_own.at[:, 2 * lanes :], local_sem.at[2]
        ),
        pltpu.make_async_copy(wv_ref.at[:, joint_own.shape[1] - 2 * lanes :], more_own, local_sem.at[3]),
    ]
    for copy in assembled:
        copy.start()
    meet(others + [across_x, across_y])
    copies.start(*[("gain", i) for i in range(1, n_sp)])
    for copy in assembled:
        copy.wait()
    gathers[0].stage(0)
    gathers[1].stage(0)
    out_own[...] = wo_ref[...].T
    width = wd_ref.shape[0]
    for own, (first, last) in zip(ffn_own, units_of(width)):
        lo, hi = first * CHUNK, min(last * CHUNK, width)
        span = (last - first) * CHUNK
        for i, piece in enumerate((wg_ref[lo:hi, :].T, wu_ref[lo:hi, :].T, wd_ref[lo:hi, :].T)):
            if hi - lo < span:
                own[:, (i + 1) * span - CHUNK : (i + 1) * span] = jnp.zeros((own.shape[0], CHUNK), BF16)
            own[:, i * span : i * span + hi - lo] = piece

    table = table_ref[...]
    row = lax.broadcasted_iota(jnp.int32, (tok, tok), 0)
    col = lax.broadcasted_iota(jnp.int32, (tok, tok), 1)
    mask_ref[...] = jnp.where((row >= col) & (docs.column == docs.row), 1.0, 0.0)
    prior_ref[...] = jnp.broadcast_to(jnp.where(docs.column == docs.last(sp - 1), 1.0, 0.0), prior_ref.shape)
    copies.arrived(*[("gain", i) for i in range(1, n_sp)])
    gain_ref[...] = gains_ref[...] + rows_sum([gains_in[i] for i in range(n_sp - 1)])
    x = x_ref[...].astype(F32)
    scale = lax.rsqrt(jnp.mean(x * x, axis=1, keepdims=True) + EPSILON)
    normed_scr[...] = (x * scale * gain_ref[0:1]).astype(BF16)
    normed_t[...] = normed_scr[...].T
    local = [
        pltpu.make_async_copy(own, gather.own_place, local_sem.at[k])
        for k, (own, gather) in enumerate(zip(owns, gathers))
    ] + [
        pltpu.make_async_copy(own, keep, local_sem.at[len(owns) + k])
        for k, (own, keep) in enumerate(zip(ffn_own[EARLY:], kept))
    ]
    for copy in local:
        copy.start()
    gathers[0].stage(1)
    gathers[1].stage(1)
    gathers[0].stage(2)
    gathers[2].stage(0)
    gathers[3].stage(0)
    gathers[1].stage(2)
    gathers[0].stage(3)
    gathers[1].stage(3)
    gathers[0].stage(4)
    for copy in local:
        copy.wait()
    split = joint_full.shape[1]
    fetches = [
        pltpu.make_async_copy(joint_full, joint_vm.at[:, 0:split], local_sem.at[0]),
        pltpu.make_async_copy(more_full, joint_vm.at[:, split:], local_sem.at[1]),
    ]
    fetches[0].start()
    fetches[0].wait()
    project = lambda first: mm(normed_scr[...], joint_vm[:, pl.ds(first, BLK)]).astype(BF16)
    for first in range(0, lanes, BLK):
        q_scr[:, first : first + BLK] = project(first)
        k_scr[:, first : first + BLK] = project(lanes + first)

    def values_block(i, carry):
        @pl.when(i == (split - 2 * lanes) // BLK)
        def _():
            gathers[1].stage(4)
            fetches[1].start()
            fetches[1].wait()

        first = pl.multiple_of(i * BLK, BLK)
        v_scr[:, pl.ds(first, BLK)] = project(2 * lanes + first)
        return carry

    lax.fori_loop(0, v_scr.shape[1] // BLK, values_block, 0)
    saves = [
        pltpu.make_async_copy(src, dst, local_sem.at[i])
        for i, (src, dst) in enumerate(
            ((q_scr, q_ref), (k_scr, k_ref), (v_scr, v_ref), (normed_t, normed_ref), (joint_vm, w_joint_ref))
        )
    ]
    for copy in saves:
        copy.start()

    tail = jnp.where(docs.row == docs.last(sp), 1.0, 0.0)

    def at(p, step, *todo):
        @pl.when(p == step)
        def _():
            for k, n in todo:
                gathers[k].stage(n)

    def state_pair(p, carry):
        at(p, 0, (2, 1))
        at(p, 2, (3, 1), (4, 0))
        at(p, 5, (2, 2))
        columns = pl.ds(pl.multiple_of(p * 128, 128), 128)
        v_t = v_scr[:, columns].astype(F32).T * tail
        ones = jnp.broadcast_to(tail, (16, tail.shape[1]))
        for side in range(2):
            head = p * 2 + side
            sel = selectors(table, head, lanes)
            one, two = factors(k_scr[...], sel, table)
            phi = (one * two).astype(BF16)
            lhs = jnp.concatenate([v_t[side * 64 : side * 64 + 64], ones], axis=0)
            pack(own_state, 2 * pairs, p, side, mm(lhs.astype(BF16), phi))
        return carry

    lax.fori_loop(0, pairs, state_pair, 0)

    chain.begin()
    turn = jnp.minimum(z * CHAIN_STEPS, pairs - 1)

    lane = lax.broadcasted_iota(jnp.int32, (BLK, 128), 1)

    def intra_pair(p, carry):
        at(p, 1, (2, 3), (3, 2))
        at(p, 3, (4, 1))
        at(p, 4, (3, 3))
        at(p, 7, (4, 2))
        chain.middle(p == turn)
        columns = pl.ds(pl.multiple_of(p * 128, 128), 128)
        v_hat = with_ones(v_scr[:, columns])
        heads = [head_lanes(q_scr[...], p * 2 + side) for side in range(2)]
        for i in range(tok // BLK):
            rows = slice(i * BLK, (i + 1) * BLK)
            keys = slice(0, (i + 1) * BLK)
            totals = []
            for side in range(2):
                t = mm(heads[side][rows], k_scr[keys, :], NT) + 4.0
                w = ((t * t + 16.0) * mask_ref[rows, keys]).astype(BF16)
                totals.append(mm(w, v_hat[keys]))
            num_ref[rows, columns] = jnp.where(lane < 64, totals[0][:, :128], totals[1][:, :128])
            den_ref[rows, columns] = jnp.where(lane < 64, totals[0][:, 128:], totals[1][:, 128:])
        return carry

    lax.fori_loop(0, pairs, intra_pair, 0)
    chain.finish(state_ref, table[4:5])
    prior = prior_ref[:, 0:1]
    wide_lane = lax.broadcasted_iota(jnp.int32, (tok, 128), 1)

    def inter_pair(p, carry):
        at(p, 4, (4, 3))
        columns = pl.ds(pl.multiple_of(p * 128, 128), 128)
        totals = []
        for side in range(2):
            head = p * 2 + side
            sel = selectors(table, head, lanes)
            state = state_ref[head]
            z_rows = jnp.broadcast_to(state[64:65].astype(F32), (128, PAD_F)).astype(BF16)
            one, two = factors(q_scr[...], sel, table)
            totals.append(mm((one * two).astype(BF16), placed(state, side, z_rows), NT) * prior)
        num = num_ref[:, columns] + jnp.where(wide_lane < 64, totals[0][:, :128], totals[1][:, :128])
        den = den_ref[:, columns] + jnp.where(wide_lane < 64, totals[0][:, 128:], totals[1][:, 128:])
        inv = 1.0 / den
        inv_ref[:, columns] = inv.astype(BF16)
        att_ref[:, columns] = (num * inv).astype(BF16)
        return carry

    lax.fori_loop(0, pairs, inter_pair, 0)
    for gather in gathers[2:]:
        gather.stage(4)
    for copy in saves:
        copy.wait()
    copies.sent(*[("gain", i) for i in range(1, n_sp)])
    chain.drain()


def forward(n_sp, x, gain_a, gain_m, docs, table, wo, wg, wu, wd, wq, wk, wv):
    tok, dim = x.shape
    lanes, values = wq.shape[1], wv.shape[1]
    heads = lanes // FEAT
    shard = wq.shape[0]
    vmem, anywhere = pl.BlockSpec(memory_space=pltpu.VMEM), pl.BlockSpec(memory_space=pl.ANY)
    n_z = n_sp // 2
    spans = [3 * CHUNK * (last - first) for first, last in units_of(wd.shape[0])]
    joint = 2 * lanes + values
    gathered = [joint // 2, joint // 2, dim] + spans[:EARLY]
    sems = len(gathered) * n_copies(n_z) + n_sp + 2
    shape = jax.ShapeDtypeStruct
    result = pl.pallas_call(
        functools.partial(forward_kernel, n_sp),
        out_shape=(
            shape((tok, values), BF16), shape((tok, values), BF16), shape((heads, ROWS_S, PAD_F), BF16),
            shape((8, dim), F32), shape((tok, lanes), BF16), shape((tok, lanes), BF16),
            shape((tok, values), BF16), shape((dim, tok), BF16), shape((dim, joint), BF16),
        )
        + tuple(shape((shard * n_sp, w), BF16) for w in gathered)
        + tuple(shape((shard, w), BF16) for w in spans[EARLY:]),
        in_specs=[vmem] * 9 + [anywhere] * 3,
        out_specs=(vmem,) * 4 + (anywhere,) * (5 + len(gathered) + len(spans) - EARLY),
        scratch_shapes=[pltpu.VMEM((shard, w), BF16) for w in [joint // 2, joint // 2, dim] + spans]
        + [
            pltpu.VMEM((tok, tok), F32),
            pltpu.VMEM((dim, joint), BF16),
            pltpu.VMEM((tok, values), F32),
            pltpu.VMEM((tok, values), F32),
            pltpu.VMEM(packed_shape(heads), BF16),
            pltpu.VMEM(packed_shape(heads), BF16),
            pltpu.VMEM(packed_shape(heads), BF16),
            pltpu.VMEM(packed_shape(heads), BF16),
            pltpu.VMEM((8, dim), F32),
            pltpu.VMEM((n_sp - 1, 8, dim), F32),
            pltpu.VMEM((tok, 128), F32),
            pltpu.VMEM((tok, lanes), BF16),
            pltpu.VMEM((tok, lanes), BF16),
            pltpu.VMEM((tok, values), BF16),
            pltpu.VMEM((tok, dim), BF16),
            pltpu.VMEM((dim, tok), BF16),
            pltpu.SemaphoreType.DMA((sems,)),
            pltpu.SemaphoreType.DMA((sems,)),
            pltpu.SemaphoreType.DMA((10,)),
        ],
        compiler_params=pltpu.CompilerParams(
            collective_id=0, has_side_effects=True, vmem_limit_bytes=60 << 20
        ),
        name="forward",
    )(x, gain_a, gain_m, docs, table, wo, wg, wu, wd, wq, wk, wv)
    n = 9 + len(gathered)
    return result[:9], result[11], result[12:n], result[n:]


def backward_kernel(
    n_sp, widths, q_ref, k_ref, v_ref, g_ref, att_ref, inv_ref, prior_state_ref, doc_ref, table_ref, *rest,
):
    n_red = len(widths)
    sources, rest = rest[:n_red], rest[n_red:]
    (gq_ref, gk_ref, gv_ref), rest = rest[:3], rest[3:]
    finals, rest = rest[:n_red], rest[n_red:]
    swaps, rest = rest[:n_red], rest[n_red:]
    buffers, rest = [rest[4 * i : 4 * i + 4] for i in range(n_red)], rest[4 * n_red :]
    (
        stage_buf, mask_ref, ghat_ref, gq_acc, gk_acc, own_state, mate_state, in_state, out_state, later_state,
        prior_ref, later_ref,
        send_sem, recv_sem, local_sem,
    ) = rest
    tok, lanes = q_ref.shape
    n_z = n_sp // 2
    pairs = v_ref.shape[1] // 128
    where = place(n_sp)
    dp, sp, g, gy, gx, z, c, across_x, across_y, diagonal, partner = where
    copies = Copies(send_sem, recv_sem)
    reduces = [
        Reduce(
            copies, k, n_z, where, sources[k], swaps[k], buffers[k], finals[k],
            stage_buf.at[:, :, :, :, :, 0 : widths[k]], local_sem,
        )
        for k in range(n_red)
    ]
    docs = Documents(doc_ref, sp, n_sp)
    even = sp - c
    chain = Chain(
        copies, where, n_z, False, own_state, mate_state, in_state, out_state,
        docs.through(docs.first(even), docs.first(even + 1)), docs.through(docs.first(even + 1), docs.first(even + 2)),
    )
    along = [(dp, lax.rem(z + i, n_z) * 2 + c) for i in range(1, n_z)]
    meet([partner, across_x, across_y, diagonal] + along)
    for reduce in reduces:
        reduce.stage(0)

    def at(p, step, *todo):
        @pl.when(p == step)
        def _():
            for k, n in todo:
                reduces[k].stage(n)

    table = table_ref[...]
    row = lax.broadcasted_iota(jnp.int32, (tok, tok), 0)
    col = lax.broadcasted_iota(jnp.int32, (tok, tok), 1)
    mask_ref[...] = jnp.where((row <= col) & (docs.column == docs.row), 1.0, 0.0)
    prior_ref[...] = jnp.broadcast_to(jnp.where(docs.column == docs.last(sp - 1), 1.0, 0.0), prior_ref.shape)
    later_ref[...] = jnp.broadcast_to(jnp.where(docs.column == docs.first(sp + 1), 1.0, 0.0), later_ref.shape)
    gq_acc[...] = jnp.zeros_like(gq_acc)
    gk_acc[...] = jnp.zeros_like(gk_acc)
    r = lax.broadcasted_iota(jnp.int32, (128, 128), 0)
    c128 = lax.broadcasted_iota(jnp.int32, (128, 128), 1)
    same = jnp.where(r // 64 == c128 // 64, 1.0, 0.0).astype(BF16)
    lane64 = lax.broadcasted_iota(jnp.int32, (tok, 128), 1) % 64
    head_row = jnp.where(docs.row == docs.first(sp), 1.0, 0.0)

    def ghat_pair(p, carry):
        for when, todo in GHAT_SCHEDULE:
            at(p, when, *todo)
        columns = pl.ds(pl.multiple_of(p * 128, 128), 128)
        scaled = g_ref[:, columns].astype(F32) * inv_ref[:, columns].astype(F32)
        product = scaled * att_ref[:, columns].astype(F32)
        high = product.astype(BF16)
        low = (product - high.astype(F32)).astype(BF16)
        dots = -(mm(high, same) + mm(low, same))
        dots_high = dots.astype(BF16)
        dots_low = (dots - dots_high.astype(F32)).astype(BF16)
        extra = jnp.where(lane64 == 0, dots_high, jnp.where(lane64 == 1, dots_low, jnp.zeros_like(dots_low)))
        ghat = jnp.concatenate([scaled.astype(BF16), extra], axis=1)
        ghat_ref[p] = ghat
        ghat_t = ghat.astype(F32).T * head_row
        for side in range(2):
            head = p * 2 + side
            sel = selectors(table, head, lanes)
            one, two = factors(q_ref[...], sel, table)
            phi = (one * two).astype(BF16)
            lhs = jnp.concatenate(
                [ghat_t[side * 64 : side * 64 + 64], ghat_t[128 + side * 64 : 128 + side * 64 + 16]], axis=0
            )
            state = mm(lhs.astype(BF16), phi)
            z_row = jnp.sum(state[64:80], axis=0, keepdims=True)
            pack(
                own_state, 2 * pairs, p, side,
                jnp.concatenate([state[0:64], jnp.broadcast_to(z_row, (16, PAD_F))], axis=0),
            )
        return carry

    lax.fori_loop(0, pairs, ghat_pair, 0)

    chain.begin()
    turn = jnp.minimum((n_z - 1 - z) * CHAIN_BACK_STEPS, 2 * pairs - 1)

    lane = lax.broadcasted_iota(jnp.int32, (tok, 256), 1)
    first_row = lax.broadcasted_iota(jnp.int32, (128, PAD_F), 0)

    def main_pair(p, carry):
        columns = pl.ds(pl.multiple_of(p * 128, 128), 128)
        v_hat = with_ones(v_ref[:, columns])
        gv = [jnp.zeros((BLK, 128), F32) for _ in range(tok // BLK)]
        for side in range(2):
            step = p * 2 + side
            for when, todo in SCHEDULE:
                if when % 2 == side:
                    at(step, when, *todo)
            chain.middle(step == turn)
            head = p * 2 + side
            sel = selectors(table, head, lanes)
            ghat = jnp.where((lane % 128) // 64 == side, ghat_ref[p], jnp.zeros((tok, 256), BF16))
            q_head = head_lanes(q_ref[...], head)
            q_twice = q_head + q_head
            k_twice = head_lanes(k_ref[...], head, 2)
            prior = prior_state_ref[head]
            z_two = jnp.where(first_row // 2 == side * 32, prior[64:65], jnp.zeros((128, PAD_F), BF16))
            rows_p = placed(prior, side, z_two)
            q_one, q_two = factors(q_ref[...], sel, table)
            d_phi = mm(ghat, rows_p) * prior_ref[:, 0:1]
            gq_acc[...] += mm((d_phi * q_two).astype(BF16), sel[0], NT) + mm(
                (d_phi * q_one).astype(BF16), sel[1], NT
            )
            for j in range(tok // BLK):
                rows = slice(j * BLK, (j + 1) * BLK)
                onward = slice(j * BLK, tok)
                t = mm(k_ref[rows, :], q_head[onward], NT) + 4.0
                g_w = mm(v_hat[rows], ghat[onward], NT)
                mask = mask_ref[rows, onward]
                masked_t = t * mask
                w = (masked_t * t + 16.0 * mask).astype(BF16)
                g_s = (g_w * masked_t).astype(BF16)
                gv[j] = gv[j] + mm(w, ghat[onward, 0:128])
                gk_acc[rows, :] += mm(g_s, q_twice[onward])
                gq_acc[onward, :] += mm(g_s, k_twice[rows], TN)
        for j in range(tok // BLK):
            rows = slice(j * BLK, (j + 1) * BLK)
            gv_ref[rows, columns] = gv[j].astype(BF16)
        return carry

    lax.fori_loop(0, pairs, main_pair, 0)
    chain.drain()
    chain.finish(later_state, table[4:5])

    def later_pair(p, carry):
        for when, todo in LATE_SCHEDULE:
            at(p, when, *todo)
        columns = pl.ds(pl.multiple_of(p * 128, 128), 128)
        v_hat = with_ones(v_ref[:, columns])
        gv_inter = None
        for side in range(2):
            head = p * 2 + side
            sel = selectors(table, head, lanes)
            later = later_state[head]
            z_one = jnp.where(first_row == 0, later[64:65], jnp.zeros((128, PAD_F), BF16))
            rows_n = placed(later, side, z_one)
            k_one, k_two = factors(k_ref[...], sel, table)
            phi_k = (k_one * k_two).astype(BF16)
            gvi = mm(phi_k, rows_n[0:128], NT)
            gv_inter = gvi if gv_inter is None else gv_inter + gvi
            d_phi = mm(v_hat, rows_n) * later_ref[:, 0:1]
            gk_acc[...] += mm((d_phi * k_two).astype(BF16), sel[0], NT) + mm(
                (d_phi * k_one).astype(BF16), sel[1], NT
            )
        gv_ref[:, columns] = (gv_ref[:, columns].astype(F32) + gv_inter * later_ref[...]).astype(BF16)
        return carry

    lax.fori_loop(0, pairs, later_pair, 0)
    gq_ref[...] = gq_acc[...].astype(BF16)
    gk_ref[...] = gk_acc[...].astype(BF16)
    for k, n in LAST_SCHEDULE:
        reduces[k].stage(n)


GHAT_SCHEDULE = ((1, ((0, 1),)), (3, ((1, 1),)), (4, ((0, 2),)), (6, ((2, 1),)), (7, ((1, 2),)), )
SCHEDULE = ((1, ((0, 3),)), (2, ((3, 1),)), (4, ((2, 2),)), (6, ((1, 3),)), (7, ((0, 4),)), (9, ((3, 2),)), (10, ((2, 3),)), (12, ((1, 4),)), (14, ((0, 5),)), (15, ((3, 3),)), )
LATE_SCHEDULE = ((1, ((2, 4),)), (2, ((1, 5),)), (4, ((3, 4),)), (5, ((2, 5),)), (7, ((3, 5),)), )
LAST_SCHEDULE = ()


def shards_of(parts):
    return [part.reshape(-1, part.shape[-1]) for part in parts]


def backward(n_sp, arrays, grads):
    q, v = arrays[0], arrays[2]
    tok, lanes = q.shape
    heads = lanes // FEAT
    n_z = n_sp // 2
    rows = grads[0].shape[4]
    widths = tuple(grad.shape[5] for grad in grads)
    n_red = len(grads)
    vmem, anywhere = pl.BlockSpec(memory_space=pltpu.VMEM), pl.BlockSpec(memory_space=pl.ANY)
    shape = jax.ShapeDtypeStruct
    sems = n_red * n_reduce(n_z) + 3
    result = pl.pallas_call(
        functools.partial(backward_kernel, n_sp, widths),
        out_shape=(shape(q.shape, BF16), shape(q.shape, BF16), shape(v.shape, BF16))
        + tuple(shape((2, 2, rows, w), BF16) for w in widths)
        + tuple(shape((n_z, 2, 2, rows, w), BF16) for w in widths),
        in_specs=[vmem] * len(arrays) + [anywhere] * n_red,
        out_specs=(vmem,) * (3 + n_red) + (anywhere,) * n_red,
        scratch_shapes=sum([reduce_scratch(n_z, rows, w) for w in widths], [])
        + [
            pltpu.VMEM((2, 2, 2, 2, rows, max(widths)), BF16),
            pltpu.VMEM((tok, tok), F32),
            pltpu.VMEM((heads // 2, tok, 256), BF16),
            pltpu.VMEM(q.shape, F32),
            pltpu.VMEM(q.shape, F32),
            pltpu.VMEM(packed_shape(heads), BF16),
            pltpu.VMEM(packed_shape(heads), BF16),
            pltpu.VMEM(packed_shape(heads), BF16),
            pltpu.VMEM(packed_shape(heads), BF16),
            pltpu.VMEM((heads, ROWS_S, PAD_F), BF16),
            pltpu.VMEM((tok, 128), F32),
            pltpu.VMEM((tok, 128), F32),
            pltpu.SemaphoreType.DMA((sems,)),
            pltpu.SemaphoreType.DMA((sems,)),
            pltpu.SemaphoreType.DMA((2, 2)),
        ],
        compiler_params=pltpu.CompilerParams(
            collective_id=1, has_side_effects=True, vmem_limit_bytes=63 << 20
        ),
        name="backward",
    )(*arrays, *grads)
    return result[:3], shards_of(result[3 : 3 + n_red])


def reduce_units(chunks):
    edges = [0, 2, 4, 6, 8, chunks]
    return list(zip(edges[:-1], edges[1:]))


IN_FFN = 2
FFN_SCHEDULE = {
    1: (("g", 0, 1), ("g", 1, 0)),
    3: (("g", 0, 2), ("r", 0, 0)),
    4: (("g", 1, 1), ("g", 0, 3), ("r", 0, 1)),
    5: (("g", 0, 4), ("r", 1, 0)),
    6: (("g", 1, 2), ("r", 0, 2), ("r", 1, 1)),
    7: (("g", 1, 3),),
    8: (("g", 1, 4), ("r", 0, 3), ("r", 1, 2)),
    9: (("r", 1, 3),),
    10: (("r", 0, 4),),
}
FFN_LATE = (("r", 1, 4),)
FFN_LAST = (("r", 0, 5), ("r", 1, 5))


def ffn_kernel(n_sp, gather_units, chunks, x_ref, att_ref, out_w_ref, gain_ref, cot_ref, *rest):
    n_unit = len(gather_units)
    sums = reduce_units(chunks)
    n_sum = len(sums)
    early, rest = rest[:EARLY], rest[EARLY:]
    kept, rest = rest[: n_unit - EARLY], rest[n_unit - EARLY :]
    ggain_ref, rest = rest[0], rest[1:]
    finals, rest = rest[:IN_FFN], rest[IN_FFN:]
    (output_ref, gh_ref, gatt_ref, gout_ref), rest = rest[:4], rest[4:]
    grads, rest = rest[: n_sum - IN_FFN], rest[n_sum - IN_FFN :]
    late, rest = rest[: n_unit - EARLY], rest[n_unit - EARLY :]
    grads, rest = rest[:IN_FFN] + grads, rest[IN_FFN:]
    swaps, rest = rest[:IN_FFN], rest[IN_FFN:]
    buffers, rest = [rest[4 * i : 4 * i + 4] for i in range(IN_FFN)], rest[4 * IN_FFN :]
    (
        hid, n2, n2_t, cot_t, acc_o, acc_n, parts, w_buf, g_buf, send_sem, recv_sem, w_sem, g_sem, o_sem,
    ) = rest
    tok, dim = x_ref.shape
    n_z = n_sp // 2
    where = place(n_sp)
    dp, sp, g, gy, gx, z, c, across_x, across_y, diagonal, partner = where
    copies = Copies(send_sem, recv_sem)
    gathers = [Gather(copies, ("g", k), n_z, own, full, where) for k, (own, full) in enumerate(zip(kept, late))]
    reduces = [
        Reduce(copies, ("r", k), n_z, where, grads[k], swaps[k], buffers[k], finals[k])
        for k in range(IN_FFN)
    ]
    along = [(dp, lax.rem(z + i, n_z) * 2 + c) for i in range(1, n_z)]
    meet([partner, across_x, across_y, diagonal] + along)
    gathers[0].stage(0)
    own_copies = [
        pltpu.make_async_copy(own, gather.own_place, o_sem.at[k])
        for k, (own, gather) in enumerate(zip(kept, gathers))
    ]
    for copy in own_copies:
        copy.start()

    def run(todo):
        for kind, k, n in todo:
            (gathers if kind == "g" else reduces)[k].stage(n)

    fulls = list(early) + list(late)

    def load(chunk, slot, do_wait=False):
        if do_wait:
            for i in range(3):
                pltpu.make_async_copy(fulls[0].at[:, 0:CHUNK], w_buf.at[slot, i], w_sem.at[slot, i]).wait()
            return
        for full, (first, last) in zip(fulls, gather_units):
            @pl.when((chunk >= first) & (chunk < last))
            def _():
                for i in range(3):
                    lane = pl.multiple_of((chunk - first + i * (last - first)) * CHUNK, CHUNK)
                    pltpu.make_async_copy(full.at[:, pl.ds(lane, CHUNK)], w_buf.at[slot, i], w_sem.at[slot, i]).start()

    def save(chunk, slot, do_wait=False):
        if do_wait:
            for i in range(3):
                pltpu.make_async_copy(
                    g_buf.at[slot, i], grads[0].at[:, :, :, :, :, 0:CHUNK], g_sem.at[slot, i]
                ).wait()
            return
        for grad, (first, last) in zip(grads, sums):
            @pl.when((chunk >= first) & (chunk < last))
            def _():
                for i in range(3):
                    lane = pl.multiple_of((chunk - first + i * (last - first)) * CHUNK, CHUNK)
                    pltpu.make_async_copy(
                        g_buf.at[slot, i], grad.at[:, :, :, :, :, pl.ds(lane, CHUNK)], g_sem.at[slot, i]
                    ).start()

    load(0, 0)
    gain = gain_ref[4:5]
    def prepare(i, carry):
        rows = pl.ds(pl.multiple_of(i * BLK, BLK), BLK)
        hidden = x_ref[rows, :].astype(F32) + mm(att_ref[rows, :], out_w_ref[...], NT)
        hid[rows, :] = hidden
        scale = lax.rsqrt(jnp.mean(hidden * hidden, axis=1, keepdims=True) + EPSILON)
        normed = (hidden * scale * gain).astype(BF16)
        n2[rows, :] = normed
        n2_t[:, rows] = normed.T
        cot_t[:, rows] = cot_ref[rows, :].T
        return carry

    lax.fori_loop(0, tok // BLK, prepare, 0)
    acc_o[...] = jnp.zeros_like(acc_o)
    acc_n[...] = jnp.zeros_like(acc_n)
    for copy in own_copies:
        copy.wait()
    grad_shape = g_buf.shape[2:]

    def step(chunk, carry):
        slot = lax.rem(chunk, 2)
        load(chunk, slot, True)

        @pl.when(chunk >= 2)
        def _():
            save(chunk, slot, True)

        for when, todo in FFN_SCHEDULE.items():
            @pl.when(chunk == when)
            def _():
                run(todo)

        @pl.when(chunk + 1 < chunks)
        def _():
            load(chunk + 1, 1 - slot)

        def rows_part(i, carry):
            rows = pl.ds(pl.multiple_of(i * STRIP, STRIP), STRIP)
            wg, wu, wd = w_buf[slot, 0], w_buf[slot, 1], w_buf[slot, 2]
            gate = mm(n2[rows, :], wg)
            up = mm(n2[rows, :], wu)
            g_mixed = mm(cot_ref[rows, :], wd)
            sig = 1.0 / (1.0 + jnp.exp(-gate))
            act = gate * sig
            mixed = (act * up).astype(BF16)
            g_gate = (g_mixed * up * sig * (1.0 + gate * (1.0 - sig))).astype(BF16)
            g_up = (g_mixed * act).astype(BF16)
            parts[0, rows, :] = g_gate
            parts[1, rows, :] = g_up
            parts[2, rows, :] = mixed
            acc_o[rows, :] += mm(mixed, wd, NT)
            acc_n[rows, :] += mm(g_gate, wg, NT) + mm(g_up, wu, NT)
            return carry

        lax.fori_loop(0, tok // STRIP, rows_part, 0)
        g_buf[slot, 0] = mm(n2_t[...], parts[0]).astype(BF16).reshape(grad_shape)
        g_buf[slot, 1] = mm(n2_t[...], parts[1]).astype(BF16).reshape(grad_shape)
        g_buf[slot, 2] = mm(cot_t[...], parts[2]).astype(BF16).reshape(grad_shape)
        save(chunk, slot)
        return carry

    lax.fori_loop(0, chunks, step, 0)
    run(FFN_LATE)
    def conclude(i, total):
        rows = pl.ds(pl.multiple_of(i * BLK, BLK), BLK)
        hidden = hid[rows, :]
        n2[rows, :] = (hidden + acc_o[rows, :]).astype(BF16)
        scale = lax.rsqrt(jnp.mean(hidden * hidden, axis=1, keepdims=True) + EPSILON)
        e = acc_n[rows, :]
        eg = e * gain
        inner = jnp.mean(eg * hidden, axis=1, keepdims=True)
        gh = cot_ref[rows, :].astype(F32) + scale * eg - hidden * (scale * scale * scale * inner)
        acc_o[rows, :] = gh
        branch = gh.astype(BF16)
        n2_t[rows, :] = branch
        cot_t[rows, :] = mm(branch, out_w_ref[...]).astype(BF16)
        return total + jnp.sum(e * hidden * scale, axis=0, keepdims=True)

    total = lax.fori_loop(0, tok // BLK, conclude, jnp.zeros((1, dim), F32))
    ggain_ref[...] = jnp.broadcast_to(total, ggain_ref.shape)
    outs = [
        pltpu.make_async_copy(n2, output_ref, o_sem.at[0]),
        pltpu.make_async_copy(acc_o, gh_ref, o_sem.at[1]),
        pltpu.make_async_copy(cot_t, gatt_ref, o_sem.at[2]),
    ]
    for copy in outs:
        copy.start()
    save(chunks - 2, (chunks - 2) % 2, True)
    save(chunks - 1, (chunks - 1) % 2, True)
    def out_copy(i):
        lanes = pl.ds(pl.multiple_of(i * CHUNK, CHUNK), CHUNK)
        slot, part = i // 3, lax.rem(i, 3)
        return pltpu.make_async_copy(
            g_buf.at[slot, part], gout_ref.at[:, :, :, :, :, lanes], g_sem.at[slot, part]
        )

    def out_piece(i, carry):
        lanes = pl.ds(pl.multiple_of(i * CHUNK, CHUNK), CHUNK)
        g_buf[i // 3, lax.rem(i, 3)] = mm(n2_t[...], att_ref[:, lanes], TN).astype(BF16).reshape(grad_shape)
        out_copy(i).start()
        return carry

    n_out = att_ref.shape[1] // CHUNK
    lax.fori_loop(0, n_out, out_piece, 0)
    outs = outs + [out_copy(i) for i in range(n_out)]
    run(FFN_LAST)
    for copy in outs:
        copy.wait()


def ffn(n_sp, x, att, out_w, gain, cot, width, early, kept):
    tok, dim = x.shape
    values = att.shape[1]
    n_z = n_sp // 2
    chunks = -(-width // CHUNK)
    gather_units = units_of(width)
    sums = reduce_units(chunks)
    rows = dim // n_sp // GROUP
    spans = [3 * CHUNK * (last - first) for first, last in sums]
    vmem, anywhere = pl.BlockSpec(memory_space=pltpu.VMEM), pl.BlockSpec(memory_space=pl.ANY)
    shape = jax.ShapeDtypeStruct
    split = lambda w: shape((n_z, 2, 2, 2, rows, w), BF16)
    sems = len(kept) * n_copies(n_z) + IN_FFN * n_reduce(n_z)
    full_shapes = tuple(shape((k.shape[0] * n_sp, k.shape[1]), BF16) for k in kept)
    result = pl.pallas_call(
        functools.partial(ffn_kernel, n_sp, gather_units, chunks),
        out_shape=(shape((8, dim), F32),)
        + tuple(shape((2, 2, rows, w), BF16) for w in spans[:IN_FFN])
        + (shape((tok, dim), BF16), shape((tok, dim), F32), shape((tok, values), BF16), split(values))
        + tuple(split(w) for w in spans[IN_FFN:])
        + full_shapes,
        in_specs=[vmem] * 5 + [anywhere] * len(early) + [vmem] * len(kept),
        out_specs=(vmem,) * (1 + IN_FFN) + (anywhere,) * (4 + len(spans) - IN_FFN + len(kept)),
        scratch_shapes=[pltpu.VMEM((n_z, 2, 2, 2, rows, w), BF16) for w in spans[:IN_FFN]]
        + [pltpu.VMEM((n_z, 2, 2, rows, w), BF16) for w in spans[:IN_FFN]]
        + sum([reduce_scratch(n_z, rows, w) for w in spans[:IN_FFN]], [])
        + [
            pltpu.VMEM((tok, dim), F32),
            pltpu.VMEM((tok, dim), BF16),
            pltpu.VMEM((dim, tok), BF16),
            pltpu.VMEM((dim, tok), BF16),
            pltpu.VMEM((tok, dim), F32),
            pltpu.VMEM((tok, dim), F32),
            pltpu.VMEM((3, tok, CHUNK), BF16),
            pltpu.VMEM((2, 3, dim, CHUNK), BF16),
            pltpu.VMEM((2, 3, n_z, 2, 2, 2, rows, CHUNK), BF16),
            pltpu.SemaphoreType.DMA((sems,)),
            pltpu.SemaphoreType.DMA((sems,)),
            pltpu.SemaphoreType.DMA((2, 3)),
            pltpu.SemaphoreType.DMA((2, 3)),
            pltpu.SemaphoreType.DMA((4,)),
        ],
        compiler_params=pltpu.CompilerParams(
            collective_id=2, has_side_effects=True, vmem_limit_bytes=63 << 20
        ),
        name="ffn",
    )(x, att, out_w, gain, cot, *early, *kept)
    n = 1 + IN_FFN
    shards = shards_of(result[1:n])
    output, g_hidden, g_att, g_out = result[n : n + 4]
    grads = result[n + 4 : n + 4 + len(spans) - IN_FFN]
    return output, g_hidden, g_att, result[0], g_out, shards, grads


def tail_kernel(
    n_sp, normed_ref, gq_ref, gk_ref, gv_ref, gain_ref, ggain_ref, w_hbm, x_hbm, gh_hbm, gains_ref, *rest,
):
    finals, rest = rest[:3], rest[3:]
    gin_ref, rest = rest[0], rest[1:]
    sources, rest = rest[:3], rest[3:]
    swaps, rest = rest[:3], rest[3:]
    buffers, rest = [rest[4 * i : 4 * i + 4] for i in range(3)], rest[12:]
    w_ref, x_ref, gh_ref, own_gains, sum_gains, in_sp, in_dp, send_sem, recv_sem, local_sem = rest
    tok, dim = x_ref.shape
    n_z = n_sp // 2
    lanes = gq_ref.shape[1]
    where = place(n_sp)
    dp, sp, g, gy, gx, z, c, across_x, across_y, diagonal, partner = where
    loads = [
        pltpu.make_async_copy(src, dst, local_sem.at[i])
        for i, (src, dst) in enumerate(((w_hbm, w_ref), (x_hbm, x_ref), (gh_hbm, gh_ref)))
    ]
    for copy in loads:
        copy.start()
    copies = Copies(send_sem, recv_sem)
    reduces = [Reduce(copies, k, n_z, where, sources[k], swaps[k], buffers[k], finals[k]) for k in range(3)]
    others = [(dp, lax.rem(sp + i, n_sp)) for i in range(1, n_sp)]
    groups = [across_x, across_y, diagonal]
    for i, device in enumerate(others):
        copies.add(("sp", i), own_gains, in_sp.at[i], device)
    for i, device in enumerate(groups):
        copies.add(("dp", i), sum_gains, in_dp.at[i], device)
    meet(others + groups)
    block = sources[0].shape[:-1] + (BLK,)
    half = gv_ref.shape[1] // 2

    def product(k, j, ref, i):
        sources[k][:, :, :, :, :, pl.ds(j, BLK)] = (
            mm(normed_ref[...], ref[:, pl.ds(i, BLK)]).astype(BF16).reshape(block)
        )

    def values_piece(n, carry):
        first = pl.multiple_of(n * BLK, BLK)
        product(0, first, gv_ref, first)
        return carry

    def more_values_piece(n, carry):
        first = pl.multiple_of(n * BLK, BLK)
        product(1, first, gv_ref, pl.multiple_of(half + first, BLK))
        return carry

    lax.fori_loop(0, half // BLK, values_piece, 0)
    lax.fori_loop(0, half // BLK, more_values_piece, 0)
    reduces[0].stage(0)
    for j in range(0, lanes, BLK):
        product(2, j, gq_ref, j)
        if j == 0:
            reduces[1].stage(0)
        product(2, lanes + j, gk_ref, j)
    for copy in loads:
        copy.wait()
    todo = [[(2, 0), (0, 1)], [(1, 1)], [(0, 2), (2, 1)], [(1, 2)]]
    gain = gain_ref[0:1]
    n_block = tok // BLK

    def norm_back(i, total):
        rows = pl.ds(pl.multiple_of(i * BLK, BLK), BLK)
        e = (
            mm(gq_ref[rows, :], w_ref[:, 0:lanes], NT)
            + mm(gk_ref[rows, :], w_ref[:, lanes : 2 * lanes], NT)
            + mm(gv_ref[rows, :], w_ref[:, 2 * lanes :], NT)
        )
        u = x_ref[rows, :].astype(F32)
        scale = lax.rsqrt(jnp.mean(u * u, axis=1, keepdims=True) + EPSILON)
        eg = e * gain
        inner = jnp.mean(eg * u, axis=1, keepdims=True)
        gh_ref[rows, :] = gh_ref[rows, :] + scale * eg - u * (scale * scale * scale * inner)
        for step, stages in enumerate(todo):
            @pl.when(i == min(step, n_block - 1))
            def _():
                for k, n in stages:
                    reduces[k].stage(n)

        return total + jnp.sum(e * u * scale, axis=0, keepdims=True)

    total = lax.fori_loop(0, n_block, norm_back, jnp.zeros((1, dim), F32))
    save = pltpu.make_async_copy(gh_ref, gin_ref, local_sem.at[0])
    save.start()
    row = lax.broadcasted_iota(jnp.int32, own_gains.shape, 0)
    own_gains[...] = jnp.where(row == 0, jnp.broadcast_to(total, own_gains.shape), ggain_ref[...])
    reduces[0].stage(3)
    reduces[2].stage(2)
    copies.start(*[("sp", i) for i in range(n_sp - 1)])
    reduces[1].stage(3)
    reduces[0].stage(4)
    reduces[2].stage(3)
    copies.arrived(*[("sp", i) for i in range(n_sp - 1)])
    sum_gains[...] = own_gains[...] + rows_sum([in_sp[i] for i in range(n_sp - 1)])
    reduces[1].stage(4)
    copies.start(*[("dp", i) for i in range(3)])
    reduces[2].stage(4)
    copies.arrived(*[("dp", i) for i in range(3)])
    gains_ref[...] = sum_gains[...] + rows_sum([in_dp[i] for i in range(3)])
    for reduce in reduces:
        reduce.stage(5)
    copies.sent(*[("sp", i) for i in range(n_sp - 1)], *[("dp", i) for i in range(3)])
    save.wait()


def tail(n_sp, normed, gq, gk, gv, w_joint, x, g_hidden, gain, ggain):
    tok, dim = x.shape
    lanes, values = gq.shape[1], gv.shape[1]
    n_z = n_sp // 2
    rows = dim // n_sp // GROUP
    vmem, anywhere = pl.BlockSpec(memory_space=pltpu.VMEM), pl.BlockSpec(memory_space=pl.ANY)
    shape = jax.ShapeDtypeStruct
    widths = (values // 2, values // 2, 2 * lanes)
    sems = 3 * n_reduce(n_z) + n_sp + 2
    return pl.pallas_call(
        functools.partial(tail_kernel, n_sp),
        out_shape=(shape((8, dim), F32),)
        + tuple(shape((2, 2, rows, w), BF16) for w in widths)
        + (shape((tok, dim), F32),),
        in_specs=[vmem] * 6 + [anywhere] * 3,
        out_specs=(vmem,) * 4 + (anywhere,),
        scratch_shapes=[pltpu.VMEM((n_z, 2, 2, 2, rows, w), BF16) for w in widths]
        + [pltpu.VMEM((n_z, 2, 2, rows, w), BF16) for w in widths]
        + sum([reduce_scratch(n_z, rows, w) for w in widths], [])
        + [
            pltpu.VMEM(w_joint.shape, BF16),
            pltpu.VMEM(x.shape, BF16),
            pltpu.VMEM((tok, dim), F32),
            pltpu.VMEM((8, dim), F32),
            pltpu.VMEM((8, dim), F32),
            pltpu.VMEM((n_sp - 1, 8, dim), F32),
            pltpu.VMEM((3, 8, dim), F32),
            pltpu.SemaphoreType.DMA((sems,)),
            pltpu.SemaphoreType.DMA((sems,)),
            pltpu.SemaphoreType.DMA((3,)),
        ],
        compiler_params=pltpu.CompilerParams(
            collective_id=3, has_side_effects=True, vmem_limit_bytes=63 << 20
        ),
        name="tail",
    )(normed, gq, gk, gv, gain, ggain, w_joint, x, g_hidden)


def finish_kernel(sums, *refs):
    n = len(sums) + 4
    sources, refs = refs[:n], refs[n:]
    (q_out, k_out, v_out, out_out, gate_out, up_out, down_out), refs = refs[:7], refs[7:]
    held, sem = refs[:n], refs[n]
    copies = [pltpu.make_async_copy(src, dst, sem.at[i]) for i, (src, dst) in enumerate(zip(sources, held))]
    for copy in copies:
        copy.start()
    for copy in copies:
        copy.wait()
    qk_ref, va_ref, vb_ref, out_ref, units = held[0], held[1], held[2], held[3], held[4:]
    lanes = q_out.shape[1]
    width = gate_out.shape[0]
    q_out[...] = qk_ref[:, :lanes].astype(F32)
    k_out[...] = qk_ref[:, lanes:].astype(F32)
    v_out[:, : va_ref.shape[1]] = va_ref[...].astype(F32)
    v_out[:, va_ref.shape[1] :] = vb_ref[...].astype(F32)
    out_out[...] = out_ref[...].astype(F32).T
    for unit, (first, last) in zip(units, sums):
        lo, hi = first * CHUNK, min(last * CHUNK, width)
        span = (last - first) * CHUNK
        for i, out in enumerate((gate_out, up_out, down_out)):
            out[lo:hi, :] = unit[:, i * span : i * span + hi - lo].astype(F32).T


def finish(width, lanes, qk, va, vb, out, units):
    shard = va.shape[0]
    vmem, anywhere = pl.BlockSpec(memory_space=pltpu.VMEM), pl.BlockSpec(memory_space=pl.ANY)
    shape = jax.ShapeDtypeStruct
    arrays = (qk, va, vb, out, *units)
    return pl.pallas_call(
        functools.partial(finish_kernel, reduce_units(-(-width // CHUNK))),
        out_shape=(
            shape((shard, lanes), F32), shape((shard, lanes), F32), shape((shard, 2 * va.shape[1]), F32),
            shape(out.shape[::-1], F32), shape((width, shard), F32), shape((width, shard), F32),
            shape((width, shard), F32),
        ),
        in_specs=[anywhere] * len(arrays),
        out_specs=(vmem,) * 7,
        scratch_shapes=[pltpu.VMEM(a.shape, BF16) for a in arrays] + [pltpu.SemaphoreType.DMA((len(arrays),))],
        compiler_params=pltpu.CompilerParams(vmem_limit_bytes=63 << 20),
        name="finish",
    )(*arrays)


def body(
    tokens, doc_ids, gain_attn, w_query, w_key, w_value, w_out, gain_mlp, w_gate, w_up, w_down, cotangent
):
    n_sp = lax.axis_size("sp")
    me = lax.axis_index("sp")
    tok = tokens.shape[0]
    heads = w_query.shape[1] // FEAT
    table = feature_table()
    docs = doc_ids
    width = gain_attn.shape[0]
    lanes = heads * FEAT
    hidden_units = w_gate.shape[1]
    parts = [part[None, :] for part in (gain_attn, gain_mlp)]
    if width % 128:
        parts = [jnp.tile(part, (1, n_sp)) for part in parts]
    (
        (att, inv, prior_state, gain, q, k, v, normed_one, w_joint), out_t, early, kept
    ) = forward(
        n_sp, tokens, *parts, docs, table, w_out, w_gate.T, w_up.T, w_down, w_query, w_key, w_value
    )
    output, g_hidden, g_att, grad_gain_two, g_out, shards, grads = ffn(
        n_sp, tokens, att, out_t, gain, cotangent, hidden_units, early, kept
    )
    (gq, gk, gv), (s_out, *more) = backward(
        n_sp, (q, k, v, g_att, att, inv, prior_state, docs, table), (g_out, *grads)
    )
    grad_gains, *joint, grad_input = tail(
        n_sp, normed_one, gq, gk, gv, w_joint, tokens, g_hidden, gain, grad_gain_two
    )
    n_dp = lax.axis_size("dp")

    def over_groups(shard):
        if n_dp > GROUP:
            shard = lax.psum(shard, "dp") * jnp.asarray(GROUP / n_dp, shard.dtype)
        return shard

    s_va, s_vb, s_query_key = shards_of(joint)
    g_query, g_key, g_value, g_w_out, g_gate, g_up, g_down = finish(
        hidden_units, lanes, over_groups(s_query_key), over_groups(s_va), over_groups(s_vb), over_groups(s_out),
        [over_groups(shard) for shard in (*shards, *more)],
    )
    s_gains = over_groups(lax.dynamic_slice(grad_gains, (0, me * width), (2, width)))
    return (
        output, grad_input, s_gains[0], g_query, g_key, g_value, g_w_out, s_gains[1], g_gate.T, g_up.T, g_down
    )


def solution(mesh):
    placed_in = (
        P(("dp", "sp"), None), P("dp", None), P("sp"), P("sp", None), P("sp", None), P("sp", None),
        P(None, "sp"), P("sp"), P("sp", None), P("sp", None), P(None, "sp"), P(("dp", "sp"), None),
    )
    return jax.shard_map(
        body,
        mesh=mesh,
        in_specs=placed_in,
        out_specs=(
            P(("dp", "sp"), None), P(("dp", "sp"), None), P("sp"), P("sp", None), P("sp", None),
            P("sp", None), P(None, "sp"), P("sp"), P("sp", None), P("sp", None), P(None, "sp"),
        ),
        check_vma=False,
    )
```

```python
import functools
import math

import jax
import jax.numpy as jnp
import numpy as np
from jax import lax
from jax.experimental import pallas as pl
from jax.experimental.pallas import tpu as pltpu
from jax.sharding import PartitionSpec as P

FEAT = 16
HEAD_V = 64
EPSILON = 1e-05
BF16 = jnp.bfloat16
F32 = jnp.float32
BLK = 256
PAD_F = 256
ROWS_S = 80
NN = (((1,), (0,)), ((), ()))
NT = (((1,), (1,)), ((), ()))
TN = (((0,), (0,)), ((), ()))


def mm(a, b, dims=NN):
    return lax.dot_general(a, b, dims, preferred_element_type=F32)


def feature_table():
    rows = []
    for a in range(FEAT):
        for b in range(a, FEAT):
            rows.append((a, b, 0.0, 0.0, 1.0 if a == b else 2.0))
    for a in range(FEAT):
        rows.append((a, -1, 0.0, 1.0, 8.0))
    rows.append((-1, -1, 1.0, 1.0, 32.0))
    while len(rows) < PAD_F:
        rows.append((-1, -1, 0.0, 0.0, 0.0))
    table = np.zeros((8, PAD_F), np.float32)
    table[:5] = np.array(rows, np.float32).T
    return jnp.asarray(table)


def selectors(table, head, lanes):
    row = lax.broadcasted_iota(jnp.int32, (lanes, PAD_F), 0).astype(F32)
    base = (head * FEAT).astype(F32)
    first = jnp.where((row == table[0:1] + base) & (table[0:1] >= 0), 1.0, 0.0).astype(BF16)
    second = jnp.where((row == table[1:2] + base) & (table[1:2] >= 0), 1.0, 0.0).astype(BF16)
    return first, second


def head_lanes(values, head, scale=1):
    lane = lax.broadcasted_iota(jnp.int32, values.shape, 1)
    return jnp.where(lane // FEAT == head, values * scale, jnp.zeros_like(values))


def factors(values, sel, table):
    one = mm(values, sel[0]) + table[2:3]
    two = mm(values, sel[1]) + table[3:4]
    return one, two


def with_ones(v_pair):
    return jnp.concatenate([v_pair, jnp.ones_like(v_pair)], axis=1)


class Copies:
    def __init__(self, send_sem, recv_sem):
        self.send_sem, self.recv_sem, self.made = send_sem, recv_sem, {}

    def add(self, name, src, dst, device):
        self.made[name] = (src, dst, len(self.made), device)

    def get(self, name):
        src, dst, index, device = self.made[name]
        return pltpu.make_async_remote_copy(
            src_ref=src,
            dst_ref=dst,
            send_sem=self.send_sem.at[index],
            recv_sem=self.recv_sem.at[index],
            device_id=device,
            device_id_type=pl.DeviceIdType.MESH,
        )

    def start(self, *names):
        for name in names:
            self.get(name).start()

    def arrived(self, *names):
        for name in names:
            self.get(name).wait_recv()

    def sent(self, *names):
        for name in names:
            self.get(name).wait_send()


GROUP = 4


def place(n_sp):
    dp, sp = lax.axis_index("dp"), lax.axis_index("sp")
    g = lax.rem(dp, GROUP)
    gy, gx = g // 2, lax.rem(g, 2)
    z, c = sp // 2, lax.rem(sp, 2)
    across_x = (dp - g + gy * 2 + (1 - gx), sp)
    across_y = (dp - g + (1 - gy) * 2 + gx, sp)
    diagonal = (dp - g + (1 - gy) * 2 + (1 - gx), sp)
    partner = (dp, z * 2 + (1 - c))
    return dp, sp, g, gy, gx, z, c, across_x, across_y, diagonal, partner


class Gather:
    def __init__(self, copies, tag, n_z, own, full, where):
        dp, sp, g, gy, gx, z, c, across_x, across_y, _, partner = where
        self.copies, self.tag, self.n_z = copies, tag, n_z
        shard, width = own.shape
        quarter = shard // GROUP
        lower, upper = pl.ds(0, width // 2), pl.ds(width // 2, width // 2)

        def rows(zz, gg, count, lanes=None):
            start = pl.multiple_of((zz * 2 + c) * shard + gg * quarter, 16)
            return full.at[pl.ds(start, count)] if lanes is None else full.at[pl.ds(start, count), lanes]

        gx_of, gy_of = gy * 2 + (1 - gx), (1 - gy) * 2 + gx
        diag = (1 - gy) * 2 + (1 - gx)
        add = lambda name, src, dst, device: copies.add((tag, name), src, dst, device)
        mine = own.at[pl.ds(pl.multiple_of(g * quarter, 16), quarter)]
        self.own_place = rows(z, 0, shard)
        add("c0", own, self.own_place, partner)
        for i in range(1, n_z):
            zt = lax.rem(z + i, n_z)
            zs = lax.rem(z + n_z - i, n_z)
            add(f"z{i}", mine, rows(z, g, quarter), (dp, zt * 2 + c))
            here = rows(zs, g, quarter)
            add(f"x{i}", here, here, across_x)
            add(f"y{i}", here, here, across_y)
            add(f"c1{i}", here, here, partner)
            first = rows(zs, gx_of, quarter, lower)
            add(f"d0{i}", first, first, across_y)
            second = rows(zs, gy_of, quarter, upper)
            add(f"d1{i}", second, second, across_x)
            for name, gg in (("c2", gx_of), ("c3", gy_of), ("c4", diag)):
                there = rows(zs, gg, quarter)
                add(f"{name}{i}", there, there, partner)

    def each(self, *names):
        return [(self.tag, f"{name}{i}") for i in range(1, self.n_z) for name in names]

    def stage(self, n):
        copies = self.copies
        if n == 0:
            copies.start(*self.each("z"), (self.tag, "c0"))
        elif n == 1:
            for i in range(1, self.n_z):
                copies.arrived((self.tag, f"z{i}"))
                copies.start(*[(self.tag, f"{name}{i}") for name in ("x", "y", "c1")])
        elif n == 2:
            for i in range(1, self.n_z):
                copies.arrived((self.tag, f"x{i}"), (self.tag, f"y{i}"))
                copies.start(*[(self.tag, f"{name}{i}") for name in ("d0", "d1", "c2", "c3")])
        elif n == 3:
            for i in range(1, self.n_z):
                copies.arrived((self.tag, f"d0{i}"), (self.tag, f"d1{i}"))
                copies.start((self.tag, f"c4{i}"))
        else:
            copies.arrived((self.tag, "c0"), *self.each("c1", "c2", "c3", "c4"))
            copies.sent((self.tag, "c0"), *self.each("z", "x", "y", "c1", "d0", "d1", "c2", "c3", "c4"))


def n_copies(n_z):
    return 1 + 9 * (n_z - 1)


def meet(devices):
    barrier = pltpu.get_barrier_semaphore()
    for device in devices:
        pl.semaphore_signal(barrier, inc=1, device_id=device, device_id_type=pl.DeviceIdType.MESH)
    pl.semaphore_wait(barrier, len(devices))


def placed(state, side, z_rows):
    zero = jnp.zeros((64, PAD_F), state.dtype)
    values = [state[0:64], zero] if side == 0 else [zero, state[0:64]]
    return jnp.concatenate(values + [z_rows], axis=0)


class Reduce:
    def __init__(self, copies, tag, n_z, where, source, swapped, buffers, final, stage_buf=None, local_sem=None):
        dp, sp, g, gy, gx, z, c, across_x, across_y, diagonal, partner = where
        self.copies, self.tag, self.n_z = copies, tag, n_z
        self.gy, self.gx, self.z, self.c = gy, gx, z, c
        self.source, self.swapped, self.final = source, swapped, final
        self.work, self.first, self.second, self.along = buffers
        self.stage_buf, self.local_sem = stage_buf, local_sem
        work = self.work
        half = work.shape[-1] // 2
        self.halves = (pl.ds(0, half), pl.ds(half, half))
        lower, upper = self.halves
        everything = slice(None)
        add = lambda name, src, dst, device: copies.add((tag, name), src, dst, device)
        add("s", source.at[:, 1 - c], swapped, partner)
        add("a1", work.at[:, :, 1 - gx, everything, lower], self.first.at[0], across_x)
        add("b1", work.at[:, 1 - gy, :, everything, upper], self.first.at[1], across_y)
        add("a2", work.at[:, 1 - gy, gx, everything, lower], self.second.at[0], across_y)
        add("b2", work.at[:, gy, 1 - gx, everything, upper], self.second.at[1], across_x)
        for i in range(1, n_z):
            zt = lax.rem(z + i, n_z)
            add(f"z{i}", work.at[zt, gy, gx], self.along.at[i - 1], (dp, zt * 2 + c))
        for name, device in (("fx", across_x), ("fy", across_y), ("fd", diagonal)):
            add(name, final.at[gy, gx], final.at[gy, gx], device)

    def names(self, *names):
        return [(self.tag, name) for name in names]

    def load(self, zz):
        slot = zz % 2
        return (
            pltpu.make_async_copy(self.source.at[zz, self.c], self.stage_buf.at[slot, 0], self.local_sem.at[slot, 0]),
            pltpu.make_async_copy(self.swapped.at[zz], self.stage_buf.at[slot, 1], self.local_sem.at[slot, 1]),
        )

    def stage(self, n):
        copies, work, gy, gx, n_z = self.copies, self.work, self.gy, self.gx, self.n_z
        zs = ["z%d" % i for i in range(1, n_z)]
        lower, upper = self.halves
        if n == 0:
            copies.start(*self.names("s"))
        elif n == 1:
            copies.arrived(*self.names("s"))
            if self.stage_buf is None:

                def add_held(i, carry):
                    zz, yy, xx = i // 4, lax.rem(i // 2, 2), lax.rem(i, 2)
                    work[zz, yy, xx] = self.source[zz, self.c, yy, xx] + self.swapped[zz, yy, xx]
                    return carry

                lax.fori_loop(0, 4 * n_z, add_held, 0)
                copies.start(*self.names("a1", "b1"))
                return
            for copy in self.load(0):
                copy.start()
            for zz in range(n_z):
                if zz + 1 < n_z:
                    for copy in self.load(zz + 1):
                        copy.start()
                for copy in self.load(zz):
                    copy.wait()
                slot = zz % 2

                def add_quarter(i, carry):
                    yy, xx = i // 2, lax.rem(i, 2)
                    work[zz, yy, xx] = self.stage_buf[slot, 0, yy, xx] + self.stage_buf[slot, 1, yy, xx]
                    return carry

                lax.fori_loop(0, 4, add_quarter, 0)
            copies.start(*self.names("a1", "b1"))
        elif n == 2:
            copies.arrived(*self.names("a1"))

            def add_a(i, carry):
                zz, yy = i // 2, lax.rem(i, 2)
                work[zz, yy, gx, :, lower] = work[zz, yy, gx, :, lower] + self.first[0, zz, yy]
                return carry

            lax.fori_loop(0, 2 * n_z, add_a, 0)
            copies.start(*self.names("a2"))
            copies.arrived(*self.names("b1"))

            def add_b(i, carry):
                zz, xx = i // 2, lax.rem(i, 2)
                work[zz, gy, xx, :, upper] = work[zz, gy, xx, :, upper] + self.first[1, zz, xx]
                return carry

            lax.fori_loop(0, 2 * n_z, add_b, 0)
            copies.start(*self.names("b2"))
        elif n == 3:
            copies.arrived(*self.names("a2", "b2"))

            def add_c(zz, carry):
                work[zz, gy, gx, :, lower] = work[zz, gy, gx, :, lower] + self.second[0, zz]
                work[zz, gy, gx, :, upper] = work[zz, gy, gx, :, upper] + self.second[1, zz]
                return carry

            lax.fori_loop(0, n_z, add_c, 0)
            copies.start(*self.names(*zs))
        elif n == 4:
            copies.arrived(*self.names(*zs))
            total = work[self.z, gy, gx].astype(F32)
            for i in range(n_z - 1):
                total = total + self.along[i].astype(F32)
            self.final[gy, gx] = total.astype(BF16)
            copies.start(*self.names("fx", "fy", "fd"))
        else:
            copies.arrived(*self.names("fx", "fy", "fd"))
            copies.sent(*self.names("s", "a1", "b1", "a2", "b2", "fx", "fy", "fd", *zs))


def reduce_scratch(n_z, rows, width):
    return [
        pltpu.VMEM((n_z, 2, 2, rows, width), BF16),
        pltpu.VMEM((2, n_z, 2, rows, width // 2), BF16),
        pltpu.VMEM((2, n_z, rows, width // 2), BF16),
        pltpu.VMEM((n_z - 1, rows, width), BF16),
    ]


def n_reduce(n_z):
    return 8 + n_z - 1


TAIL_LANES = 32
PER_TILE = 128 // TAIL_LANES


def packed_shape(heads):
    return (heads + heads // PER_TILE, ROWS_S, 128)


def pack(ref, heads, p, side, state):
    head = p * 2 + side
    block = heads + head // PER_TILE
    ref[head] = state[:, :128].astype(BF16)
    rest = state[:, 128:]
    first, second = [pltpu.roll(rest, TAIL_LANES * (side + 2 * half), 1) if side + 2 * half else rest for half in range(2)]
    moved = jnp.where(lax.rem(p, 2) == 0, first, second).astype(BF16)
    if side == 0:
        held = jnp.where(lax.rem(p, 2) == 0, jnp.zeros_like(moved), ref[block])
        ref[block] = held + moved
    else:
        ref[block] = ref[block] + moved


class Chain:
    def __init__(self, copies, where, n_z, onward, own, mate, carry, out, pass_lead, pass_other):
        dp, sp, g, gy, gx, z, c, across_x, across_y, diagonal, partner = where
        lead = 1 if onward else 0
        self.copies, self.n_z = copies, n_z
        self.own, self.mate, self.carry, self.out = own, mate, carry, out
        self.pass_lead, self.pass_other = pass_lead, pass_other
        self.leads = c == lead
        self.place = z if onward else n_z - 1 - z
        to = lax.rem(z + 1, n_z) if onward else lax.rem(z + n_z - 1, n_z)
        before = lax.rem(z + n_z - 1, n_z) if onward else lax.rem(z + 1, n_z)
        self.next_device, self.last_device = (dp, to * 2 + c), (dp, before * 2 + c)
        copies.add("own", own, mate, partner)
        copies.add("raw", carry, carry, partner)
        copies.add("carry", out, carry, self.next_device)

    def begin(self):
        @pl.when(jnp.logical_not(self.leads))
        def _():
            self.copies.start("own")

        @pl.when(self.leads & (self.place == 0))
        def _():
            self.carry[...] = jnp.zeros_like(self.carry)

    def middle(self, now):
        now = now & self.leads

        @pl.when(now)
        def _():
            self.copies.arrived("own")

        @pl.when(now & (self.place > 0))
        def _():
            self.copies.arrived("carry")

        @pl.when(now)
        def _():
            self.copies.start("raw")

        @pl.when(now & (self.place < self.n_z - 1))
        def _():
            def one(head, carry):
                inner = self.mate[head].astype(F32) + self.pass_other * self.carry[head].astype(F32)
                self.out[head] = (self.own[head].astype(F32) + self.pass_lead * inner).astype(BF16)
                return carry

            lax.fori_loop(0, self.own.shape[0], one, 0)
            self.copies.start("carry")

    def finish(self, result, weights):
        heads = result.shape[0]

        def unpack(value):
            def group(q, carry):
                rest = value(heads + q)
                for j in range(PER_TILE):
                    head = q * PER_TILE + j
                    tail = pltpu.roll(rest, 128 - TAIL_LANES * j, 1) if j else rest
                    result[head] = jnp.concatenate(
                        [value(head) * weights[:, :128], tail * weights[:, 128:]], axis=1
                    ).astype(BF16)
                return carry

            lax.fori_loop(0, heads // PER_TILE, group, 0)

        @pl.when(jnp.logical_not(self.leads))
        def _():
            self.copies.arrived("raw")
            unpack(lambda i: self.carry[i].astype(F32))

        @pl.when(self.leads)
        def _():
            unpack(lambda i: self.mate[i].astype(F32) + self.pass_other * self.carry[i].astype(F32))

    def drain(self):
        @pl.when(jnp.logical_not(self.leads))
        def _():
            self.copies.sent("own")

        @pl.when(self.leads)
        def _():
            self.copies.sent("raw")

        @pl.when(self.leads & (self.place < self.n_z - 1))
        def _():
            self.copies.sent("carry")


class Documents:
    def __init__(self, doc_ref, sp, n_sp):
        self.ref, self.n_sp, self.tok = doc_ref, n_sp, doc_ref.shape[1] // n_sp
        self.row = self.of(sp)
        self.column = jnp.broadcast_to(self.row, (128, self.tok)).T[:, 0:1]

    def of(self, sp):
        return self.ref[:, pl.ds(pl.multiple_of(sp * self.tok, 128), self.tok)].astype(F32)

    def last(self, sp):
        value = self.of(jnp.maximum(sp, 0))[:, self.tok - 1 : self.tok]
        return jnp.where(sp >= 0, value, -1.0)

    def first(self, sp):
        value = self.of(jnp.minimum(sp, self.n_sp - 1))[:, 0:1]
        return jnp.where(sp < self.n_sp, value, -2.0)

    def through(self, here, there):
        return jnp.broadcast_to(jnp.where(here == there, 1.0, 0.0), (1, 128))


def rows_sum(values):
    total = values[0]
    for value in values[1:]:
        total = total + value
    return total


STRIP = 512
CHAIN_STEPS = 3
CHAIN_BACK_STEPS = 5
CHUNK = 256
UNITS = 4
EARLY = 2


def units_of(width):
    chunks = -(-width // CHUNK)
    step = -(-chunks // UNITS)
    return [(first, min(chunks, first + step)) for first in range(0, chunks, step)]


def forward_kernel(
    n_sp, x_ref, gain_a_ref, gain_m_ref, doc_ref, table_ref, wo_ref, wg_ref, wu_ref, wd_ref, wq_ref, wk_ref, wv_ref, *rest,
):
    n_unit = len(units_of(wd_ref.shape[0]))
    (att_ref, inv_ref, state_ref, gain_ref, q_ref, k_ref, v_ref, normed_ref, w_joint_ref), rest = rest[:9], rest[9:]
    fulls, rest = rest[: 3 + EARLY], rest[3 + EARLY :]
    kept, rest = rest[: n_unit - EARLY], rest[n_unit - EARLY :]
    (joint_own, more_own, out_own), rest = rest[:3], rest[3:]
    ffn_own, rest = rest[:n_unit], rest[n_unit:]
    (
        mask_ref, joint_vm, num_ref, den_ref, own_state, mate_state, in_state, out_state, gains_ref, gains_in,
        prior_ref, q_scr, k_scr, v_scr, normed_scr, normed_t, send_sem, recv_sem, local_sem,
    ) = rest
    tok = x_ref.shape[0]
    n_z = n_sp // 2
    lanes = q_ref.shape[1]
    pairs = v_ref.shape[1] // 128
    where = place(n_sp)
    dp, sp, g, gy, gx, z, c, across_x, across_y, diagonal, partner = where
    copies = Copies(send_sem, recv_sem)
    joint_full, more_full = fulls[:2]
    owns = (joint_own, more_own, out_own) + tuple(ffn_own[:EARLY])
    gathers = [Gather(copies, k, n_z, own, full, where) for k, (own, full) in enumerate(zip(owns, fulls))]
    others = [(dp, lax.rem(sp + i, n_sp)) for i in range(1, n_sp)]
    for i, device in enumerate(others, 1):
        copies.add(("gain", i), gains_ref, gains_in.at[i - 1], device)
    docs = Documents(doc_ref, sp, n_sp)
    even = sp - c
    chain = Chain(
        copies, where, n_z, True, own_state, mate_state, in_state, out_state,
        docs.through(docs.last(even + 1), docs.last(even)), docs.through(docs.last(even), docs.last(even - 1)),
    )
    part_lane = lax.broadcasted_iota(jnp.int32, gains_ref.shape, 1)
    part = jnp.concatenate([jnp.broadcast_to(gain_a_ref[...], (4, gain_a_ref.shape[1])),
                            jnp.broadcast_to(gain_m_ref[...], (4, gain_m_ref.shape[1]))], axis=0).astype(F32)
    if part.shape[1] < gains_ref.shape[1]:
        part = jnp.concatenate([part] * n_sp, axis=1)
    gains_ref[...] = jnp.where(part_lane // (gains_ref.shape[1] // n_sp) == sp, part, 0.0)
    assembled = [
        pltpu.make_async_copy(wq_ref, joint_own.at[:, 0:lanes], local_sem.at[0]),
        pltpu.make_async_copy(wk_ref, joint_own.at[:, lanes : 2 * lanes], local_sem.at[1]),
        pltpu.make_async_copy(
            wv_ref.at[:, 0 : joint_own.shape[1] - 2 * lanes], joint_own.at[:, 2 * lanes :], local_sem.at[2]
        ),
        pltpu.make_async_copy(wv_ref.at[:, joint_own.shape[1] - 2 * lanes :], more_own, local_sem.at[3]),
    ]
    for copy in assembled:
        copy.start()
    meet(others + [across_x, across_y])
    copies.start(*[("gain", i) for i in range(1, n_sp)])
    for copy in assembled:
        copy.wait()
    gathers[0].stage(0)
    gathers[1].stage(0)
    out_own[...] = wo_ref[...].T
    width = wd_ref.shape[0]
    for own, (first, last) in zip(ffn_own, units_of(width)):
        lo, hi = first * CHUNK, min(last * CHUNK, width)
        span = (last - first) * CHUNK
        for i, piece in enumerate((wg_ref[lo:hi, :].T, wu_ref[lo:hi, :].T, wd_ref[lo:hi, :].T)):
            if hi - lo < span:
                own[:, (i + 1) * span - CHUNK : (i + 1) * span] = jnp.zeros((own.shape[0], CHUNK), BF16)
            own[:, i * span : i * span + hi - lo] = piece

    table = table_ref[...]
    row = lax.broadcasted_iota(jnp.int32, (tok, tok), 0)
    col = lax.broadcasted_iota(jnp.int32, (tok, tok), 1)
    mask_ref[...] = jnp.where((row >= col) & (docs.column == docs.row), 1.0, 0.0)
    prior_ref[...] = jnp.broadcast_to(jnp.where(docs.column == docs.last(sp - 1), 1.0, 0.0), prior_ref.shape)
    copies.arrived(*[("gain", i) for i in range(1, n_sp)])
    gain_ref[...] = gains_ref[...] + rows_sum([gains_in[i] for i in range(n_sp - 1)])
    x = x_ref[...].astype(F32)
    scale = lax.rsqrt(jnp.mean(x * x, axis=1, keepdims=True) + EPSILON)
    normed_scr[...] = (x * scale * gain_ref[0:1]).astype(BF16)
    normed_t[...] = normed_scr[...].T
    local = [
        pltpu.make_async_copy(own, gather.own_place, local_sem.at[k])
        for k, (own, gather) in enumerate(zip(owns, gathers))
    ] + [
        pltpu.make_async_copy(own, keep, local_sem.at[len(owns) + k])
        for k, (own, keep) in enumerate(zip(ffn_own[EARLY:], kept))
    ]
    for copy in local:
        copy.start()
    gathers[0].stage(1)
    gathers[1].stage(1)
    gathers[0].stage(2)
    gathers[2].stage(0)
    gathers[3].stage(0)
    gathers[1].stage(2)
    gathers[0].stage(3)
    gathers[1].stage(3)
    gathers[0].stage(4)
    for copy in local:
        copy.wait()
    split = joint_full.shape[1]
    fetches = [
        pltpu.make_async_copy(joint_full, joint_vm.at[:, 0:split], local_sem.at[0]),
        pltpu.make_async_copy(more_full, joint_vm.at[:, split:], local_sem.at[1]),
    ]
    fetches[0].start()
    fetches[0].wait()
    project = lambda first: mm(normed_scr[...], joint_vm[:, pl.ds(first, BLK)]).astype(BF16)
    for first in range(0, lanes, BLK):
        q_scr[:, first : first + BLK] = project(first)
        k_scr[:, first : first + BLK] = project(lanes + first)

    def values_block(i, carry):
        @pl.when(i == (split - 2 * lanes) // BLK)
        def _():
            gathers[1].stage(4)
            fetches[1].start()
            fetches[1].wait()

        first = pl.multiple_of(i * BLK, BLK)
        v_scr[:, pl.ds(first, BLK)] = project(2 * lanes + first)
        return carry

    lax.fori_loop(0, v_scr.shape[1] // BLK, values_block, 0)
    saves = [
        pltpu.make_async_copy(src, dst, local_sem.at[i])
        for i, (src, dst) in enumerate(
            ((q_scr, q_ref), (k_scr, k_ref), (v_scr, v_ref), (normed_t, normed_ref), (joint_vm, w_joint_ref))
        )
    ]
    for copy in saves:
        copy.start()

    tail = jnp.where(docs.row == docs.last(sp), 1.0, 0.0)

    def at(p, step, *todo):
        @pl.when(p == step)
        def _():
            for k, n in todo:
                gathers[k].stage(n)

    def state_pair(p, carry):
        at(p, 0, (2, 1))
        at(p, 2, (3, 1), (4, 0))
        at(p, 5, (2, 2))
        columns = pl.ds(pl.multiple_of(p * 128, 128), 128)
        v_t = v_scr[:, columns].astype(F32).T * tail
        ones = jnp.broadcast_to(tail, (16, tail.shape[1]))
        for side in range(2):
            head = p * 2 + side
            sel = selectors(table, head, lanes)
            one, two = factors(k_scr[...], sel, table)
            phi = (one * two).astype(BF16)
            lhs = jnp.concatenate([v_t[side * 64 : side * 64 + 64], ones], axis=0)
            pack(own_state, 2 * pairs, p, side, mm(lhs.astype(BF16), phi))
        return carry

    lax.fori_loop(0, pairs, state_pair, 0)

    chain.begin()
    turn = jnp.minimum(z * CHAIN_STEPS, pairs - 1)

    lane = lax.broadcasted_iota(jnp.int32, (BLK, 128), 1)

    def intra_pair(p, carry):
        at(p, 1, (2, 3), (3, 2))
        at(p, 3, (4, 1))
        at(p, 4, (3, 3))
        at(p, 7, (4, 2))
        chain.middle(p == turn)
        columns = pl.ds(pl.multiple_of(p * 128, 128), 128)
        v_hat = with_ones(v_scr[:, columns])
        heads = [head_lanes(q_scr[...], p * 2 + side) for side in range(2)]
        for i in range(tok // BLK):
            rows = slice(i * BLK, (i + 1) * BLK)
            keys = slice(0, (i + 1) * BLK)
            totals = []
            for side in range(2):
                t = mm(heads[side][rows], k_scr[keys, :], NT) + 4.0
                w = ((t * t + 16.0) * mask_ref[rows, keys]).astype(BF16)
                totals.append(mm(w, v_hat[keys]))
            num_ref[rows, columns] = jnp.where(lane < 64, totals[0][:, :128], totals[1][:, :128])
            den_ref[rows, columns] = jnp.where(lane < 64, totals[0][:, 128:], totals[1][:, 128:])
        return carry

    lax.fori_loop(0, pairs, intra_pair, 0)
    chain.finish(state_ref, table[4:5])
    prior = prior_ref[:, 0:1]
    wide_lane = lax.broadcasted_iota(jnp.int32, (tok, 128), 1)

    def inter_pair(p, carry):
        at(p, 4, (4, 3))
        columns = pl.ds(pl.multiple_of(p * 128, 128), 128)
        totals = []
        for side in range(2):
            head = p * 2 + side
            sel = selectors(table, head, lanes)
            state = state_ref[head]
            z_rows = jnp.broadcast_to(state[64:65].astype(F32), (128, PAD_F)).astype(BF16)
            one, two = factors(q_scr[...], sel, table)
            totals.append(mm((one * two).astype(BF16), placed(state, side, z_rows), NT) * prior)
        num = num_ref[:, columns] + jnp.where(wide_lane < 64, totals[0][:, :128], totals[1][:, :128])
        den = den_ref[:, columns] + jnp.where(wide_lane < 64, totals[0][:, 128:], totals[1][:, 128:])
        inv = 1.0 / den
        inv_ref[:, columns] = inv.astype(BF16)
        att_ref[:, columns] = (num * inv).astype(BF16)
        return carry

    lax.fori_loop(0, pairs, inter_pair, 0)
    for gather in gathers[2:]:
        gather.stage(4)
    for copy in saves:
        copy.wait()
    copies.sent(*[("gain", i) for i in range(1, n_sp)])
    chain.drain()


def forward(n_sp, x, gain_a, gain_m, docs, table, wo, wg, wu, wd, wq, wk, wv):
    tok, dim = x.shape
    lanes, values = wq.shape[1], wv.shape[1]
    heads = lanes // FEAT
    shard = wq.shape[0]
    vmem, anywhere = pl.BlockSpec(memory_space=pltpu.VMEM), pl.BlockSpec(memory_space=pl.ANY)
    n_z = n_sp // 2
    spans = [3 * CHUNK * (last - first) for first, last in units_of(wd.shape[0])]
    joint = 2 * lanes + values
    gathered = [joint // 2, joint // 2, dim] + spans[:EARLY]
    sems = len(gathered) * n_copies(n_z) + n_sp + 2
    shape = jax.ShapeDtypeStruct
    result = pl.pallas_call(
        functools.partial(forward_kernel, n_sp),
        out_shape=(
            shape((tok, values), BF16), shape((tok, values), BF16), shape((heads, ROWS_S, PAD_F), BF16),
            shape((8, dim), F32), shape((tok, lanes), BF16), shape((tok, lanes), BF16),
            shape((tok, values), BF16), shape((dim, tok), BF16), shape((dim, joint), BF16),
        )
        + tuple(shape((shard * n_sp, w), BF16) for w in gathered)
        + tuple(shape((shard, w), BF16) for w in spans[EARLY:]),
        in_specs=[vmem] * 9 + [anywhere] * 3,
        out_specs=(vmem,) * 4 + (anywhere,) * (5 + len(gathered) + len(spans) - EARLY),
        scratch_shapes=[pltpu.VMEM((shard, w), BF16) for w in [joint // 2, joint // 2, dim] + spans]
        + [
            pltpu.VMEM((tok, tok), F32),
            pltpu.VMEM((dim, joint), BF16),
            pltpu.VMEM((tok, values), F32),
            pltpu.VMEM((tok, values), F32),
            pltpu.VMEM(packed_shape(heads), BF16),
            pltpu.VMEM(packed_shape(heads), BF16),
            pltpu.VMEM(packed_shape(heads), BF16),
            pltpu.VMEM(packed_shape(heads), BF16),
            pltpu.VMEM((8, dim), F32),
            pltpu.VMEM((n_sp - 1, 8, dim), F32),
            pltpu.VMEM((tok, 128), F32),
            pltpu.VMEM((tok, lanes), BF16),
            pltpu.VMEM((tok, lanes), BF16),
            pltpu.VMEM((tok, values), BF16),
            pltpu.VMEM((tok, dim), BF16),
            pltpu.VMEM((dim, tok), BF16),
            pltpu.SemaphoreType.DMA((sems,)),
            pltpu.SemaphoreType.DMA((sems,)),
            pltpu.SemaphoreType.DMA((10,)),
        ],
        compiler_params=pltpu.CompilerParams(
            collective_id=0, has_side_effects=True, vmem_limit_bytes=60 << 20
        ),
        name="forward",
    )(x, gain_a, gain_m, docs, table, wo, wg, wu, wd, wq, wk, wv)
    n = 9 + len(gathered)
    return result[:9], result[11], result[12:n], result[n:]


def backward_kernel(
    n_sp, widths, q_ref, k_ref, v_ref, g_ref, att_ref, inv_ref, prior_state_ref, doc_ref, table_ref, *rest,
):
    n_red = len(widths)
    sources, rest = rest[:n_red], rest[n_red:]
    (gq_ref, gk_ref, gv_ref), rest = rest[:3], rest[3:]
    finals, rest = rest[:n_red], rest[n_red:]
    swaps, rest = rest[:n_red], rest[n_red:]
    buffers, rest = [rest[4 * i : 4 * i + 4] for i in range(n_red)], rest[4 * n_red :]
    (
        stage_buf, mask_ref, ghat_ref, gq_acc, gk_acc, own_state, mate_state, in_state, out_state, later_state,
        prior_ref, later_ref,
        send_sem, recv_sem, local_sem,
    ) = rest
    tok, lanes = q_ref.shape
    n_z = n_sp // 2
    pairs = v_ref.shape[1] // 128
    where = place(n_sp)
    dp, sp, g, gy, gx, z, c, across_x, across_y, diagonal, partner = where
    copies = Copies(send_sem, recv_sem)
    reduces = [
        Reduce(
            copies, k, n_z, where, sources[k], swaps[k], buffers[k], finals[k],
            stage_buf.at[:, :, :, :, :, 0 : widths[k]], local_sem,
        )
        for k in range(n_red)
    ]
    docs = Documents(doc_ref, sp, n_sp)
    even = sp - c
    chain = Chain(
        copies, where, n_z, False, own_state, mate_state, in_state, out_state,
        docs.through(docs.first(even), docs.first(even + 1)), docs.through(docs.first(even + 1), docs.first(even + 2)),
    )
    along = [(dp, lax.rem(z + i, n_z) * 2 + c) for i in range(1, n_z)]
    meet([partner, across_x, across_y, diagonal] + along)
    for reduce in reduces:
        reduce.stage(0)

    def at(p, step, *todo):
        @pl.when(p == step)
        def _():
            for k, n in todo:
                reduces[k].stage(n)

    table = table_ref[...]
    row = lax.broadcasted_iota(jnp.int32, (tok, tok), 0)
    col = lax.broadcasted_iota(jnp.int32, (tok, tok), 1)
    mask_ref[...] = jnp.where((row <= col) & (docs.column == docs.row), 1.0, 0.0)
    prior_ref[...] = jnp.broadcast_to(jnp.where(docs.column == docs.last(sp - 1), 1.0, 0.0), prior_ref.shape)
    later_ref[...] = jnp.broadcast_to(jnp.where(docs.column == docs.first(sp + 1), 1.0, 0.0), later_ref.shape)
    gq_acc[...] = jnp.zeros_like(gq_acc)
    gk_acc[...] = jnp.zeros_like(gk_acc)
    r = lax.broadcasted_iota(jnp.int32, (128, 128), 0)
    c128 = lax.broadcasted_iota(jnp.int32, (128, 128), 1)
    same = jnp.where(r // 64 == c128 // 64, 1.0, 0.0).astype(BF16)
    lane64 = lax.broadcasted_iota(jnp.int32, (tok, 128), 1) % 64
    head_row = jnp.where(docs.row == docs.first(sp), 1.0, 0.0)

    def ghat_pair(p, carry):
        for when, todo in GHAT_SCHEDULE:
            at(p, when, *todo)
        columns = pl.ds(pl.multiple_of(p * 128, 128), 128)
        scaled = g_ref[:, columns].astype(F32) * inv_ref[:, columns].astype(F32)
        product = scaled * att_ref[:, columns].astype(F32)
        high = product.astype(BF16)
        low = (product - high.astype(F32)).astype(BF16)
        dots = -(mm(high, same) + mm(low, same))
        dots_high = dots.astype(BF16)
        dots_low = (dots - dots_high.astype(F32)).astype(BF16)
        extra = jnp.where(lane64 == 0, dots_high, jnp.where(lane64 == 1, dots_low, jnp.zeros_like(dots_low)))
        ghat = jnp.concatenate([scaled.astype(BF16), extra], axis=1)
        ghat_ref[p] = ghat
        ghat_t = ghat.astype(F32).T * head_row
        for side in range(2):
            head = p * 2 + side
            sel = selectors(table, head, lanes)
            one, two = factors(q_ref[...], sel, table)
            phi = (one * two).astype(BF16)
            lhs = jnp.concatenate(
                [ghat_t[side * 64 : side * 64 + 64], ghat_t[128 + side * 64 : 128 + side * 64 + 16]], axis=0
            )
            state = mm(lhs.astype(BF16), phi)
            z_row = jnp.sum(state[64:80], axis=0, keepdims=True)
            pack(
                own_state, 2 * pairs, p, side,
                jnp.concatenate([state[0:64], jnp.broadcast_to(z_row, (16, PAD_F))], axis=0),
            )
        return carry

    lax.fori_loop(0, pairs, ghat_pair, 0)

    chain.begin()
    turn = jnp.minimum((n_z - 1 - z) * CHAIN_BACK_STEPS, 2 * pairs - 1)

    lane = lax.broadcasted_iota(jnp.int32, (tok, 256), 1)
    first_row = lax.broadcasted_iota(jnp.int32, (128, PAD_F), 0)

    def main_pair(p, carry):
        columns = pl.ds(pl.multiple_of(p * 128, 128), 128)
        v_hat = with_ones(v_ref[:, columns])
        gv = [jnp.zeros((BLK, 128), F32) for _ in range(tok // BLK)]
        for side in range(2):
            step = p * 2 + side
            for when, todo in SCHEDULE:
                if when % 2 == side:
                    at(step, when, *todo)
            chain.middle(step == turn)
            head = p * 2 + side
            sel = selectors(table, head, lanes)
            ghat = jnp.where((lane % 128) // 64 == side, ghat_ref[p], jnp.zeros((tok, 256), BF16))
            q_head = head_lanes(q_ref[...], head)
            q_twice = q_head + q_head
            k_twice = head_lanes(k_ref[...], head, 2)
            prior = prior_state_ref[head]
            z_two = jnp.where(first_row // 2 == side * 32, prior[64:65], jnp.zeros((128, PAD_F), BF16))
            rows_p = placed(prior, side, z_two)
            q_one, q_two = factors(q_ref[...], sel, table)
            d_phi = mm(ghat, rows_p) * prior_ref[:, 0:1]
            gq_acc[...] += mm((d_phi * q_two).astype(BF16), sel[0], NT) + mm(
                (d_phi * q_one).astype(BF16), sel[1], NT
            )
            for j in range(tok // BLK):
                rows = slice(j * BLK, (j + 1) * BLK)
                onward = slice(j * BLK, tok)
                t = mm(k_ref[rows, :], q_head[onward], NT) + 4.0
                g_w = mm(v_hat[rows], ghat[onward], NT)
                mask = mask_ref[rows, onward]
                masked_t = t * mask
                w = (masked_t * t + 16.0 * mask).astype(BF16)
                g_s = (g_w * masked_t).astype(BF16)
                gv[j] = gv[j] + mm(w, ghat[onward, 0:128])
                gk_acc[rows, :] += mm(g_s, q_twice[onward])
                gq_acc[onward, :] += mm(g_s, k_twice[rows], TN)
        for j in range(tok // BLK):
            rows = slice(j * BLK, (j + 1) * BLK)
            gv_ref[rows, columns] = gv[j].astype(BF16)
        return carry

    lax.fori_loop(0, pairs, main_pair, 0)
    chain.drain()
    chain.finish(later_state, table[4:5])

    def later_pair(p, carry):
        for when, todo in LATE_SCHEDULE:
            at(p, when, *todo)
        columns = pl.ds(pl.multiple_of(p * 128, 128), 128)
        v_hat = with_ones(v_ref[:, columns])
        gv_inter = None
        for side in range(2):
            head = p * 2 + side
            sel = selectors(table, head, lanes)
            later = later_state[head]
            z_one = jnp.where(first_row == 0, later[64:65], jnp.zeros((128, PAD_F), BF16))
            rows_n = placed(later, side, z_one)
            k_one, k_two = factors(k_ref[...], sel, table)
            phi_k = (k_one * k_two).astype(BF16)
            gvi = mm(phi_k, rows_n[0:128], NT)
            gv_inter = gvi if gv_inter is None else gv_inter + gvi
            d_phi = mm(v_hat, rows_n) * later_ref[:, 0:1]
            gk_acc[...] += mm((d_phi * k_two).astype(BF16), sel[0], NT) + mm(
                (d_phi * k_one).astype(BF16), sel[1], NT
            )
        gv_ref[:, columns] = (gv_ref[:, columns].astype(F32) + gv_inter * later_ref[...]).astype(BF16)
        return carry

    lax.fori_loop(0, pairs, later_pair, 0)
    gq_ref[...] = gq_acc[...].astype(BF16)
    gk_ref[...] = gk_acc[...].astype(BF16)
    for k, n in LAST_SCHEDULE:
        reduces[k].stage(n)


GHAT_SCHEDULE = ((1, ((0, 1),)), (3, ((1, 1),)), (4, ((0, 2),)), (6, ((2, 1),)), (7, ((1, 2),)), )
SCHEDULE = ((1, ((0, 3),)), (2, ((3, 1),)), (4, ((2, 2),)), (6, ((1, 3),)), (7, ((0, 4),)), (9, ((3, 2),)), (10, ((2, 3),)), (12, ((1, 4),)), (14, ((0, 5),)), (15, ((3, 3),)), )
LATE_SCHEDULE = ((1, ((2, 4),)), (2, ((1, 5),)), (4, ((3, 4),)), (5, ((2, 5),)), (7, ((3, 5),)), )
LAST_SCHEDULE = ()


def shards_of(parts):
    return [part.reshape(-1, part.shape[-1]) for part in parts]


def backward(n_sp, arrays, grads):
    q, v = arrays[0], arrays[2]
    tok, lanes = q.shape
    heads = lanes // FEAT
    n_z = n_sp // 2
    rows = grads[0].shape[4]
    widths = tuple(grad.shape[5] for grad in grads)
    n_red = len(grads)
    vmem, anywhere = pl.BlockSpec(memory_space=pltpu.VMEM), pl.BlockSpec(memory_space=pl.ANY)
    shape = jax.ShapeDtypeStruct
    sems = n_red * n_reduce(n_z) + 3
    result = pl.pallas_call(
        functools.partial(backward_kernel, n_sp, widths),
        out_shape=(shape(q.shape, BF16), shape(q.shape, BF16), shape(v.shape, BF16))
        + tuple(shape((2, 2, rows, w), BF16) for w in widths)
        + tuple(shape((n_z, 2, 2, rows, w), BF16) for w in widths),
        in_specs=[vmem] * len(arrays) + [anywhere] * n_red,
        out_specs=(vmem,) * (3 + n_red) + (anywhere,) * n_red,
        scratch_shapes=sum([reduce_scratch(n_z, rows, w) for w in widths], [])
        + [
            pltpu.VMEM((2, 2, 2, 2, rows, max(widths)), BF16),
            pltpu.VMEM((tok, tok), F32),
            pltpu.VMEM((heads // 2, tok, 256), BF16),
            pltpu.VMEM(q.shape, F32),
            pltpu.VMEM(q.shape, F32),
            pltpu.VMEM(packed_shape(heads), BF16),
            pltpu.VMEM(packed_shape(heads), BF16),
            pltpu.VMEM(packed_shape(heads), BF16),
            pltpu.VMEM(packed_shape(heads), BF16),
            pltpu.VMEM((heads, ROWS_S, PAD_F), BF16),
            pltpu.VMEM((tok, 128), F32),
            pltpu.VMEM((tok, 128), F32),
            pltpu.SemaphoreType.DMA((sems,)),
            pltpu.SemaphoreType.DMA((sems,)),
            pltpu.SemaphoreType.DMA((2, 2)),
        ],
        compiler_params=pltpu.CompilerParams(
            collective_id=1, has_side_effects=True, vmem_limit_bytes=63 << 20
        ),
        name="backward",
    )(*arrays, *grads)
    return result[:3], shards_of(result[3 : 3 + n_red])


def reduce_units(chunks):
    edges = [0, 2, 4, 6, 8, chunks]
    return list(zip(edges[:-1], edges[1:]))


IN_FFN = 2
FFN_SCHEDULE = {
    1: (("g", 0, 1), ("g", 1, 0)),
    3: (("g", 0, 2), ("r", 0, 0)),
    4: (("g", 1, 1), ("g", 0, 3), ("r", 0, 1)),
    5: (("g", 0, 4), ("r", 1, 0)),
    6: (("g", 1, 2), ("r", 0, 2), ("r", 1, 1)),
    7: (("g", 1, 3),),
    8: (("g", 1, 4), ("r", 0, 3), ("r", 1, 2)),
    9: (("r", 1, 3),),
    10: (("r", 0, 4),),
}
FFN_LATE = (("r", 1, 4),)
FFN_LAST = (("r", 0, 5), ("r", 1, 5))


def ffn_kernel(n_sp, gather_units, chunks, x_ref, att_ref, out_w_ref, gain_ref, cot_ref, *rest):
    n_unit = len(gather_units)
    sums = reduce_units(chunks)
    n_sum = len(sums)
    early, rest = rest[:EARLY], rest[EARLY:]
    kept, rest = rest[: n_unit - EARLY], rest[n_unit - EARLY :]
    ggain_ref, rest = rest[0], rest[1:]
    finals, rest = rest[:IN_FFN], rest[IN_FFN:]
    (output_ref, gh_ref, gatt_ref, gout_ref), rest = rest[:4], rest[4:]
    grads, rest = rest[: n_sum - IN_FFN], rest[n_sum - IN_FFN :]
    late, rest = rest[: n_unit - EARLY], rest[n_unit - EARLY :]
    grads, rest = rest[:IN_FFN] + grads, rest[IN_FFN:]
    swaps, rest = rest[:IN_FFN], rest[IN_FFN:]
    buffers, rest = [rest[4 * i : 4 * i + 4] for i in range(IN_FFN)], rest[4 * IN_FFN :]
    (
        hid, n2, n2_t, cot_t, acc_o, acc_n, parts, w_buf, g_buf, send_sem, recv_sem, w_sem, g_sem, o_sem,
    ) = rest
    tok, dim = x_ref.shape
    n_z = n_sp // 2
    where = place(n_sp)
    dp, sp, g, gy, gx, z, c, across_x, across_y, diagonal, partner = where
    copies = Copies(send_sem, recv_sem)
    gathers = [Gather(copies, ("g", k), n_z, own, full, where) for k, (own, full) in enumerate(zip(kept, late))]
    reduces = [
        Reduce(copies, ("r", k), n_z, where, grads[k], swaps[k], buffers[k], finals[k])
        for k in range(IN_FFN)
    ]
    along = [(dp, lax.rem(z + i, n_z) * 2 + c) for i in range(1, n_z)]
    meet([partner, across_x, across_y, diagonal] + along)
    gathers[0].stage(0)
    own_copies = [
        pltpu.make_async_copy(own, gather.own_place, o_sem.at[k])
        for k, (own, gather) in enumerate(zip(kept, gathers))
    ]
    for copy in own_copies:
        copy.start()

    def run(todo):
        for kind, k, n in todo:
            (gathers if kind == "g" else reduces)[k].stage(n)

    fulls = list(early) + list(late)

    def load(chunk, slot, do_wait=False):
        if do_wait:
            for i in range(3):
                pltpu.make_async_copy(fulls[0].at[:, 0:CHUNK], w_buf.at[slot, i], w_sem.at[slot, i]).wait()
            return
        for full, (first, last) in zip(fulls, gather_units):
            @pl.when((chunk >= first) & (chunk < last))
            def _():
                for i in range(3):
                    lane = pl.multiple_of((chunk - first + i * (last - first)) * CHUNK, CHUNK)
                    pltpu.make_async_copy(full.at[:, pl.ds(lane, CHUNK)], w_buf.at[slot, i], w_sem.at[slot, i]).start()

    def save(chunk, slot, do_wait=False):
        if do_wait:
            for i in range(3):
                pltpu.make_async_copy(
                    g_buf.at[slot, i], grads[0].at[:, :, :, :, :, 0:CHUNK], g_sem.at[slot, i]
                ).wait()
            return
        for grad, (first, last) in zip(grads, sums):
            @pl.when((chunk >= first) & (chunk < last))
            def _():
                for i in range(3):
                    lane = pl.multiple_of((chunk - first + i * (last - first)) * CHUNK, CHUNK)
                    pltpu.make_async_copy(
                        g_buf.at[slot, i], grad.at[:, :, :, :, :, pl.ds(lane, CHUNK)], g_sem.at[slot, i]
                    ).start()

    load(0, 0)
    gain = gain_ref[4:5]
    def prepare(i, carry):
        rows = pl.ds(pl.multiple_of(i * BLK, BLK), BLK)
        hidden = x_ref[rows, :].astype(F32) + mm(att_ref[rows, :], out_w_ref[...], NT)
        hid[rows, :] = hidden
        scale = lax.rsqrt(jnp.mean(hidden * hidden, axis=1, keepdims=True) + EPSILON)
        normed = (hidden * scale * gain).astype(BF16)
        n2[rows, :] = normed
        n2_t[:, rows] = normed.T
        cot_t[:, rows] = cot_ref[rows, :].T
        return carry

    lax.fori_loop(0, tok // BLK, prepare, 0)
    acc_o[...] = jnp.zeros_like(acc_o)
    acc_n[...] = jnp.zeros_like(acc_n)
    for copy in own_copies:
        copy.wait()
    grad_shape = g_buf.shape[2:]

    def step(chunk, carry):
        slot = lax.rem(chunk, 2)
        load(chunk, slot, True)

        @pl.when(chunk >= 2)
        def _():
            save(chunk, slot, True)

        for when, todo in FFN_SCHEDULE.items():
            @pl.when(chunk == when)
            def _():
                run(todo)

        @pl.when(chunk + 1 < chunks)
        def _():
            load(chunk + 1, 1 - slot)

        def rows_part(i, carry):
            rows = pl.ds(pl.multiple_of(i * STRIP, STRIP), STRIP)
            wg, wu, wd = w_buf[slot, 0], w_buf[slot, 1], w_buf[slot, 2]
            gate = mm(n2[rows, :], wg)
            up = mm(n2[rows, :], wu)
            g_mixed = mm(cot_ref[rows, :], wd)
            sig = 1.0 / (1.0 + jnp.exp(-gate))
            act = gate * sig
            mixed = (act * up).astype(BF16)
            g_gate = (g_mixed * up * sig * (1.0 + gate * (1.0 - sig))).astype(BF16)
            g_up = (g_mixed * act).astype(BF16)
            parts[0, rows, :] = g_gate
            parts[1, rows, :] = g_up
            parts[2, rows, :] = mixed
            acc_o[rows, :] += mm(mixed, wd, NT)
            acc_n[rows, :] += mm(g_gate, wg, NT) + mm(g_up, wu, NT)
            return carry

        lax.fori_loop(0, tok // STRIP, rows_part, 0)
        g_buf[slot, 0] = mm(n2_t[...], parts[0]).astype(BF16).reshape(grad_shape)
        g_buf[slot, 1] = mm(n2_t[...], parts[1]).astype(BF16).reshape(grad_shape)
        g_buf[slot, 2] = mm(cot_t[...], parts[2]).astype(BF16).reshape(grad_shape)
        save(chunk, slot)
        return carry

    lax.fori_loop(0, chunks, step, 0)
    run(FFN_LATE)
    def conclude(i, total):
        rows = pl.ds(pl.multiple_of(i * BLK, BLK), BLK)
        hidden = hid[rows, :]
        n2[rows, :] = (hidden + acc_o[rows, :]).astype(BF16)
        scale = lax.rsqrt(jnp.mean(hidden * hidden, axis=1, keepdims=True) + EPSILON)
        e = acc_n[rows, :]
        eg = e * gain
        inner = jnp.mean(eg * hidden, axis=1, keepdims=True)
        gh = cot_ref[rows, :].astype(F32) + scale * eg - hidden * (scale * scale * scale * inner)
        acc_o[rows, :] = gh
        branch = gh.astype(BF16)
        n2_t[rows, :] = branch
        cot_t[rows, :] = mm(branch, out_w_ref[...]).astype(BF16)
        return total + jnp.sum(e * hidden * scale, axis=0, keepdims=True)

    total = lax.fori_loop(0, tok // BLK, conclude, jnp.zeros((1, dim), F32))
    ggain_ref[...] = jnp.broadcast_to(total, ggain_ref.shape)
    outs = [
        pltpu.make_async_copy(n2, output_ref, o_sem.at[0]),
        pltpu.make_async_copy(acc_o, gh_ref, o_sem.at[1]),
        pltpu.make_async_copy(cot_t, gatt_ref, o_sem.at[2]),
    ]
    for copy in outs:
        copy.start()
    save(chunks - 2, (chunks - 2) % 2, True)
    save(chunks - 1, (chunks - 1) % 2, True)
    def out_copy(i):
        lanes = pl.ds(pl.multiple_of(i * CHUNK, CHUNK), CHUNK)
        slot, part = i // 3, lax.rem(i, 3)
        return pltpu.make_async_copy(
            g_buf.at[slot, part], gout_ref.at[:, :, :, :, :, lanes], g_sem.at[slot, part]
        )

    def out_piece(i, carry):
        lanes = pl.ds(pl.multiple_of(i * CHUNK, CHUNK), CHUNK)
        g_buf[i // 3, lax.rem(i, 3)] = mm(n2_t[...], att_ref[:, lanes], TN).astype(BF16).reshape(grad_shape)
        out_copy(i).start()
        return carry

    n_out = att_ref.shape[1] // CHUNK
    lax.fori_loop(0, n_out, out_piece, 0)
    outs = outs + [out_copy(i) for i in range(n_out)]
    run(FFN_LAST)
    for copy in outs:
        copy.wait()


def ffn(n_sp, x, att, out_w, gain, cot, width, early, kept):
    tok, dim = x.shape
    values = att.shape[1]
    n_z = n_sp // 2
    chunks = -(-width // CHUNK)
    gather_units = units_of(width)
    sums = reduce_units(chunks)
    rows = dim // n_sp // GROUP
    spans = [3 * CHUNK * (last - first) for first, last in sums]
    vmem, anywhere = pl.BlockSpec(memory_space=pltpu.VMEM), pl.BlockSpec(memory_space=pl.ANY)
    shape = jax.ShapeDtypeStruct
    split = lambda w: shape((n_z, 2, 2, 2, rows, w), BF16)
    sems = len(kept) * n_copies(n_z) + IN_FFN * n_reduce(n_z)
    full_shapes = tuple(shape((k.shape[0] * n_sp, k.shape[1]), BF16) for k in kept)
    result = pl.pallas_call(
        functools.partial(ffn_kernel, n_sp, gather_units, chunks),
        out_shape=(shape((8, dim), F32),)
        + tuple(shape((2, 2, rows, w), BF16) for w in spans[:IN_FFN])
        + (shape((tok, dim), BF16), shape((tok, dim), F32), shape((tok, values), BF16), split(values))
        + tuple(split(w) for w in spans[IN_FFN:])
        + full_shapes,
        in_specs=[vmem] * 5 + [anywhere] * len(early) + [vmem] * len(kept),
        out_specs=(vmem,) * (1 + IN_FFN) + (anywhere,) * (4 + len(spans) - IN_FFN + len(kept)),
        scratch_shapes=[pltpu.VMEM((n_z, 2, 2, 2, rows, w), BF16) for w in spans[:IN_FFN]]
        + [pltpu.VMEM((n_z, 2, 2, rows, w), BF16) for w in spans[:IN_FFN]]
        + sum([reduce_scratch(n_z, rows, w) for w in spans[:IN_FFN]], [])
        + [
            pltpu.VMEM((tok, dim), F32),
            pltpu.VMEM((tok, dim), BF16),
            pltpu.VMEM((dim, tok), BF16),
            pltpu.VMEM((dim, tok), BF16),
            pltpu.VMEM((tok, dim), F32),
            pltpu.VMEM((tok, dim), F32),
            pltpu.VMEM((3, tok, CHUNK), BF16),
            pltpu.VMEM((2, 3, dim, CHUNK), BF16),
            pltpu.VMEM((2, 3, n_z, 2, 2, 2, rows, CHUNK), BF16),
            pltpu.SemaphoreType.DMA((sems,)),
            pltpu.SemaphoreType.DMA((sems,)),
            pltpu.SemaphoreType.DMA((2, 3)),
            pltpu.SemaphoreType.DMA((2, 3)),
            pltpu.SemaphoreType.DMA((4,)),
        ],
        compiler_params=pltpu.CompilerParams(
            collective_id=2, has_side_effects=True, vmem_limit_bytes=63 << 20
        ),
        name="ffn",
    )(x, att, out_w, gain, cot, *early, *kept)
    n = 1 + IN_FFN
    shards = shards_of(result[1:n])
    output, g_hidden, g_att, g_out = result[n : n + 4]
    grads = result[n + 4 : n + 4 + len(spans) - IN_FFN]
    return output, g_hidden, g_att, result[0], g_out, shards, grads


def tail_kernel(
    n_sp, normed_ref, gq_ref, gk_ref, gv_ref, gain_ref, ggain_ref, w_hbm, x_hbm, gh_hbm, gains_ref, *rest,
):
    finals, rest = rest[:3], rest[3:]
    gin_ref, rest = rest[0], rest[1:]
    sources, rest = rest[:3], rest[3:]
    swaps, rest = rest[:3], rest[3:]
    buffers, rest = [rest[4 * i : 4 * i + 4] for i in range(3)], rest[12:]
    w_ref, x_ref, gh_ref, own_gains, sum_gains, in_sp, in_dp, send_sem, recv_sem, local_sem = rest
    tok, dim = x_ref.shape
    n_z = n_sp // 2
    lanes = gq_ref.shape[1]
    where = place(n_sp)
    dp, sp, g, gy, gx, z, c, across_x, across_y, diagonal, partner = where
    loads = [
        pltpu.make_async_copy(src, dst, local_sem.at[i])
        for i, (src, dst) in enumerate(((w_hbm, w_ref), (x_hbm, x_ref), (gh_hbm, gh_ref)))
    ]
    for copy in loads:
        copy.start()
    copies = Copies(send_sem, recv_sem)
    reduces = [Reduce(copies, k, n_z, where, sources[k], swaps[k], buffers[k], finals[k]) for k in range(3)]
    others = [(dp, lax.rem(sp + i, n_sp)) for i in range(1, n_sp)]
    groups = [across_x, across_y, diagonal]
    for i, device in enumerate(others):
        copies.add(("sp", i), own_gains, in_sp.at[i], device)
    for i, device in enumerate(groups):
        copies.add(("dp", i), sum_gains, in_dp.at[i], device)
    meet(others + groups)
    block = sources[0].shape[:-1] + (BLK,)
    half = gv_ref.shape[1] // 2

    def product(k, j, ref, i):
        sources[k][:, :, :, :, :, pl.ds(j, BLK)] = (
            mm(normed_ref[...], ref[:, pl.ds(i, BLK)]).astype(BF16).reshape(block)
        )

    def values_piece(n, carry):
        first = pl.multiple_of(n * BLK, BLK)
        product(0, first, gv_ref, first)
        return carry

    def more_values_piece(n, carry):
        first = pl.multiple_of(n * BLK, BLK)
        product(1, first, gv_ref, pl.multiple_of(half + first, BLK))
        return carry

    lax.fori_loop(0, half // BLK, values_piece, 0)
    lax.fori_loop(0, half // BLK, more_values_piece, 0)
    reduces[0].stage(0)
    for j in range(0, lanes, BLK):
        product(2, j, gq_ref, j)
        if j == 0:
            reduces[1].stage(0)
        product(2, lanes + j, gk_ref, j)
    for copy in loads:
        copy.wait()
    todo = [[(2, 0), (0, 1)], [(1, 1)], [(0, 2), (2, 1)], [(1, 2)]]
    gain = gain_ref[0:1]
    n_block = tok // BLK

    def norm_back(i, total):
        rows = pl.ds(pl.multiple_of(i * BLK, BLK), BLK)
        e = (
            mm(gq_ref[rows, :], w_ref[:, 0:lanes], NT)
            + mm(gk_ref[rows, :], w_ref[:, lanes : 2 * lanes], NT)
            + mm(gv_ref[rows, :], w_ref[:, 2 * lanes :], NT)
        )
        u = x_ref[rows, :].astype(F32)
        scale = lax.rsqrt(jnp.mean(u * u, axis=1, keepdims=True) + EPSILON)
        eg = e * gain
        inner = jnp.mean(eg * u, axis=1, keepdims=True)
        gh_ref[rows, :] = gh_ref[rows, :] + scale * eg - u * (scale * scale * scale * inner)
        for step, stages in enumerate(todo):
            @pl.when(i == min(step, n_block - 1))
            def _():
                for k, n in stages:
                    reduces[k].stage(n)

        return total + jnp.sum(e * u * scale, axis=0, keepdims=True)

    total = lax.fori_loop(0, n_block, norm_back, jnp.zeros((1, dim), F32))
    save = pltpu.make_async_copy(gh_ref, gin_ref, local_sem.at[0])
    save.start()
    row = lax.broadcasted_iota(jnp.int32, own_gains.shape, 0)
    own_gains[...] = jnp.where(row == 0, jnp.broadcast_to(total, own_gains.shape), ggain_ref[...])
    reduces[0].stage(3)
    reduces[2].stage(2)
    copies.start(*[("sp", i) for i in range(n_sp - 1)])
    reduces[1].stage(3)
    reduces[0].stage(4)
    reduces[2].stage(3)
    copies.arrived(*[("sp", i) for i in range(n_sp - 1)])
    sum_gains[...] = own_gains[...] + rows_sum([in_sp[i] for i in range(n_sp - 1)])
    reduces[1].stage(4)
    copies.start(*[("dp", i) for i in range(3)])
    reduces[2].stage(4)
    copies.arrived(*[("dp", i) for i in range(3)])
    gains_ref[...] = sum_gains[...] + rows_sum([in_dp[i] for i in range(3)])
    for reduce in reduces:
        reduce.stage(5)
    copies.sent(*[("sp", i) for i in range(n_sp - 1)], *[("dp", i) for i in range(3)])
    save.wait()


def tail(n_sp, normed, gq, gk, gv, w_joint, x, g_hidden, gain, ggain):
    tok, dim = x.shape
    lanes, values = gq.shape[1], gv.shape[1]
    n_z = n_sp // 2
    rows = dim // n_sp // GROUP
    vmem, anywhere = pl.BlockSpec(memory_space=pltpu.VMEM), pl.BlockSpec(memory_space=pl.ANY)
    shape = jax.ShapeDtypeStruct
    widths = (values // 2, values // 2, 2 * lanes)
    sems = 3 * n_reduce(n_z) + n_sp + 2
    return pl.pallas_call(
        functools.partial(tail_kernel, n_sp),
        out_shape=(shape((8, dim), F32),)
        + tuple(shape((2, 2, rows, w), BF16) for w in widths)
        + (shape((tok, dim), F32),),
        in_specs=[vmem] * 6 + [anywhere] * 3,
        out_specs=(vmem,) * 4 + (anywhere,),
        scratch_shapes=[pltpu.VMEM((n_z, 2, 2, 2, rows, w), BF16) for w in widths]
        + [pltpu.VMEM((n_z, 2, 2, rows, w), BF16) for w in widths]
        + sum([reduce_scratch(n_z, rows, w) for w in widths], [])
        + [
            pltpu.VMEM(w_joint.shape, BF16),
            pltpu.VMEM(x.shape, BF16),
            pltpu.VMEM((tok, dim), F32),
            pltpu.VMEM((8, dim), F32),
            pltpu.VMEM((8, dim), F32),
            pltpu.VMEM((n_sp - 1, 8, dim), F32),
            pltpu.VMEM((3, 8, dim), F32),
            pltpu.SemaphoreType.DMA((sems,)),
            pltpu.SemaphoreType.DMA((sems,)),
            pltpu.SemaphoreType.DMA((3,)),
        ],
        compiler_params=pltpu.CompilerParams(
            collective_id=3, has_side_effects=True, vmem_limit_bytes=63 << 20
        ),
        name="tail",
    )(normed, gq, gk, gv, gain, ggain, w_joint, x, g_hidden)


PASS_PARTS = 4


def finish_kernel(sums, *refs):
    n = len(sums) + 4
    sources, whole, refs = refs[:n], refs[n : n + 2], refs[n + 2 :]
    (q_out, k_out, v_out, out_out, gate_out, up_out, down_out), refs = refs[:7], refs[7:]
    whole_out, refs = refs[:2], refs[2:]
    held, passing, (sem, in_sem, out_sem) = refs[:n], refs[n : n + 2], refs[n + 2 :]
    reads, writes = [], []
    for a, (src, mid, dst) in enumerate(zip(whole, passing, whole_out)):
        count = src.shape[0] // PASS_PARTS
        for i in range(PASS_PARTS):
            rows = pl.ds(i * count, count)
            reads.append(pltpu.make_async_copy(src.at[rows], mid.at[rows], in_sem.at[a, i]))
            writes.append(pltpu.make_async_copy(mid.at[rows], dst.at[rows], out_sem.at[a, i]))
    copies = [pltpu.make_async_copy(src, dst, sem.at[i]) for i, (src, dst) in enumerate(zip(sources, held))]
    for copy in copies + reads:
        copy.start()
    for copy in copies:
        copy.wait()
    for read, write in zip(reads, writes):
        read.wait()
        write.start()
    qk_ref, va_ref, vb_ref, out_ref, units = held[0], held[1], held[2], held[3], held[4:]
    lanes = q_out.shape[1]
    width = gate_out.shape[0]
    q_out[...] = qk_ref[:, :lanes].astype(F32)
    k_out[...] = qk_ref[:, lanes:].astype(F32)
    v_out[:, : va_ref.shape[1]] = va_ref[...].astype(F32)
    v_out[:, va_ref.shape[1] :] = vb_ref[...].astype(F32)
    out_out[...] = out_ref[...].astype(F32).T
    for unit, (first, last) in zip(units, sums):
        lo, hi = first * CHUNK, min(last * CHUNK, width)
        span = (last - first) * CHUNK
        for i, out in enumerate((gate_out, up_out, down_out)):
            out[lo:hi, :] = unit[:, i * span : i * span + hi - lo].astype(F32).T
    for write in writes:
        write.wait()


def finish(width, lanes, qk, va, vb, out, units, whole):
    shard = va.shape[0]
    vmem, anywhere = pl.BlockSpec(memory_space=pltpu.VMEM), pl.BlockSpec(memory_space=pl.ANY)
    shape = jax.ShapeDtypeStruct
    arrays = (qk, va, vb, out, *units)
    return pl.pallas_call(
        functools.partial(finish_kernel, reduce_units(-(-width // CHUNK))),
        out_shape=(
            shape((shard, lanes), F32), shape((shard, lanes), F32), shape((shard, 2 * va.shape[1]), F32),
            shape(out.shape[::-1], F32), shape((width, shard), F32), shape((width, shard), F32),
            shape((width, shard), F32), *[shape(w.shape, w.dtype) for w in whole],
        ),
        in_specs=[anywhere] * (len(arrays) + len(whole)),
        out_specs=(vmem,) * 7 + (anywhere,) * len(whole),
        scratch_shapes=[pltpu.VMEM(a.shape, a.dtype) for a in (*arrays, *whole)]
        + [
            pltpu.SemaphoreType.DMA((len(arrays),)),
            pltpu.SemaphoreType.DMA((len(whole), PASS_PARTS)),
            pltpu.SemaphoreType.DMA((len(whole), PASS_PARTS)),
        ],
        compiler_params=pltpu.CompilerParams(vmem_limit_bytes=63 << 20),
        name="finish",
    )(*arrays, *whole)


def body(
    tokens, doc_ids, gain_attn, w_query, w_key, w_value, w_out, gain_mlp, w_gate, w_up, w_down, cotangent
):
    n_sp = lax.axis_size("sp")
    me = lax.axis_index("sp")
    tok = tokens.shape[0]
    heads = w_query.shape[1] // FEAT
    table = feature_table()
    docs = doc_ids
    width = gain_attn.shape[0]
    lanes = heads * FEAT
    hidden_units = w_gate.shape[1]
    parts = [part[None, :] for part in (gain_attn, gain_mlp)]
    if width % 128:
        parts = [jnp.tile(part, (1, n_sp)) for part in parts]
    (
        (att, inv, prior_state, gain, q, k, v, normed_one, w_joint), out_t, early, kept
    ) = forward(
        n_sp, tokens, *parts, docs, table, w_out, w_gate.T, w_up.T, w_down, w_query, w_key, w_value
    )
    output, g_hidden, g_att, grad_gain_two, g_out, shards, grads = ffn(
        n_sp, tokens, att, out_t, gain, cotangent, hidden_units, early, kept
    )
    (gq, gk, gv), (s_out, *more) = backward(
        n_sp, (q, k, v, g_att, att, inv, prior_state, docs, table), (g_out, *grads)
    )
    grad_gains, *joint, grad_input = tail(
        n_sp, normed_one, gq, gk, gv, w_joint, tokens, g_hidden, gain, grad_gain_two
    )
    n_dp = lax.axis_size("dp")

    def over_groups(shard):
        if n_dp > GROUP:
            shard = lax.psum(shard, "dp") * jnp.asarray(GROUP / n_dp, shard.dtype)
        return shard

    s_va, s_vb, s_query_key = shards_of(joint)
    g_query, g_key, g_value, g_w_out, g_gate, g_up, g_down, grad_input, output = finish(
        hidden_units, lanes, over_groups(s_query_key), over_groups(s_va), over_groups(s_vb), over_groups(s_out),
        [over_groups(shard) for shard in (*shards, *more)],
        (grad_input, output),
    )
    s_gains = over_groups(lax.dynamic_slice(grad_gains, (0, me * width), (2, width)))
    return (
        output, grad_input, s_gains[0], g_query, g_key, g_value, g_w_out, s_gains[1], g_gate.T, g_up.T, g_down
    )


def solution(mesh):
    placed_in = (
        P(("dp", "sp"), None), P("dp", None), P("sp"), P("sp", None), P("sp", None), P("sp", None),
        P(None, "sp"), P("sp"), P("sp", None), P("sp", None), P(None, "sp"), P(("dp", "sp"), None),
    )
    return jax.shard_map(
        body,
        mesh=mesh,
        in_specs=placed_in,
        out_specs=(
            P(("dp", "sp"), None), P(("dp", "sp"), None), P("sp"), P("sp", None), P("sp", None),
            P("sp", None), P(None, "sp"), P("sp"), P("sp", None), P("sp", None), P(None, "sp"),
        ),
        check_vma=False,
    )
```
